32 devices in a mesh: dp: 4 (over z), ctx: 4 (over x, core), tensor: 2 (over y).
Axes of the slice: x: 2, y: 2, z: 4, core: 2. Of those that a mesh axis runs over, the one named last changes fastest.
Arguments:
- layer_input: bfloat16 [4, 1024, 2048], P('dp', 'ctx'), may hold values from -6 to 6
- output_grad: bfloat16 [4, 1024, 2048], P('dp', 'ctx'), may hold values from -6 to 6
- prefix: int32 [4], P('dp'), may hold values from 204 to 1024
- attn_gain: float32 [2048], replicated, may hold values from 0.1 to 1.9
- w_query: bfloat16 [2048, 2048], P(None, 'tensor'), may hold values from -0.125 to 0.125
- w_key: bfloat16 [2048, 512], P(None, 'tensor'), may hold values from -0.125 to 0.125
- w_value: bfloat16 [2048, 512], P(None, 'tensor'), may hold values from -0.125 to 0.125
- w_out: bfloat16 [2048, 2048], P('tensor'), may hold values from -1 to 1
- mlp_gain: float32 [2048], replicated, may hold values from 0.1 to 1.9
- w_gate: bfloat16 [2048, 8192], P(None, 'tensor'), may hold values from -0.125 to 0.125
- w_up: bfloat16 [2048, 8192], P(None, 'tensor'), may hold values from -0.125 to 0.125
- w_down: bfloat16 [8192, 2048], P('tensor'), may hold values from -0.0625 to 0.0625
Outputs:
- layer_output: bfloat16 [4, 1024, 2048], P('dp', 'ctx')
- input_grad: float32 [4, 1024, 2048], P('dp', 'ctx')
- d_attn_gain: float32 [2048], P(('dp', 'ctx'))
- d_query: float32 [2048, 2048], P(('dp', 'ctx'), 'tensor')
- d_key: float32 [2048, 512], P(('dp', 'ctx'), 'tensor')
- d_value: float32 [2048, 512], P(('dp', 'ctx'), 'tensor')
- d_out_proj: float32 [2048, 2048], P('tensor', ('dp', 'ctx'))
- d_mlp_gain: float32 [2048], P(('dp', 'ctx'))
- d_gate: float32 [2048, 8192], P(('dp', 'ctx'), 'tensor')
- d_up: float32 [2048, 8192], P(('dp', 'ctx'), 'tensor')
- d_down: float32 [8192, 2048], P('tensor', ('dp', 'ctx'))
The draws below stay inside these ranges and needn't reach their ends.
All inputs are finite; a program needn't handle non-finite values.
Results may differ from the reference program's by a relative error of at most 0.024.
Values may be sent and summed in bfloat16 or wider, within the bound.
A program may use at most 256 MiB of HBM per device.

```python
import math
import jax
import jax.numpy as jnp
from jax import lax

D = 2048
H = 32
KV = 8
HD = 64
FF = 8192
LENGTH = 1024
SEQS = 4


def place_ends(array, stream_key, smallest, high):
    longest = array.shape.index(max(array.shape))
    spots = []
    for shift in (0, 1):
        where = [jax.random.randint(jax.random.fold_in(stream_key, axis), (), 0, length) for axis, length in enumerate(array.shape)]
        where[longest] = (where[longest] + shift) % array.shape[longest]
        spots.append(tuple(where))
    return array.at[spots[0]].set(smallest).at[spots[1]].set(high)


def block_scale(rng, extent, split, low, high):
    loudness = 1.0
    for dim, parts in split:
        steps = jax.random.uniform(jax.random.fold_in(jax.random.fold_in(rng, 6), dim), (parts,), jnp.float32, low / len(split), high / len(split))
        loudness = loudness * jnp.repeat(jnp.exp(steps), extent[dim] // parts).reshape((-1,) + (1,) * (len(extent) - 1 - dim))
    return loudness


def noise(key, shape, spread, limit, pieces=(), kind=jnp.bfloat16):
    entries = jax.random.normal(key, shape, jnp.float32) * spread
    if len(pieces) > 0:
        entries = block_scale(key, shape, pieces, -0.22, 0.18) * entries
    return jnp.clip(entries, min=-limit, max=limit).astype(kind)


def setup_inputs(seed: int = 0) -> dict:
    arg_keys = jax.random.split(jax.random.key(seed), 13)
    return {
        "layer_input": noise(arg_keys[0], (SEQS, LENGTH, D), 1.0, 6.0, ((0, 4), (1, 4))),
        "output_grad": noise(arg_keys[1], (SEQS, LENGTH, D), 1.0, 6.0, ((0, 4), (1, 4))),
        "prefix": place_ends(jax.random.randint(arg_keys[2], (SEQS,), LENGTH // 5, LENGTH + 1), jax.random.fold_in(arg_keys[2], 1), LENGTH // 5, LENGTH).astype(jnp.int32),
        "attn_gain": jnp.clip(1.0 + 0.18 * jax.random.normal(arg_keys[3], (D,), jnp.float32), 0.1, 1.9),
        "w_query": noise(arg_keys[4], (D, H * HD), D ** -0.5, 0.125, ((1, 2),)),
        "w_key": noise(arg_keys[5], (D, KV * HD), D ** -0.5, 0.125, ((1, 2),)),
        "w_value": noise(arg_keys[6], (D, KV * HD), D ** -0.5, 0.125, ((1, 2),)),
        "w_out": noise(arg_keys[7], (H * HD, D), (H * HD // 64) ** -0.5, 1.0, ((0, 2),)),
        "mlp_gain": jnp.clip(1.0 + 0.18 * jax.random.normal(arg_keys[8], (D,), jnp.float32), 0.1, 1.9),
        "w_gate": noise(arg_keys[9], (D, FF), D ** -0.5, 0.125, ((1, 2),)),
        "w_up": noise(arg_keys[10], (D, FF), D ** -0.5, 0.125, ((1, 2),)),
        "w_down": noise(arg_keys[11], (FF, D), FF ** -0.5, 0.0625, ((0, 2),)),
    }


EPS = 1e-05
ROPE_BASE = 500000.0
NEG = -1e+30

@jax.custom_vjp
def low(v):
    return lax.optimization_barrier(v.astype(jnp.bfloat16)).astype(jnp.float32)

@jax.custom_vjp
def low_back(v):
    return v

def low_keep(v):
    return (low(v), None)

def low_pass(kept, grad):
    return (grad,)

def back_keep(v):
    return (v, None)

def back_low(kept, grad):
    return (low(grad),)
low.defvjp(low_keep, low_pass)
low_back.defvjp(back_keep, back_low)

def matmul(a, b):
    return jnp.dot(a, b, precision=lax.Precision.HIGHEST)

def rms(v, gain):
    return v * lax.rsqrt(lax.optimization_barrier(jnp.mean(v * v, axis=-1, keepdims=True)) + EPS) * gain

def rotate(t, cosine, sine):
    half = t.shape[-1] // 2
    first, second = (t[..., :half], t[..., half:])
    return jnp.concatenate([first * cosine - second * sine, second * cosine + first * sine], axis=-1)

def layer(rows, prefix_len, attn_gain, w_query, w_key, w_value, w_out, mlp_gain, w_gate, w_up, w_down):
    length = rows.shape[0]
    group = H // KV
    position = jnp.arange(length).astype(jnp.float32)
    frequency = ROPE_BASE ** (-jnp.arange(HD // 2).astype(jnp.float32) * 2.0 / HD)
    angle = position[:, None] * frequency[None, :]
    cosine = jnp.cos(angle)[:, None, :]
    sine = jnp.sin(angle)[:, None, :]
    normed1 = low(rms(rows, attn_gain))
    query_pre = low_back(matmul(normed1, w_query)).reshape(length, H, HD)
    key_pre = low_back(matmul(normed1, w_key)).reshape(length, KV, HD)
    value = low(low_back(matmul(normed1, w_value))).reshape(length, KV, HD)
    query = low(rotate(query_pre, cosine, sine)).reshape(length, KV, group, HD)
    key = low(rotate(key_pre, cosine, sine))
    block = math.gcd(length, 512)
    query_blocks = query.reshape(length // block, block, KV, group, HD)
    starts = (jnp.arange(length // block) * block).astype(jnp.int32)
    key_pos = jnp.arange(length).astype(jnp.int32)

    def attend(item):
        query_block, start = item
        scores = jnp.einsum('cngd,lnd->ngcl', query_block, key, precision=lax.Precision.HIGHEST) * HD ** (-0.5)
        scores = low_back(scores)
        query_pos = start + jnp.arange(block).astype(jnp.int32)
        allowed = (key_pos[None, :] <= query_pos[:, None]) | (key_pos[None, :] < prefix_len)
        scores = jnp.where(allowed[None, None], scores, NEG)
        probs = low(jax.nn.softmax(scores, axis=-1))
        mixed = jnp.einsum('ngcl,lnd->cngd', probs, value, precision=lax.Precision.HIGHEST)
        return low(low_back(mixed))
    attended = lax.map(jax.checkpoint(attend), (query_blocks, starts)).reshape(length, H * HD)
    attn = low_back(matmul(attended, w_out))
    resid = rows + attn
    normed2 = low(rms(resid, mlp_gain))
    gate = low_back(matmul(normed2, w_gate))
    up = low_back(matmul(normed2, w_up))
    act = low(jax.nn.silu(gate) * up)
    return resid + matmul(act, w_down)

def reference(layer_input, output_grad, prefix, attn_gain, w_query, w_key, w_value, w_out, mlp_gain, w_gate, w_up, w_down):
    params = tuple((p.astype(jnp.float32) for p in (attn_gain, w_query, w_key, w_value, w_out, mlp_gain, w_gate, w_up, w_down)))
    inputs = layer_input.astype(jnp.float32)
    cotangent = output_grad.astype(jnp.float32)

    def per_sequence(carry, item):
        rows, grad_rows, prefix_len = item

        def apply(inputs_rows, *weights):
            return layer(inputs_rows, prefix_len, *weights)
        result, pull = jax.vjp(apply, rows, *params)
        grads = pull(grad_rows)
        return (tuple((c + g for c, g in zip(carry, grads[1:]))), (result, grads[0]))
    init = tuple((jnp.zeros_like(p) for p in params))
    sums, (results, d_inputs) = lax.scan(per_sequence, init, (inputs, cotangent, prefix.astype(jnp.int32)))
    return (results.astype(jnp.bfloat16), d_inputs, sums[0], sums[1], sums[2], sums[3], sums[4], sums[5], sums[6], sums[7], sums[8])
```

```python
import jax
import jax.numpy as jnp
from jax import lax
from jax.sharding import PartitionSpec as P

HD = 64


EPS = 1e-05
ROPE_BASE = 500000.0
NEG = -1e30
BF = jnp.bfloat16
F32 = jnp.float32


def dot_plain(left, right):
    return jnp.dot(left, right, preferred_element_type=F32)


def dot_right(left, right):
    return lax.dot_general(left, right, (((1,), (1,)), ((), ())), preferred_element_type=F32)


def dot_left(left, right):
    return lax.dot_general(left, right, (((0,), (0,)), ((), ())), preferred_element_type=F32)


def normed(v, gain):
    return v * lax.rsqrt(jnp.mean(v * v, axis=-1, keepdims=True) + EPS) * gain


def norm_back(v, gain, grad):
    factor = lax.rsqrt(jnp.mean(v * v, axis=-1, keepdims=True) + EPS)
    unit = v * factor
    d_unit = grad * gain
    d_gain = jnp.sum(grad * unit, axis=0)
    d_v = factor * (d_unit - unit * jnp.mean(d_unit * unit, axis=-1, keepdims=True))
    return (d_v, d_gain)


def rotate(t, cosine, sine):
    half = t.shape[-1] // 2
    first, second = (t[..., :half], t[..., half:])
    return jnp.concatenate(
        [first * cosine - second * sine, second * cosine + first * sine], axis=-1
    )


def rotate_back(t, cosine, sine):
    half = t.shape[-1] // 2
    first, second = (t[..., :half], t[..., half:])
    return jnp.concatenate(
        [first * cosine + second * sine, second * cosine - first * sine], axis=-1
    )


def score_block(query5, key_all, allowed):
    scores = jnp.einsum(
        "scngd,slnd->sngcl", query5, key_all, preferred_element_type=F32
    ) * HD ** (-0.5)
    return jnp.where(allowed[:, None, None], scores, NEG)


def build(ndp, nctx, nten):
    def pull(v, axis, n, s):
        return lax.ppermute(v, axis, [((i + s) % n, i) for i in range(n)])

    def flip(v, axis, n, bit):
        return lax.ppermute(v, axis, [(i, i ^ bit) for i in range(n)])

    def tensor_sum(v):
        low = v.astype(BF)
        if nten == 2:
            return low.astype(F32) + flip(low, "tensor", 2, 1).astype(F32)
        return lax.psum(low, "tensor").astype(F32)

    def gather_dp(v):
        rows = v.shape[0] // nten
        part = lax.dynamic_slice_in_dim(v, lax.axis_index("tensor") * rows, rows, 0)
        pieces = [v]
        for s in range(1, ndp):
            got = pull(part, "dp", ndp, s)
            pieces.append(got)
            for t in range(1, nten):
                pieces.append(pull(got, "tensor", nten, t))
        return jnp.concatenate(pieces, axis=0)

    def ctx_sum(full):
        r = full.shape[0] // (ndp * nctx)
        me = lax.axis_index("ctx")
        work = full.reshape(ndp, nctx, r, full.shape[1])
        bit = 1
        while bit < nctx:
            left = work.shape[1] // 2
            work = work.reshape(ndp, left, 2, r, full.shape[1])
            mine = (me // bit) % 2
            keep = lax.dynamic_index_in_dim(work, mine, 2, keepdims=False)
            give = lax.dynamic_index_in_dim(work, 1 - mine, 2, keepdims=False)
            got = flip(give, "ctx", nctx, bit)
            work = (keep.astype(F32) + got.astype(F32)).astype(BF)
            bit *= 2
        return work.reshape(ndp, r, full.shape[1])

    def finish_slices(full):
        got = lax.all_to_all(ctx_sum(full), "dp", 0, 0, tiled=True)
        return jnp.swapaxes(got, 0, 1).reshape(got.shape[1], -1).astype(F32)

    def finish_sum(full):
        got = lax.all_to_all(ctx_sum(full), "dp", 0, 0, tiled=True)
        return jnp.sum(got.astype(F32), axis=0)

    def local(
        layer_input,
        output_grad,
        prefix,
        attn_gain,
        w_query,
        w_key,
        w_value,
        w_out,
        mlp_gain,
        w_gate,
        w_up,
        w_down,
    ):
        seqs, span, width = layer_input.shape
        q_heads = w_query.shape[1] // HD
        kv_heads = w_key.shape[1] // HD
        group = q_heads // kv_heads
        zi = lax.axis_index("dp")
        rows = layer_input.astype(F32).reshape(seqs * span, width)
        grad_low = output_grad.reshape(seqs * span, width)
        grad_rows = grad_low.astype(F32)
        grad_all = gather_dp(grad_low)

        first = lax.axis_index("ctx") * span
        position = (first + jnp.arange(span)).astype(F32)
        frequency = ROPE_BASE ** (-jnp.arange(HD // 2).astype(F32) * 2.0 / HD)
        angle = position[:, None] * frequency[None, :]
        cosine = jnp.cos(angle)[None, :, None, :]
        sine = jnp.sin(angle)[None, :, None, :]
        normed1 = normed(rows, attn_gain).astype(BF)
        query = rotate(
            dot_plain(normed1, w_query).reshape(seqs, span, q_heads, HD), cosine, sine
        ).astype(BF)
        keyed = rotate(
            dot_plain(normed1, w_key).reshape(seqs, span, kv_heads, HD), cosine, sine
        ).astype(BF)
        valued = dot_plain(normed1, w_value).astype(BF).reshape(seqs, span, kv_heads * HD)
        key_all, value_all = (
            lax.all_gather(
                keyed.reshape(seqs, span, kv_heads * HD), "ctx", axis=1, tiled=True
            ),
            lax.all_gather(valued, "ctx", axis=1, tiled=True),
        )
        length = key_all.shape[1]
        key_all = key_all.reshape(seqs, length, kv_heads, HD)
        value_all = value_all.reshape(seqs, length, kv_heads, HD)
        query5 = query.reshape(seqs, span, kv_heads, group, HD)
        query_pos = first + jnp.arange(span)
        key_pos = jnp.arange(length)
        allowed = (key_pos[None, None, :] <= query_pos[None, :, None]) | (
            key_pos[None, None, :] < prefix[:, None, None]
        )
        scores = score_block(query5, key_all, allowed)
        top = jnp.max(scores, axis=-1, keepdims=True)
        exponent = jnp.exp(scores - top)
        total = jnp.sum(exponent, axis=-1, keepdims=True)
        log_total = top + jnp.log(total)
        probs_low = (exponent / total).astype(BF)
        attended = jnp.einsum(
            "sngcl,slnd->scngd", probs_low, value_all, preferred_element_type=F32
        )
        attended = attended.astype(BF).reshape(seqs * span, q_heads * HD)
        resid = rows + tensor_sum(dot_plain(attended, w_out))
        normed2 = normed(resid, mlp_gain).astype(BF)
        normed2_all = gather_dp(normed2)
        gate = dot_plain(normed2, w_gate)
        up = dot_plain(normed2, w_up)
        act = (jax.nn.silu(gate) * up).astype(BF)

        def mlp_back(gate, up, d_act):
            sigmoid_gate = jax.nn.sigmoid(gate)
            d_gate_pre = (
                d_act * up * sigmoid_gate * (1.0 + gate * (1.0 - sigmoid_gate))
            ).astype(BF)
            d_up_pre = (d_act * gate * sigmoid_gate).astype(BF)
            return d_gate_pre, d_up_pre

        d_act = dot_right(grad_low, w_down)
        d_gate_pre, d_up_pre = mlp_back(gate, up, d_act)
        back_terms = dot_right(d_gate_pre, w_gate) + dot_right(d_up_pre, w_up)
        d_normed2 = tensor_sum(back_terms)
        output = (resid + tensor_sum(dot_plain(act, w_down))).astype(BF)
        output = output.reshape(seqs, span, width)

        units = w_gate.shape[1] // ndp
        wg = lax.dynamic_slice_in_dim(w_gate, zi * units, units, 1)
        wu = lax.dynamic_slice_in_dim(w_up, zi * units, units, 1)
        wd = lax.dynamic_slice_in_dim(w_down, zi * units, units, 0)
        gate_s = dot_plain(normed2_all, wg)
        up_s = dot_plain(normed2_all, wu)
        d_act_s = dot_right(grad_all, wd)
        act_s = (jax.nn.silu(gate_s) * up_s).astype(BF)
        d_gate_s, d_up_s = mlp_back(gate_s, up_s, d_act_s)
        s_down = finish_slices(dot_left(grad_all, act_s).astype(BF)).T
        s_gate = finish_slices(dot_left(normed2_all, d_gate_s).astype(BF))
        s_up = finish_slices(dot_left(normed2_all, d_up_s).astype(BF))

        d_resid_norm, g_mlp_gain = norm_back(resid, mlp_gain, d_normed2)
        d_resid = grad_rows + d_resid_norm
        d_resid_low = d_resid.astype(BF)
        s_out = finish_sum(dot_left(d_resid_low, attended).astype(BF)).T
        d_attended = dot_right(d_resid_low, w_out).astype(BF).reshape(query5.shape)
        scores = score_block(query5, key_all, allowed)
        probs = jnp.exp(scores - log_total)
        probs_low = probs.astype(BF)
        d_probs = jnp.einsum(
            "scngd,slnd->sngcl", d_attended, value_all, preferred_element_type=F32
        )
        delta = jnp.sum(probs * d_probs, axis=-1, keepdims=True)
        d_scores = (probs * (d_probs - delta)).astype(BF)
        scale = HD ** (-0.5)
        d_query = (
            jnp.einsum("sngcl,slnd->scngd", d_scores, key_all, preferred_element_type=F32) * scale
        )
        d_key_all = (
            jnp.einsum("sngcl,scngd->slnd", d_scores, query5, preferred_element_type=F32) * scale
        )
        d_value_all = jnp.einsum(
            "sngcl,scngd->slnd", probs_low, d_attended, preferred_element_type=F32
        )
        d_kv = jnp.concatenate(
            [
                d_key_all.reshape(length, kv_heads * HD).astype(BF),
                d_value_all.reshape(length, kv_heads * HD).astype(BF),
            ],
            axis=1,
        )
        d_kv = lax.psum_scatter(d_kv, "ctx", scatter_dimension=0, tiled=True).astype(F32)
        d_key, d_val = d_kv[:, : kv_heads * HD], d_kv[:, kv_heads * HD :]
        d_qp = (
            rotate_back(d_query.reshape(seqs, span, q_heads, HD), cosine, sine)
            .astype(BF)
            .reshape(seqs * span, q_heads * HD)
        )
        d_kp = (
            rotate_back(d_key.reshape(seqs, span, kv_heads, HD), cosine, sine)
            .astype(BF)
            .reshape(seqs * span, kv_heads * HD)
        )
        d_vp = d_val.astype(BF).reshape(seqs * span, kv_heads * HD)
        front_terms = dot_right(d_qp, w_query) + dot_right(d_kp, w_key) + dot_right(d_vp, w_value)
        d_normed1 = tensor_sum(front_terms)
        d_rows_norm, g_attn_gain = norm_back(rows, attn_gain, d_normed1)
        d_input = d_resid + d_rows_norm
        d_input = d_input.reshape(seqs, span, width)
        s_qkv = finish_sum(
            dot_left(normed1, jnp.concatenate([d_qp, d_kp, d_vp], axis=1)).astype(BF)
        )
        nq, nk = q_heads * HD, kv_heads * HD
        s_query, s_key, s_value = s_qkv[:, :nq], s_qkv[:, nq : nq + nk], s_qkv[:, nq + nk :]
        gains = jnp.stack([g_attn_gain, g_mlp_gain])
        gains = lax.psum_scatter(gains, ("dp", "ctx"), scatter_dimension=1, tiled=True)
        return (
            output,
            d_input,
            gains[0],
            s_query,
            s_key,
            s_value,
            s_out,
            gains[1],
            s_gate,
            s_up,
            s_down,
        )

    return local


def solution(mesh):
    sizes = mesh.shape
    return jax.shard_map(
        build(sizes["dp"], sizes["ctx"], sizes["tensor"]),
        mesh=mesh,
        in_specs=(
            P("dp", "ctx", None),
            P("dp", "ctx", None),
            P("dp"),
            P(),
            P(None, "tensor"),
            P(None, "tensor"),
            P(None, "tensor"),
            P("tensor", None),
            P(),
            P(None, "tensor"),
            P(None, "tensor"),
            P("tensor", None),
        ),
        out_specs=(
            P("dp", "ctx", None),
            P("dp", "ctx", None),
            P(("dp", "ctx")),
            P(("dp", "ctx"), "tensor"),
            P(("dp", "ctx"), "tensor"),
            P(("dp", "ctx"), "tensor"),
            P("tensor", ("dp", "ctx")),
            P(("dp", "ctx")),
            P(("dp", "ctx"), "tensor"),
            P(("dp", "ctx"), "tensor"),
            P("tensor", ("dp", "ctx")),
        ),
        check_vma=False,
    )
```

```python
import functools
import jax
import jax.numpy as jnp
from jax import lax
from jax.experimental import pallas as pl
from jax.experimental.pallas import tpu as pltpu
from jax.sharding import PartitionSpec as P

HD = 64
EPS = 1e-05
ROPE_BASE = 500000.0
NEG = -1e30
BF = jnp.bfloat16
F32 = jnp.float32
VMEM_MOST = 60 * 1024 * 1024


def cost(flops, nbytes, trans=0):
    return pl.CostEstimate(flops=int(flops), bytes_accessed=int(nbytes), transcendentals=int(trans))


def nt(a, b):
    return lax.dot_general(a, b, (((1,), (1,)), ((), ())), preferred_element_type=F32)


def tn(a, b):
    return lax.dot_general(a, b, (((0,), (0,)), ((), ())), preferred_element_type=F32)


def nn(a, b):
    return jnp.dot(a, b, preferred_element_type=F32)


def swap_halves(t):
    lane = lax.broadcasted_iota(jnp.int32, t.shape, 1) % HD
    n = t.shape[1]
    return jnp.where(
        lane < HD // 2, pltpu.roll(t, n - HD // 2, 1), pltpu.roll(t, HD // 2, 1)
    )


def rope_tables(first, span):
    position = (first + jnp.arange(span)).astype(F32)
    frequency = ROPE_BASE ** (-jnp.arange(HD // 2).astype(F32) * 2.0 / HD)
    angle = position[:, None] * frequency[None, :]
    cosine, sine = jnp.cos(angle), jnp.sin(angle)
    return (
        jnp.concatenate([cosine, cosine, cosine, cosine], axis=1),
        jnp.concatenate([-sine, sine, -sine, sine], axis=1),
    )


def qkv_kernel(x_ref, gain_ref, wq_ref, wk_ref, wv_ref, cos_ref, sin_ref, n_ref, q_ref, kv_ref):
    cosine, sine = cos_ref[...], sin_ref[...]

    def rope(t):
        pieces = []
        for i in range(t.shape[1] // 128):
            part = t[:, 128 * i : 128 * (i + 1)]
            pieces.append((part * cosine + swap_halves(part) * sine).astype(BF))
        return pieces

    @pl.when(pl.program_id(0) == 0)
    def _():
        v = x_ref[...].astype(F32)
        factor = lax.rsqrt(jnp.mean(v * v, axis=-1, keepdims=True) + EPS)
        n_ref[...] = (v * factor * gain_ref[...]).astype(BF)
        width = wk_ref.shape[1]
        for i, part in enumerate(rope(nn(n_ref[...], wk_ref[...]))):
            kv_ref[:, 128 * i : 128 * (i + 1)] = part
        kv_ref[:, width:] = nn(n_ref[...], wv_ref[...]).astype(BF)

    for i, part in enumerate(rope(nn(n_ref[...], wq_ref[...]))):
        q_ref[:, 128 * i : 128 * (i + 1)] = part


def qkv(x, gain, wq, wk, wv, cosine, sine):
    rows, width = x.shape
    step = 256
    grid = wq.shape[1] // step
    whole = lambda a: pl.BlockSpec(a.shape, lambda j: (0, 0))
    kv_width = wk.shape[1] + wv.shape[1]
    return pl.pallas_call(
        qkv_kernel,
        grid=(grid,),
        in_specs=[
            whole(x),
            pl.BlockSpec((1, width), lambda j: (0, 0)),
            pl.BlockSpec((width, step), lambda j: (0, j)),
            whole(wk),
            whole(wv),
            whole(cosine),
            whole(sine),
        ],
        out_specs=[
            pl.BlockSpec((rows, width), lambda j: (0, 0)),
            pl.BlockSpec((rows, step), lambda j: (0, j)),
            pl.BlockSpec((rows, kv_width), lambda j: (0, 0)),
        ],
        out_shape=[
            jax.ShapeDtypeStruct((rows, width), BF),
            jax.ShapeDtypeStruct((rows, wq.shape[1]), BF),
            jax.ShapeDtypeStruct((rows, kv_width), BF),
        ],
        compiler_params=pltpu.CompilerParams(vmem_limit_bytes=40 * 1024 * 1024),
        cost_estimate=cost(
            2 * rows * width * (wq.shape[1] + kv_width), 2 * width * (wq.shape[1] + kv_width)
        ),
        name="qkv",
    )(x, gain.reshape(1, width), wq, wk, wv, cosine, sine)


def mask_bias(first, prefix, length, span):
    key = lax.broadcasted_iota(jnp.int32, (length, span), 0)
    query = lax.broadcasted_iota(jnp.int32, (length, span), 1) + first
    return jnp.where((key <= query) | (key < prefix), 0.0, NEG).astype(F32)


def attend_kernel(group, where_ref, q_ref, k_ref, v_ref, o_ref, lse_ref, bias_ref):
    length, span = bias_ref.shape

    @pl.when(pl.program_id(0) == 0)
    def _():
        bias_ref[...] = mask_bias(where_ref[0], where_ref[1], length, span)

    heads = q_ref.shape[1] // HD
    pair = []
    for h in range(heads):
        kv = h // group
        key = k_ref[:, HD * kv : HD * (kv + 1)]
        value = v_ref[:, HD * kv : HD * (kv + 1)]
        query = q_ref[:, HD * h : HD * (h + 1)] * jnp.asarray(HD**-0.5, BF)
        scores = nt(key, query) + bias_ref[...]
        top = jnp.max(scores, axis=0, keepdims=True)
        exponent = jnp.exp(scores - top)
        total = jnp.sum(exponent, axis=0, keepdims=True)
        lse_ref[h : h + 1, :] = top + jnp.log(total)
        mixed = tn(value, exponent.astype(BF)) / total
        pair.append(mixed)
        if h % 2:
            o_ref[:, HD * (h - 1) : HD * (h + 1)] = jnp.concatenate(pair, axis=0).T.astype(BF)
            pair = []


def attend(where, q, kv):
    span, length = q.shape[0], kv.shape[0]
    blocks = kv.shape[1] // 256
    wide = q.shape[1] // blocks
    group = 2 * q.shape[1] // kv.shape[1]
    return pl.pallas_call(
        functools.partial(attend_kernel, group),
        grid=(blocks,),
        in_specs=[
            pl.BlockSpec(memory_space=pltpu.SMEM),
            pl.BlockSpec((span, wide), lambda j: (0, j)),
            pl.BlockSpec((length, 128), lambda j: (0, j)),
            pl.BlockSpec((length, 128), lambda j: (0, blocks + j)),
        ],
        out_specs=[
            pl.BlockSpec((span, wide), lambda j: (0, j)),
            pl.BlockSpec((wide // HD, span), lambda j: (j, 0)),
        ],
        out_shape=[
            jax.ShapeDtypeStruct(q.shape, BF),
            jax.ShapeDtypeStruct((q.shape[1] // HD, span), F32),
        ],
        scratch_shapes=[pltpu.VMEM((length, span), F32)],
        compiler_params=pltpu.CompilerParams(vmem_limit_bytes=40 * 1024 * 1024),
        cost_estimate=cost(4 * 4 * length * span * q.shape[1], 4 * span * q.shape[1], length * span * 16),
        name="attend",
    )(where, q, kv, kv)


def attend_back_kernel(
    group, where_ref, q_ref, k_ref, v_ref, do_ref, lse_ref, cos_ref, sin_ref, dq_ref, dk_ref, dv_ref, bias_ref
):
    length, span = bias_ref.shape

    @pl.when(pl.program_id(0) == 0)
    def _():
        bias_ref[...] = mask_bias(where_ref[0], where_ref[1], length, span)

    heads = q_ref.shape[1] // HD
    scale = jnp.asarray(HD**-0.5, BF)
    pair = []
    for h in range(heads):
        kv = h // group
        lanes = slice(HD * kv, HD * (kv + 1))
        key, value = k_ref[:, lanes], v_ref[:, lanes]
        query = q_ref[:, HD * h : HD * (h + 1)] * scale
        grad = do_ref[:, HD * h : HD * (h + 1)]
        probs = jnp.exp(nt(key, query) + (bias_ref[...] - lse_ref[h : h + 1, :]))
        d_probs = nt(value, grad)
        delta = jnp.sum(probs * d_probs, axis=0, keepdims=True)
        d_scores = (probs * (d_probs - delta)).astype(BF)
        d_value = nn(probs.astype(BF), grad)
        d_key = nn(d_scores, query)
        if h % group == 0:
            sum_key, sum_value = d_key, d_value
        else:
            sum_key, sum_value = sum_key + d_key, sum_value + d_value
        if h % group == group - 1:
            dk_ref[:, lanes] = sum_key.astype(BF)
            dv_ref[:, lanes] = sum_value.astype(BF)
        pair.append(tn(key * scale, d_scores))
        if h % 2:
            both = jnp.concatenate(pair, axis=0).T
            back = both * cos_ref[...] - swap_halves(both) * sin_ref[...]
            dq_ref[:, HD * (h - 1) : HD * (h + 1)] = back.astype(BF)
            pair = []


def attend_back(where, q, kv, d_out, lse, cosine, sine):
    span, length = q.shape[0], kv.shape[0]
    blocks = kv.shape[1] // 256
    wide = q.shape[1] // blocks
    group = 2 * q.shape[1] // kv.shape[1]
    side = pl.BlockSpec((span, wide), lambda j: (0, j))
    keys = pl.BlockSpec((length, 128), lambda j: (0, j))
    table = pl.BlockSpec((span, 128), lambda j: (0, 0))
    return pl.pallas_call(
        functools.partial(attend_back_kernel, group),
        grid=(blocks,),
        in_specs=[
            pl.BlockSpec(memory_space=pltpu.SMEM),
            side,
            keys,
            pl.BlockSpec((length, 128), lambda j: (0, blocks + j)),
            side,
            pl.BlockSpec((wide // HD, span), lambda j: (j, 0)),
            table,
            table,
        ],
        out_specs=[side, keys, keys],
        out_shape=[
            jax.ShapeDtypeStruct(q.shape, BF),
            jax.ShapeDtypeStruct((length, 128 * blocks), BF),
            jax.ShapeDtypeStruct((length, 128 * blocks), BF),
        ],
        scratch_shapes=[pltpu.VMEM((length, span), F32)],
        compiler_params=pltpu.CompilerParams(vmem_limit_bytes=40 * 1024 * 1024),
        cost_estimate=cost(4 * 10 * length * span * q.shape[1], 8 * span * q.shape[1], length * span * 16),
        name="attend_back",
    )(where, q, kv, kv, d_out, lse, cosine, sine)


def kv_back_kernel(k_ref, v_ref, cos_ref, sin_ref, dk_ref, dv_ref):
    total = sum(k_ref[i].astype(F32) for i in range(k_ref.shape[0]))
    for i in range(total.shape[1] // 128):
        part = total[:, 128 * i : 128 * (i + 1)]
        back = part * cos_ref[...] - swap_halves(part) * sin_ref[...]
        dk_ref[:, 128 * i : 128 * (i + 1)] = back.astype(BF)
    dv_ref[...] = sum(v_ref[i].astype(F32) for i in range(v_ref.shape[0])).astype(BF)


def kv_back(got_key, got_value, cosine, sine):
    return pl.pallas_call(
        kv_back_kernel,
        out_shape=[jax.ShapeDtypeStruct(got_key.shape[1:], BF)] * 2,
        cost_estimate=cost(8 * got_key.size, 4 * got_key.size),
        name="kv_back",
    )(got_key, got_value, cosine, sine)


def gate_parts(gate, up, d_act):
    sig = 1.0 / (1.0 + jnp.exp(-gate))
    silu = gate * sig
    return (
        (silu * up).astype(BF),
        (d_act * up * (sig + silu * (1.0 - sig))).astype(BF),
        (d_act * silu).astype(BF),
    )


def mlp_kernel(n_ref, g_ref, wg_ref, wu_ref, wd_ref, o_ref, dn_ref, o_acc, dn_acc):
    j = pl.program_id(0)
    normed2, grad = n_ref[...], g_ref[...]
    gate = nn(normed2, wg_ref[...])
    up = nn(normed2, wu_ref[...])
    d_act = nt(grad, wd_ref[...])
    act, d_gate, d_up = gate_parts(gate, up, d_act)
    out = nn(act, wd_ref[...])
    back = nt(d_gate, wg_ref[...]) + nt(d_up, wu_ref[...])

    @pl.when(j == 0)
    def _():
        o_acc[...] = out
        dn_acc[...] = back

    @pl.when(j > 0)
    def _():
        o_acc[...] += out
        dn_acc[...] += back

    @pl.when(j == pl.num_programs(0) - 1)
    def _():
        o_ref[...] = o_acc[...].astype(BF)
        dn_ref[...] = dn_acc[...].astype(BF)


def mlp(normed2, grad, wg, wu, wd, step=512):
    rows, width = normed2.shape
    units = wg.shape[1]
    whole = pl.BlockSpec((rows, width), lambda j: (0, 0))
    cols = pl.BlockSpec((width, step), lambda j: (0, j))
    return pl.pallas_call(
        mlp_kernel,
        grid=(units // step,),
        in_specs=[whole, whole, cols, cols, pl.BlockSpec((step, width), lambda j: (j, 0))],
        out_specs=[whole, whole],
        out_shape=[jax.ShapeDtypeStruct((rows, width), BF)] * 2,
        scratch_shapes=[pltpu.VMEM((rows, width), F32)] * 2,
        compiler_params=pltpu.CompilerParams(vmem_limit_bytes=VMEM_MOST),
        cost_estimate=cost(12 * rows * width * units, 6 * width * units),
        name="mlp",
    )(normed2, grad, wg, wu, wd)


def unit_grads_kernel(
    ndp, nctx, pieces, chunk, rows, *refs
):
    n_in = refs[:pieces]
    g_in = refs[pieces : 2 * pieces]
    wg_hbm, wu_hbm, wd_hbm = refs[2 * pieces : 2 * pieces + 3]
    outs = refs[2 * pieces + 3 : 2 * pieces + 9]
    (
        n_all, g_all, wg_buf, wu_buf, wd_buf, act, d_gate, d_up,
        give, take, in_sem, w_sem, send_sem, recv_sem,
    ) = refs[2 * pieces + 9 :]
    tokens, width = n_all.shape
    units = act.shape[1]
    me = lax.axis_index("ctx")
    core = me % 2
    xpos = me // 2
    nx = nctx // 2
    start = lax.axis_index("dp") * units
    mate = {"ctx": me + 1 - 2 * core}

    barrier = pltpu.get_barrier_semaphore()
    pl.semaphore_signal(barrier, inc=1, device_id=mate, device_id_type=pl.DeviceIdType.MESH)

    loads = []
    for which, (srcs, dst) in enumerate(((n_in, n_all), (g_in, g_all))):
        at = 0
        for i, src in enumerate(srcs):
            n = src.shape[0]
            loads.append(
                pltpu.make_async_copy(src, dst.at[pl.ds(at, n)], in_sem.at[which * pieces + i])
            )
            at += n

    def weights(j, slot):
        at = pl.multiple_of(start + j * chunk, chunk)
        return (
            pltpu.make_async_copy(wg_hbm.at[:, pl.ds(at, chunk)], wg_buf.at[slot], w_sem.at[slot, 0]),
            pltpu.make_async_copy(wu_hbm.at[:, pl.ds(at, chunk)], wu_buf.at[slot], w_sem.at[slot, 1]),
            pltpu.make_async_copy(wd_hbm.at[pl.ds(at, chunk)], wd_buf.at[slot], w_sem.at[slot, 2]),
        )

    for copy in weights(0, 0):
        copy.start()
    for copy in loads:
        copy.start()
    for copy in loads:
        copy.wait()

    count = units // chunk

    @pl.loop(0, count)
    def _(j):
        slot = j % 2
        for copy in weights(j, slot):
            copy.wait()

        @pl.when(j + 1 < count)
        def _():
            for copy in weights(j + 1, 1 - slot):
                copy.start()

        cols = pl.ds(pl.multiple_of(j * chunk, chunk), chunk)

        @pl.loop(0, tokens // rows)
        def _(i):
            some = pl.ds(pl.multiple_of(i * rows, rows), rows)
            gate = nn(n_all[some], wg_buf[slot])
            up = nn(n_all[some], wu_buf[slot])
            d_act = nt(g_all[some], wd_buf[slot])
            a, dg, du = gate_parts(gate, up, d_act)
            act[some, cols] = a
            d_gate[some, cols] = dg
            d_up[some, cols] = du

    pl.semaphore_wait(barrier, 1)

    part = width // (ndp * nctx)
    terms = ((g_all, act), (n_all, d_gate), (n_all, d_up))

    def product(w, x, c):
        left, right = terms[w]
        block = jnp.concatenate(
            [
                left[:, pl.ds(pl.multiple_of((z * nctx + x * 2 + c) * part, part), part)]
                for z in range(ndp)
            ],
            axis=1,
        )
        return tn(block, right[...])

    copies = [
        pltpu.make_async_remote_copy(
            src_ref=give.at[w],
            dst_ref=take.at[w],
            send_sem=send_sem.at[w],
            recv_sem=recv_sem.at[w],
            device_id=mate,
            device_id_type=pl.DeviceIdType.MESH,
        )
        for w in range(3)
    ]

    def hand(w):
        for i in range(nx):
            x = (xpos + 1 + i) % nx
            give[w, i] = product(w, x, 1 - core).astype(BF)
        copies[w].start()

    def keep(w):
        parts = [product(w, (xpos + 1 + i) % nx, core) for i in range(nx)]
        copies[w].wait()
        for i in range(nx):
            outs[2 * w + i][...] = (parts[i] + take[w, i].astype(F32)).astype(BF)

    hand(0)
    hand(1)
    keep(0)
    hand(2)
    keep(1)
    keep(2)


def unit_grads(n_pieces, g_pieces, wg, wu, wd, ndp, nctx, chunk=256, rows=512):
    pieces = len(n_pieces)
    tokens = sum(p.shape[0] for p in n_pieces)
    width = wg.shape[0]
    units = wg.shape[1] // ndp
    part = width // (ndp * nctx)
    nx = nctx // 2
    hbm = pl.BlockSpec(memory_space=pl.ANY)
    vmem = pl.BlockSpec(memory_space=pltpu.VMEM)
    return pl.pallas_call(
        functools.partial(unit_grads_kernel, ndp, nctx, pieces, chunk, rows),
        in_specs=[hbm] * (2 * pieces + 3),
        out_specs=[vmem] * 6,
        out_shape=[jax.ShapeDtypeStruct((ndp * part, units), BF)] * 6,
        scratch_shapes=[
            pltpu.VMEM((tokens, width), BF),
            pltpu.VMEM((tokens, width), BF),
            pltpu.VMEM((2, width, chunk), BF),
            pltpu.VMEM((2, width, chunk), BF),
            pltpu.VMEM((2, chunk, width), BF),
            pltpu.VMEM((tokens, units), BF),
            pltpu.VMEM((tokens, units), BF),
            pltpu.VMEM((tokens, units), BF),
            pltpu.VMEM((3, nx, ndp * part, units), BF),
            pltpu.VMEM((3, nx, ndp * part, units), BF),
            pltpu.SemaphoreType.DMA((2 * pieces,)),
            pltpu.SemaphoreType.DMA((2, 3)),
            pltpu.SemaphoreType.DMA((3,)),
            pltpu.SemaphoreType.DMA((3,)),
        ],
        compiler_params=pltpu.CompilerParams(
            vmem_limit_bytes=VMEM_MOST, collective_id=0, has_side_effects=True
        ),
        cost_estimate=cost(12 * tokens * width * units, 2 * (2 * tokens + 3 * units) * width),
        name="unit_grads",
    )(*n_pieces, *g_pieces, wg, wu, wd)


def dot_plain(left, right):
    return jnp.dot(left, right, preferred_element_type=F32)


def dot_right(left, right):
    return lax.dot_general(left, right, (((1,), (1,)), ((), ())), preferred_element_type=F32)


def dot_left(left, right):
    return lax.dot_general(left, right, (((0,), (0,)), ((), ())), preferred_element_type=F32)


def normed(v, gain):
    return v * lax.rsqrt(jnp.mean(v * v, axis=-1, keepdims=True) + EPS) * gain


def norm_back(v, gain, grad):
    factor = lax.rsqrt(jnp.mean(v * v, axis=-1, keepdims=True) + EPS)
    unit = v * factor
    d_unit = grad * gain
    d_gain = jnp.sum(grad * unit, axis=0)
    d_v = factor * (d_unit - unit * jnp.mean(d_unit * unit, axis=-1, keepdims=True))
    return (d_v, d_gain)


def rotate(t, cosine, sine):
    half = t.shape[-1] // 2
    first, second = (t[..., :half], t[..., half:])
    return jnp.concatenate(
        [first * cosine - second * sine, second * cosine + first * sine], axis=-1
    )


def rotate_back(t, cosine, sine):
    half = t.shape[-1] // 2
    first, second = (t[..., :half], t[..., half:])
    return jnp.concatenate(
        [first * cosine + second * sine, second * cosine - first * sine], axis=-1
    )


def score_block(query5, key_all, allowed):
    scores = jnp.einsum(
        "scngd,slnd->sngcl", query5, key_all, preferred_element_type=F32
    ) * HD ** (-0.5)
    return jnp.where(allowed[:, None, None], scores, NEG)


def build(ndp, nctx, nten):
    def pull(v, axis, n, s):
        return lax.ppermute(v, axis, [((i + s) % n, i) for i in range(n)])

    def flip(v, axis, n, bit):
        return lax.ppermute(v, axis, [(i, i ^ bit) for i in range(n)])

    def tensor_sum(v):
        low = v.astype(BF)
        if nten == 2:
            return low.astype(F32) + flip(low, "tensor", 2, 1).astype(F32)
        return lax.psum(low, "tensor").astype(F32)

    def gather_dp(v):
        rows = v.shape[0] // nten
        part = lax.dynamic_slice_in_dim(v, lax.axis_index("tensor") * rows, rows, 0)
        pieces = [v]
        for s in range(1, ndp):
            got = pull(part, "dp", ndp, s)
            pieces.append(got)
            for t in range(1, nten):
                pieces.append(pull(got, "tensor", nten, t))
        return jnp.concatenate(pieces, axis=0)

    def ctx_sum(full):
        r = full.shape[0] // (ndp * nctx)
        me = lax.axis_index("ctx")
        work = full.reshape(ndp, nctx, r, full.shape[1])
        bit = 1
        while bit < nctx:
            left = work.shape[1] // 2
            work = work.reshape(ndp, left, 2, r, full.shape[1])
            mine = (me // bit) % 2
            keep = lax.dynamic_index_in_dim(work, mine, 2, keepdims=False)
            give = lax.dynamic_index_in_dim(work, 1 - mine, 2, keepdims=False)
            got = flip(give, "ctx", nctx, bit)
            work = (keep.astype(F32) + got.astype(F32)).astype(BF)
            bit *= 2
        return work.reshape(ndp, r, full.shape[1])

    def finish_slices(full):
        got = lax.all_to_all(ctx_sum(full), "dp", 0, 0, tiled=True)
        return jnp.swapaxes(got, 0, 1).reshape(got.shape[1], -1).astype(F32)

    def finish_sum(full):
        got = lax.all_to_all(ctx_sum(full), "dp", 0, 0, tiled=True)
        return jnp.sum(got.astype(F32), axis=0)

    def local(
        layer_input,
        output_grad,
        prefix,
        attn_gain,
        w_query,
        w_key,
        w_value,
        w_out,
        mlp_gain,
        w_gate,
        w_up,
        w_down,
    ):
        seqs, span, width = layer_input.shape
        q_heads = w_query.shape[1] // HD
        kv_heads = w_key.shape[1] // HD
        group = q_heads // kv_heads
        zi = lax.axis_index("dp")
        rows = layer_input.astype(F32).reshape(seqs * span, width)
        grad_low = output_grad.reshape(seqs * span, width)
        grad_rows = grad_low.astype(F32)
        grad_all = gather_dp(grad_low)

        first = lax.axis_index("ctx") * span
        position = (first + jnp.arange(span)).astype(F32)
        frequency = ROPE_BASE ** (-jnp.arange(HD // 2).astype(F32) * 2.0 / HD)
        angle = position[:, None] * frequency[None, :]
        cosine = jnp.cos(angle)[None, :, None, :]
        sine = jnp.sin(angle)[None, :, None, :]
        normed1 = normed(rows, attn_gain).astype(BF)
        query = rotate(
            dot_plain(normed1, w_query).reshape(seqs, span, q_heads, HD), cosine, sine
        ).astype(BF)
        keyed = rotate(
            dot_plain(normed1, w_key).reshape(seqs, span, kv_heads, HD), cosine, sine
        ).astype(BF)
        valued = dot_plain(normed1, w_value).astype(BF).reshape(seqs, span, kv_heads * HD)
        key_all, value_all = (
            lax.all_gather(
                keyed.reshape(seqs, span, kv_heads * HD), "ctx", axis=1, tiled=True
            ),
            lax.all_gather(valued, "ctx", axis=1, tiled=True),
        )
        length = key_all.shape[1]
        key_all = key_all.reshape(seqs, length, kv_heads, HD)
        value_all = value_all.reshape(seqs, length, kv_heads, HD)
        query5 = query.reshape(seqs, span, kv_heads, group, HD)
        query_pos = first + jnp.arange(span)
        key_pos = jnp.arange(length)
        allowed = (key_pos[None, None, :] <= query_pos[None, :, None]) | (
            key_pos[None, None, :] < prefix[:, None, None]
        )
        scores = score_block(query5, key_all, allowed)
        top = jnp.max(scores, axis=-1, keepdims=True)
        exponent = jnp.exp(scores - top)
        total = jnp.sum(exponent, axis=-1, keepdims=True)
        log_total = top + jnp.log(total)
        probs_low = (exponent / total).astype(BF)
        attended = jnp.einsum(
            "sngcl,slnd->scngd", probs_low, value_all, preferred_element_type=F32
        )
        attended = attended.astype(BF).reshape(seqs * span, q_heads * HD)
        resid = rows + tensor_sum(dot_plain(attended, w_out))
        normed2 = normed(resid, mlp_gain).astype(BF)
        normed2_all = gather_dp(normed2)
        gate = dot_plain(normed2, w_gate)
        up = dot_plain(normed2, w_up)
        act = (jax.nn.silu(gate) * up).astype(BF)

        def mlp_back(gate, up, d_act):
            sigmoid_gate = jax.nn.sigmoid(gate)
            d_gate_pre = (
                d_act * up * sigmoid_gate * (1.0 + gate * (1.0 - sigmoid_gate))
            ).astype(BF)
            d_up_pre = (d_act * gate * sigmoid_gate).astype(BF)
            return d_gate_pre, d_up_pre

        d_act = dot_right(grad_low, w_down)
        d_gate_pre, d_up_pre = mlp_back(gate, up, d_act)
        back_terms = dot_right(d_gate_pre, w_gate) + dot_right(d_up_pre, w_up)
        d_normed2 = tensor_sum(back_terms)
        output = (resid + tensor_sum(dot_plain(act, w_down))).astype(BF)
        output = output.reshape(seqs, span, width)

        units = w_gate.shape[1] // ndp
        wg = lax.dynamic_slice_in_dim(w_gate, zi * units, units, 1)
        wu = lax.dynamic_slice_in_dim(w_up, zi * units, units, 1)
        wd = lax.dynamic_slice_in_dim(w_down, zi * units, units, 0)
        gate_s = dot_plain(normed2_all, wg)
        up_s = dot_plain(normed2_all, wu)
        d_act_s = dot_right(grad_all, wd)
        act_s = (jax.nn.silu(gate_s) * up_s).astype(BF)
        d_gate_s, d_up_s = mlp_back(gate_s, up_s, d_act_s)
        s_down = finish_slices(dot_left(grad_all, act_s).astype(BF)).T
        s_gate = finish_slices(dot_left(normed2_all, d_gate_s).astype(BF))
        s_up = finish_slices(dot_left(normed2_all, d_up_s).astype(BF))

        d_resid_norm, g_mlp_gain = norm_back(resid, mlp_gain, d_normed2)
        d_resid = grad_rows + d_resid_norm
        d_resid_low = d_resid.astype(BF)
        s_out = finish_sum(dot_left(d_resid_low, attended).astype(BF)).T
        d_attended = dot_right(d_resid_low, w_out).astype(BF).reshape(query5.shape)
        scores = score_block(query5, key_all, allowed)
        probs = jnp.exp(scores - log_total)
        probs_low = probs.astype(BF)
        d_probs = jnp.einsum(
            "scngd,slnd->sngcl", d_attended, value_all, preferred_element_type=F32
        )
        delta = jnp.sum(probs * d_probs, axis=-1, keepdims=True)
        d_scores = (probs * (d_probs - delta)).astype(BF)
        scale = HD ** (-0.5)
        d_query = (
            jnp.einsum("sngcl,slnd->scngd", d_scores, key_all, preferred_element_type=F32) * scale
        )
        d_key_all = (
            jnp.einsum("sngcl,scngd->slnd", d_scores, query5, preferred_element_type=F32) * scale
        )
        d_value_all = jnp.einsum(
            "sngcl,scngd->slnd", probs_low, d_attended, preferred_element_type=F32
        )
        d_kv = jnp.concatenate(
            [
                d_key_all.reshape(length, kv_heads * HD).astype(BF),
                d_value_all.reshape(length, kv_heads * HD).astype(BF),
            ],
            axis=1,
        )
        d_kv = lax.psum_scatter(d_kv, "ctx", scatter_dimension=0, tiled=True).astype(F32)
        d_key, d_val = d_kv[:, : kv_heads * HD], d_kv[:, kv_heads * HD :]
        d_qp = (
            rotate_back(d_query.reshape(seqs, span, q_heads, HD), cosine, sine)
            .astype(BF)
            .reshape(seqs * span, q_heads * HD)
        )
        d_kp = (
            rotate_back(d_key.reshape(seqs, span, kv_heads, HD), cosine, sine)
            .astype(BF)
            .reshape(seqs * span, kv_heads * HD)
        )
        d_vp = d_val.astype(BF).reshape(seqs * span, kv_heads * HD)
        front_terms = dot_right(d_qp, w_query) + dot_right(d_kp, w_key) + dot_right(d_vp, w_value)
        d_normed1 = tensor_sum(front_terms)
        d_rows_norm, g_attn_gain = norm_back(rows, attn_gain, d_normed1)
        d_input = d_resid + d_rows_norm
        d_input = d_input.reshape(seqs, span, width)
        s_qkv = finish_sum(
            dot_left(normed1, jnp.concatenate([d_qp, d_kp, d_vp], axis=1)).astype(BF)
        )
        nq, nk = q_heads * HD, kv_heads * HD
        s_query, s_key, s_value = s_qkv[:, :nq], s_qkv[:, nq : nq + nk], s_qkv[:, nq + nk :]
        gains = jnp.stack([g_attn_gain, g_mlp_gain])
        gains = lax.psum_scatter(gains, ("dp", "ctx"), scatter_dimension=1, tiled=True)
        return (
            output,
            d_input,
            gains[0],
            s_query,
            s_key,
            s_value,
            s_out,
            gains[1],
            s_gate,
            s_up,
            s_down,
        )

    return local


def suits(ndp, nctx, nten, layer_input, output_grad, prefix, attn_gain, w_query, w_key, w_value, w_out, mlp_gain, w_gate, w_up, w_down):
    seqs, span, width = layer_input.shape
    return (
        seqs == 1
        and nctx == 4
        and nten == 2
        and ndp > 1
        and span % 256 == 0
        and width % (128 * ndp * nctx) == 0
        and w_key.shape[1] % 128 == 0
        and w_query.shape[1] % 256 == 0
        and w_gate.shape[1] % (512 * ndp) == 0
    )


def build_fast(ndp, nctx, nten):
    def pull(v, axis, n, s):
        return lax.ppermute(v, axis, [((i + s) % n, i) for i in range(n)])

    def flip(v, axis, n, bit):
        return lax.ppermute(v, axis, [(i, i ^ bit) for i in range(n)])

    def gather_dp(v):
        half = v.shape[0] // 2
        part = lax.dynamic_slice_in_dim(v, lax.axis_index("tensor") * half, half, 0)
        pieces = [v]
        for s in range(1, ndp):
            got = pull(part, "dp", ndp, s)
            pieces += [got, flip(got, "tensor", 2, 1)]
        return pieces

    def ctx_sum(full):
        r = full.shape[0] // (ndp * nctx)
        me = lax.axis_index("ctx")
        work = full.reshape(ndp, nctx, r, full.shape[1])
        bit = 1
        while bit < nctx:
            left = work.shape[1] // 2
            work = work.reshape(ndp, left, 2, r, full.shape[1])
            mine = (me // bit) % 2
            keep = lax.dynamic_index_in_dim(work, mine, 2, keepdims=False)
            give = lax.dynamic_index_in_dim(work, 1 - mine, 2, keepdims=False)
            got = flip(give, "ctx", nctx, bit)
            work = (keep.astype(F32) + got.astype(F32)).astype(BF)
            bit *= 2
        return work.reshape(ndp, r, full.shape[1])

    def finish_sum(full):
        got = lax.all_to_all(ctx_sum(full), "dp", 0, 0, tiled=True)
        return jnp.sum(got.astype(F32), axis=0)

    def local(
        layer_input,
        output_grad,
        prefix,
        attn_gain,
        w_query,
        w_key,
        w_value,
        w_out,
        mlp_gain,
        w_gate,
        w_up,
        w_down,
    ):
        seqs, span, width = layer_input.shape
        kvw = w_key.shape[1]
        low = layer_input.reshape(span, width)
        rows = low.astype(F32)
        grad_low = output_grad.reshape(span, width)
        grad_pieces = gather_dp(grad_low)
        first = lax.axis_index("ctx") * span
        where = jnp.stack([first, prefix[0]]).astype(jnp.int32)
        cosine, sine = rope_tables(first, span)
        normed1, query, kv = qkv(low, attn_gain, w_query, w_key, w_value, cosine, sine)
        kv_all = lax.all_gather(kv, "ctx", axis=0, tiled=True)
        attended, lse = attend(where, query, kv_all)
        part = dot_plain(attended, w_out).astype(BF)
        resid = rows + (part.astype(F32) + flip(part, "tensor", 2, 1).astype(F32))
        normed2 = normed(resid, mlp_gain).astype(BF)
        normed2_pieces = gather_dp(normed2)

        out_part, back_part = mlp(normed2, grad_low, w_gate, w_up, w_down)
        back = back_part.astype(F32) + flip(back_part, "tensor", 2, 1).astype(F32)
        output = resid + (out_part.astype(F32) + flip(out_part, "tensor", 2, 1).astype(F32))
        output = output.astype(BF).reshape(seqs, span, width)

        pairs = unit_grads(normed2_pieces, grad_pieces, w_gate, w_up, w_down, ndp, nctx)
        grads = []
        for w in range(3):
            give, keep = pairs[2 * w : 2 * w + 2]
            got = flip(give, "ctx", nctx, 2)
            total = (keep.astype(F32) + got.astype(F32)).astype(BF)
            total = total.reshape(ndp, -1, total.shape[1])
            grads.append(lax.all_to_all(total, "dp", 0, 0, tiled=True))
        s_down = jnp.swapaxes(grads[0], 1, 2).reshape(w_down.shape[0], -1).astype(F32)
        s_gate, s_up = (
            jnp.swapaxes(g, 0, 1).reshape(g.shape[1], -1).astype(F32) for g in grads[1:]
        )

        d_resid_norm, g_mlp_gain = norm_back(resid, mlp_gain, back)
        d_resid = grad_low.astype(F32) + d_resid_norm
        d_resid_low = d_resid.astype(BF)
        d_attended = dot_right(d_resid_low, w_out).astype(BF)
        s_out = finish_sum(dot_left(d_resid_low, attended).astype(BF)).T
        d_qp, d_key, d_value = attend_back(
            where, query, kv_all, d_attended, lse, cosine, sine
        )
        got_key = lax.all_to_all(d_key.reshape(nctx, span, kvw), "ctx", 0, 0, tiled=True)
        got_value = lax.all_to_all(d_value.reshape(nctx, span, kvw), "ctx", 0, 0, tiled=True)
        d_kp, d_vp = kv_back(got_key, got_value, cosine, sine)
        front = dot_right(d_qp, w_query) + dot_right(d_kp, w_key) + dot_right(d_vp, w_value)
        front = front.astype(BF)
        d_normed1 = front.astype(F32) + flip(front, "tensor", 2, 1).astype(F32)
        d_rows_norm, g_attn_gain = norm_back(rows, attn_gain, d_normed1)
        d_input = (d_resid + d_rows_norm).reshape(seqs, span, width)
        s_qkv = finish_sum(
            dot_left(normed1, jnp.concatenate([d_qp, d_kp, d_vp], axis=1)).astype(BF)
        )
        nq = w_query.shape[1]
        s_query, s_key, s_value = s_qkv[:, :nq], s_qkv[:, nq : nq + kvw], s_qkv[:, nq + kvw :]
        gains = jnp.stack([g_attn_gain, g_mlp_gain])
        gains = jnp.swapaxes(gains.reshape(2, ndp * nctx, -1), 0, 1)
        gains = lax.all_to_all(gains, ("dp", "ctx"), 0, 0, tiled=True)
        gains = jnp.sum(gains, axis=0)
        return (
            output,
            d_input,
            gains[0],
            s_query,
            s_key,
            s_value,
            s_out,
            gains[1],
            s_gate,
            s_up,
            s_down,
        )

    return local


def solution(mesh):
    sizes = mesh.shape["dp"], mesh.shape["ctx"], mesh.shape["tensor"]
    plain, fast = build(*sizes), build_fast(*sizes)

    def local(*args):
        return (fast if suits(*sizes, *args) else plain)(*args)

    return jax.shard_map(
        local,
        mesh=mesh,
        in_specs=(
            P("dp", "ctx", None),
            P("dp", "ctx", None),
            P("dp"),
            P(),
            P(None, "tensor"),
            P(None, "tensor"),
            P(None, "tensor"),
            P("tensor", None),
            P(),
            P(None, "tensor"),
            P(None, "tensor"),
            P("tensor", None),
        ),
        out_specs=(
            P("dp", "ctx", None),
            P("dp", "ctx", None),
            P(("dp", "ctx")),
            P(("dp", "ctx"), "tensor"),
            P(("dp", "ctx"), "tensor"),
            P(("dp", "ctx"), "tensor"),
            P("tensor", ("dp", "ctx")),
            P(("dp", "ctx")),
            P(("dp", "ctx"), "tensor"),
            P(("dp", "ctx"), "tensor"),
            P("tensor", ("dp", "ctx")),
        ),
        check_vma=False,
    )
```

```python
import functools
import jax
import jax.numpy as jnp
from jax import lax
from jax.experimental import pallas as pl
from jax.experimental.pallas import tpu as pltpu
from jax.sharding import PartitionSpec as P

HD = 64
EPS = 1e-05
ROPE_BASE = 500000.0
NEG = -1e30
BF = jnp.bfloat16
F32 = jnp.float32
VMEM_MOST = 60 * 1024 * 1024


def cost(flops, nbytes, trans=0):
    return pl.CostEstimate(flops=int(flops), bytes_accessed=int(nbytes), transcendentals=int(trans))


def nt(a, b):
    return lax.dot_general(a, b, (((1,), (1,)), ((), ())), preferred_element_type=F32)


def tn(a, b):
    return lax.dot_general(a, b, (((0,), (0,)), ((), ())), preferred_element_type=F32)


def nn(a, b):
    return jnp.dot(a, b, preferred_element_type=F32)


def swap_halves(t):
    lane = lax.broadcasted_iota(jnp.int32, t.shape, 1) % HD
    n = t.shape[1]
    return jnp.where(
        lane < HD // 2, pltpu.roll(t, n - HD // 2, 1), pltpu.roll(t, HD // 2, 1)
    )


def rope_tables(first, span):
    position = (first + jnp.arange(span)).astype(F32)
    frequency = ROPE_BASE ** (-jnp.arange(HD // 2).astype(F32) * 2.0 / HD)
    angle = position[:, None] * frequency[None, :]
    cosine, sine = jnp.cos(angle), jnp.sin(angle)
    return (
        jnp.concatenate([cosine, cosine, cosine, cosine], axis=1),
        jnp.concatenate([-sine, sine, -sine, sine], axis=1),
    )


def mask_bias(first, prefix, length, span):
    key = lax.broadcasted_iota(jnp.int32, (length, span), 0)
    query = lax.broadcasted_iota(jnp.int32, (length, span), 1) + first
    return jnp.where((key <= query) | (key < prefix), 0.0, NEG).astype(F32)


def gate_parts(gate, up, d_act):
    sig = 1.0 / (1.0 + jnp.exp(-gate))
    silu = gate * sig
    return (
        (silu * up).astype(BF),
        (d_act * up * (sig + silu * (1.0 - sig))).astype(BF),
        (d_act * silu).astype(BF),
    )


MESH = pl.DeviceIdType.MESH


def remote(src, dst, send, recv, to):
    return pltpu.make_async_remote_copy(
        src_ref=src, dst_ref=dst, send_sem=send, recv_sem=recv, device_id=to, device_id_type=MESH
    )


def enter(devices):
    barrier = pltpu.get_barrier_semaphore()
    for to in devices:
        pl.semaphore_signal(barrier, inc=1, device_id=to, device_id_type=MESH)
    pl.semaphore_wait(barrier, len(devices))


def around(z, ndp):
    return [{"dp": lax.rem(z + 1, ndp)}, {"dp": lax.rem(z + ndp - 1, ndp)}]


def mates(me, y):
    return [{"ctx": me ^ 1}, {"ctx": me ^ 2}, {"ctx": me ^ 3}, {"tensor": 1 - y}]


class Relay:
    def __init__(self, z, ndp, hop, own, blocks, sems):
        self.z, self.ndp, self.hop = z, ndp, hop
        self.own, self.blocks, self.sems = own, blocks, sems

    def copy(self, way, block, to):
        src = self.own if self.hop == 1 else self.blocks.at[block]
        at = 0 if way > 0 else 1
        return remote(
            src, self.blocks.at[block], self.sems.at[0, at], self.sems.at[1, at], {"dp": to}
        )

    def each(self, act, incoming):
        z, hop = self.z, self.hop
        for way in (1, -1):
            if incoming:
                block = z - way * hop
                ok = block >= 0 if way > 0 else block < self.ndp
            else:
                block = z - way * (hop - 1)
                ok = (block >= 0) & (z < self.ndp - 1) if way > 0 else (block < self.ndp) & (z > 0)

            @pl.when(ok)
            def _(way=way, block=block):
                act(self.copy(way, block, z if incoming else z + way))

    def start(self):
        self.each(lambda c: c.start(), False)

    def wait_recv(self):
        self.each(lambda c: c.wait_recv(), True)

    def wait_send(self):
        self.each(lambda c: c.wait_send(), False)


def rope_parts(t, cosine, sine):
    pieces = []
    for i in range(t.shape[1] // 128):
        part = t[:, 128 * i : 128 * (i + 1)]
        pieces.append((part * cosine + swap_halves(part) * sine).astype(BF))
    return pieces


def front_kernel(
    ndp, nctx, group,
    where_ref, x_ref, gain1_ref, wq_hbm, wk_hbm, wv_hbm, wo_hbm, cos_ref, sin_ref, gain2_ref, og_hbm,
    n1_ref, q_ref, kv_out, att_ref, lse_ref, resid_ref, n2_ref, og_all,
    n1_buf, wq, wk, wv, wo, kv, bias_ref, part, part_got,
    w_sem, kv_sem, kv_out_sem, part_sem, z_sem,
):
    z, me, y = lax.axis_index("dp"), lax.axis_index("ctx"), lax.axis_index("tensor")
    span, width = x_ref.shape
    length = kv.shape[0]
    kvw = wk.shape[1]
    loads = [
        pltpu.make_async_copy(src, dst, w_sem.at[i])
        for i, (src, dst) in enumerate(((wk_hbm, wk), (wv_hbm, wv), (wq_hbm, wq), (wo_hbm, wo)))
    ]
    for copy in loads:
        copy.start()
    hop1 = Relay(z, ndp, 1, og_hbm, og_all, z_sem.at[0])
    hop2 = Relay(z, ndp, 2, og_hbm, og_all, z_sem.at[1])
    enter(around(z, ndp) + mates(me, y))
    hop1.start()
    v = x_ref[...].astype(F32)
    factor = lax.rsqrt(jnp.mean(v * v, axis=-1, keepdims=True) + EPS)
    n1_buf[...] = (v * factor * gain1_ref[...]).astype(BF)
    cosine, sine = cos_ref[...], sin_ref[...]
    mine = pl.ds(pl.multiple_of(me * span, span), span)
    loads[0].wait()
    for i, piece in enumerate(rope_parts(nn(n1_buf[...], wk[...]), cosine, sine)):
        kv[mine, 128 * i : 128 * (i + 1)] = piece
    loads[1].wait()
    kv[mine, kvw:] = nn(n1_buf[...], wv[...]).astype(BF)

    def kv_copy(which, block, mask):
        rows = pl.ds(pl.multiple_of(block * span, span), span)
        return remote(kv.at[rows], kv.at[rows], kv_sem.at[0, which], kv_sem.at[1, which], {"ctx": me ^ mask})

    to_x = kv_copy(0, me, 2)
    to_core = kv_copy(1, me, 1)
    onward = kv_copy(2, me ^ 2, 1)
    to_x.start()
    to_core.start()
    loads[2].wait()
    for i, piece in enumerate(rope_parts(nn(n1_buf[...], wq[...]), cosine, sine)):
        q_ref[:, 128 * i : 128 * (i + 1)] = piece
    part_width = width // (ndp * nctx)
    for p in range(nctx):
        for b in range(ndp):
            at = (b * nctx + p) * part_width
            n1_ref[p, :, b * part_width : (b + 1) * part_width] = n1_buf[:, at : at + part_width]
    bias_ref[...] = mask_bias(where_ref[0], where_ref[1], length, span)
    to_x.wait_recv()
    onward.start()
    to_core.wait_recv()
    onward.wait_recv()
    to_x.wait_send()
    to_core.wait_send()
    onward.wait_send()
    save_kv = pltpu.make_async_copy(kv, kv_out, kv_out_sem)
    save_kv.start()

    wide = 128 * group
    heads = wide // HD

    @pl.loop(0, kvw // 128)
    def _(j):
        lanes = pl.ds(pl.multiple_of(j * wide, 128), wide)
        queries = q_ref[:, lanes] * jnp.asarray(HD**-0.5, BF)
        keys = kv[:, pl.ds(pl.multiple_of(j * 128, 128), 128)]
        values = kv[:, pl.ds(pl.multiple_of(kvw + j * 128, 128), 128)]
        rows, outs = [], []
        for h in range(heads):
            at = slice(HD * (h // group), HD * (h // group + 1))
            scores = nt(keys[:, at], queries[:, HD * h : HD * (h + 1)]) + bias_ref[...]
            top = jnp.max(scores, axis=0, keepdims=True)
            exponent = jnp.exp(scores - top)
            total = jnp.sum(exponent, axis=0, keepdims=True)
            rows.append(top + jnp.log(total))
            outs.append(tn(values[:, at], exponent.astype(BF)) / total)
            if h % 2:
                both = jnp.concatenate(outs, axis=0).T.astype(BF)
                att_ref[:, pl.ds(pl.multiple_of(j * wide + HD * (h - 1), 128), 128)] = both
                outs = []
        lse_ref[pl.ds(pl.multiple_of(j * heads, heads), heads), :] = jnp.concatenate(rows, axis=0)

    save_kv.wait()
    loads[3].wait()
    count, _, cols = part.shape
    copies = [
        remote(part.at[c], part_got.at[c], part_sem.at[0, c], part_sem.at[1, c], {"tensor": 1 - y})
        for c in range(count)
    ]
    for c in range(count):
        part[c] = nn(att_ref[...], wo[:, c * cols : (c + 1) * cols]).astype(BF)
        copies[c].start()
    hop1.wait_recv()
    hop2.start()
    square = jnp.zeros((span, 1), F32)
    for c in range(count):
        at = slice(c * cols, (c + 1) * cols)
        copies[c].wait_recv()
        r = x_ref[:, at].astype(F32) + (part[c].astype(F32) + part_got[c].astype(F32))
        resid_ref[:, at] = r
        square += jnp.sum(r * r, axis=-1, keepdims=True)
    factor = lax.rsqrt(square / width + EPS)
    for c in range(count):
        at = slice(c * cols, (c + 1) * cols)
        n2_ref[:, at] = (resid_ref[:, at] * factor * gain2_ref[:, at]).astype(BF)
    for copy in copies:
        copy.wait_send()
    hop1.wait_send()
    hop2.wait_recv()
    hop2.wait_send()


HBM_SPEC = pl.BlockSpec(memory_space=pl.ANY)
VMEM_SPEC = pl.BlockSpec(memory_space=pltpu.VMEM)
SMEM_SPEC = pl.BlockSpec(memory_space=pltpu.SMEM)


def own(number):
    return pltpu.CompilerParams(
        vmem_limit_bytes=VMEM_MOST, collective_id=number, has_side_effects=True
    )


def front(where, x, gain1, wq, wk, wv, wo, cosine, sine, gain2, og, ndp, nctx):
    span, width = x.shape
    qw, kvw = wq.shape[1], wk.shape[1]
    group = qw // kvw
    length = span * nctx
    chunks = 4
    dma = pltpu.SemaphoreType.DMA
    return pl.pallas_call(
        functools.partial(front_kernel, ndp, nctx, group),
        in_specs=[SMEM_SPEC, VMEM_SPEC, VMEM_SPEC] + [HBM_SPEC] * 4 + [VMEM_SPEC] * 3 + [HBM_SPEC],
        out_specs=[VMEM_SPEC, VMEM_SPEC, HBM_SPEC] + [VMEM_SPEC] * 4 + [HBM_SPEC],
        out_shape=[
            jax.ShapeDtypeStruct((nctx, span, width // nctx), BF),
            jax.ShapeDtypeStruct((span, qw), BF),
            jax.ShapeDtypeStruct((length, 2 * kvw), BF),
            jax.ShapeDtypeStruct((span, qw), BF),
            jax.ShapeDtypeStruct((qw // HD, span), F32),
            jax.ShapeDtypeStruct((span, width), F32),
            jax.ShapeDtypeStruct((span, width), BF),
            jax.ShapeDtypeStruct((ndp, span, width), BF),
        ],
        scratch_shapes=[
            pltpu.VMEM((span, width), BF),
            pltpu.VMEM((width, qw), BF),
            pltpu.VMEM((width, kvw), BF),
            pltpu.VMEM((width, kvw), BF),
            pltpu.VMEM((qw, width), BF),
            pltpu.VMEM((length, 2 * kvw), BF),
            pltpu.VMEM((length, span), F32),
            pltpu.VMEM((chunks, span, width // chunks), BF),
            pltpu.VMEM((chunks, span, width // chunks), BF),
            dma((4,)),
            dma((2, 3)),
            dma,
            dma((2, chunks)),
            dma((2, 2, 2)),
        ],
        compiler_params=own(0),
        cost_estimate=cost(2 * span * width * (2 * qw + 2 * kvw), 4 * width * (qw + kvw)),
        name="front",
    )(where, x, gain1.reshape(1, width), wq, wk, wv, wo, cosine, sine, gain2.reshape(1, width), og)


def middle_kernel(
    ndp, nctx,
    n_ref, g_ref, wg_ref, wu_ref, wd_ref, resid_ref, gain_ref, n_hbm, n1_hbm, att_hbm,
    o_ref, dr_ref, low_ref, lowp_ref, gain_grad_ref, n_all, n1_all, att_all,
    o_acc, dn_acc, part, part_got,
    part_sem, z_sem, n1_sem, att_sem,
):
    z, me, y = lax.axis_index("dp"), lax.axis_index("ctx"), lax.axis_index("tensor")
    j = pl.program_id(0)
    last = pl.num_programs(0) - 1
    hop1 = Relay(z, ndp, 1, n_hbm, n_all, z_sem.at[0])
    hop2 = Relay(z, ndp, 2, n_hbm, n_all, z_sem.at[1])
    spreads = []
    for m in range(1, nctx):
        spreads.append(
            remote(n1_hbm.at[me ^ m], n1_all.at[me], n1_sem.at[0, m], n1_sem.at[1, m], {"ctx": me ^ m})
        )
        spreads.append(
            remote(att_hbm, att_all.at[me], att_sem.at[0, m], att_sem.at[1, m], {"ctx": me ^ m})
        )
    count, span, cols = part.shape
    width = count * cols
    copies = [
        remote(part.at[c], part_got.at[c], part_sem.at[0, c], part_sem.at[1, c], {"tensor": 1 - y})
        for c in range(count)
    ]

    @pl.when(j == 0)
    def _():
        enter(around(z, ndp) + mates(me, y))
        hop1.start()
        for copy in spreads:
            copy.start()

    normed2, grad = n_ref[...], g_ref[...]
    gate = nn(normed2, wg_ref[...])
    up = nn(normed2, wu_ref[...])
    d_act = nt(grad, wd_ref[...])
    act, d_gate, d_up = gate_parts(gate, up, d_act)

    @pl.when(j == 0)
    def _():
        o_acc[...] = nn(act, wd_ref[...])
        dn_acc[...] = nt(d_gate, wg_ref[...]) + nt(d_up, wu_ref[...])

    @pl.when(j > 0)
    def _():
        o_acc[...] += nn(act, wd_ref[...])
        dn_acc[...] += nt(d_gate, wg_ref[...]) + nt(d_up, wu_ref[...])

    @pl.when(j == last - 1)
    def _():
        hop1.wait_recv()
        hop2.start()

    @pl.when(j == last)
    def _():
        for c in range(count):
            part[c] = dn_acc[:, c * cols : (c + 1) * cols].astype(BF)
            copies[c].start()
        o_ref[...] = o_acc[...].astype(BF)
        v = resid_ref[...]
        factor = lax.rsqrt(jnp.mean(v * v, axis=-1, keepdims=True) + EPS)
        for copy in copies:
            copy.wait_recv()
        dots = jnp.zeros((span, 1), F32)
        for c in range(count):
            at = slice(c * cols, (c + 1) * cols)
            unit = resid_ref[:, at] * factor
            back = part[c].astype(F32) + part_got[c].astype(F32)
            term = back * unit
            gain_grad_ref[:, at] = jnp.sum(term, axis=0, keepdims=True)
            dots += jnp.sum(term * gain_ref[:, at], axis=-1, keepdims=True)
        dots = dots / width
        for c in range(count):
            at = slice(c * cols, (c + 1) * cols)
            unit = resid_ref[:, at] * factor
            back = part[c].astype(F32) + part_got[c].astype(F32)
            total = g_ref[:, at].astype(F32) + factor * (back * gain_ref[:, at] - unit * dots)
            dr_ref[:, at] = total
            low_ref[:, at] = total.astype(BF)
        part_width = width // (ndp * nctx)
        for p in range(nctx):
            for b in range(ndp):
                at = (b * nctx + p) * part_width
                lowp_ref[p, :, b * part_width : (b + 1) * part_width] = low_ref[:, at : at + part_width]
        for copy in copies:
            copy.wait_send()
        for copy in spreads:
            copy.wait()
        hop1.wait_send()
        hop2.wait_recv()
        hop2.wait_send()


def middle(n2, og, wg, wu, wd, resid, gain, n1p, att, ndp, nctx, step=512):
    span, width = n2.shape
    units = wg.shape[1]
    chunks = 4
    dma = pltpu.SemaphoreType.DMA
    whole = pl.BlockSpec((span, width), lambda j: (0, 0))
    row = pl.BlockSpec((1, width), lambda j: (0, 0))
    cols = pl.BlockSpec((width, step), lambda j: (0, j))
    return pl.pallas_call(
        functools.partial(middle_kernel, ndp, nctx),
        grid=(units // step,),
        in_specs=[
            whole, whole, cols, cols, pl.BlockSpec((step, width), lambda j: (j, 0)), whole, row,
            HBM_SPEC, HBM_SPEC, HBM_SPEC,
        ],
        out_specs=[
            whole, whole, whole, pl.BlockSpec((nctx, span, width // nctx), lambda j: (0, 0, 0)), row,
            HBM_SPEC, HBM_SPEC, HBM_SPEC,
        ],
        out_shape=[
            jax.ShapeDtypeStruct((span, width), BF),
            jax.ShapeDtypeStruct((span, width), F32),
            jax.ShapeDtypeStruct((span, width), BF),
            jax.ShapeDtypeStruct((nctx, span, width // nctx), BF),
            jax.ShapeDtypeStruct((1, width), F32),
            jax.ShapeDtypeStruct((ndp, span, width), BF),
            jax.ShapeDtypeStruct((nctx, span, width // nctx), BF),
            jax.ShapeDtypeStruct((nctx,) + att.shape, BF),
        ],
        scratch_shapes=[
            pltpu.VMEM((span, width), F32),
            pltpu.VMEM((span, width), F32),
            pltpu.VMEM((chunks, span, width // chunks), BF),
            pltpu.VMEM((chunks, span, width // chunks), BF),
            dma((2, chunks)),
            dma((2, 2, 2)),
            dma((2, nctx)),
            dma((2, nctx)),
        ],
        compiler_params=own(1),
        cost_estimate=cost(12 * span * width * units, 6 * width * units),
        name="middle",
    )(n2, og, wg, wu, wd, resid, gain.reshape(1, width), n2, n1p, att)


def halves(y, span):
    return pl.ds(pl.multiple_of(y * (span // 2), span // 2), span // 2)


class Far:
    def __init__(self, z, y, blocks, far, sems):
        self.z, self.far = z, far
        rows = halves(y, far.shape[0])
        block = jnp.where(z == 1, 3, 0)
        to = jnp.where(z == 1, 0, 3)
        self.over = remote(
            blocks.at[block, rows], far.at[rows], sems.at[0, 0], sems.at[1, 0], {"dp": to}
        )
        self.swap = remote(
            far.at[rows], far.at[rows], sems.at[0, 1], sems.at[1, 1], {"tensor": 1 - y}
        )
        self.gives = (z == 1) | (z == 2)
        self.takes = (z == 0) | (z == 3)

    def start(self):
        pl.when(self.gives)(lambda: self.over.start())

    def onward(self):
        @pl.when(self.takes)
        def _():
            self.over.wait_recv()
            self.swap.start()

    def wait_recv(self):
        pl.when(self.takes)(lambda: self.swap.wait_recv())

    def finish(self):
        pl.when(self.takes)(lambda: self.swap.wait_send())
        pl.when(self.gives)(lambda: self.over.wait_send())


def back_kernel(
    ndp, nctx, group,
    where_ref, q_ref, kv_ref, low_ref, lse_ref, cos_ref, sin_ref,
    wq_hbm, wk_hbm, wv_hbm, wo_hbm, lowp_hbm, n_all,
    dqkv_ref, front_ref, low_all, n_far,
    wq, wk, wv, wo, d_att, bias_ref, dkv, land, acc,
    w_sem, low_sem, far_sem, dkv_sem,
):
    z, me, y = lax.axis_index("dp"), lax.axis_index("ctx"), lax.axis_index("tensor")
    span, qw = q_ref.shape
    length = kv_ref.shape[0]
    kvw = kv_ref.shape[1] // 2
    loads = [
        pltpu.make_async_copy(src, dst, w_sem.at[i])
        for i, (src, dst) in enumerate(((wo_hbm, wo), (wq_hbm, wq), (wk_hbm, wk), (wv_hbm, wv)))
    ]
    for copy in loads:
        copy.start()
    far = Far(z, y, n_all, n_far, far_sem)
    spreads = [
        remote(lowp_hbm.at[me ^ m], low_all.at[me], low_sem.at[0, m], low_sem.at[1, m], {"ctx": me ^ m})
        for m in range(1, nctx)
    ]
    enter(around(z, ndp) + mates(me, y))
    far.start()
    for copy in spreads:
        copy.start()
    bias_ref[...] = mask_bias(where_ref[0], where_ref[1], length, span)
    loads[0].wait()
    d_att[...] = nt(low_ref[...], wo[...]).astype(BF)
    wide = 128 * group
    heads = wide // HD
    blocks = kvw // 128
    scale = jnp.asarray(HD**-0.5, BF)

    def share(j, m):
        rows = pl.ds(pl.multiple_of((me ^ m) * span, span), span)
        return remote(
            dkv.at[j, rows], land.at[j, m], dkv_sem.at[0, j, m], dkv_sem.at[1, j, m], {"ctx": me ^ m}
        )

    @pl.loop(0, blocks)
    def _(j):
        lanes = pl.ds(pl.multiple_of(j * wide, 128), wide)
        queries = q_ref[:, lanes] * scale
        grads = d_att[:, lanes]
        keys = kv_ref[:, pl.ds(pl.multiple_of(j * 128, 128), 128)]
        values = kv_ref[:, pl.ds(pl.multiple_of(kvw + j * 128, 128), 128)]
        lse = lse_ref[pl.ds(pl.multiple_of(j * heads, heads), heads), :]
        pair = []
        for h in range(heads):
            at = slice(HD * (h // group), HD * (h // group + 1))
            key, value = keys[:, at], values[:, at]
            query = queries[:, HD * h : HD * (h + 1)]
            grad = grads[:, HD * h : HD * (h + 1)]
            probs = jnp.exp(nt(key, query) + (bias_ref[...] - lse[h : h + 1, :]))
            d_probs = nt(value, grad)
            delta = jnp.sum(probs * d_probs, axis=0, keepdims=True)
            d_scores = (probs * (d_probs - delta)).astype(BF)
            d_value = nn(probs.astype(BF), grad)
            d_key = nn(d_scores, query)
            if h % group == 0:
                sum_key, sum_value = d_key, d_value
            else:
                sum_key, sum_value = sum_key + d_key, sum_value + d_value
            if h % group == group - 1:
                dkv[j, :, at] = sum_key.astype(BF)
                dkv[j, :, slice(128 + at.start, 128 + at.stop)] = sum_value.astype(BF)
            pair.append(tn(key * scale, d_scores))
            if h % 2:
                both = jnp.concatenate(pair, axis=0).T
                back = both * cos_ref[...] - swap_halves(both) * sin_ref[...]
                dqkv_ref[:, pl.ds(pl.multiple_of(j * wide + HD * (h - 1), 128), 128)] = back.astype(BF)
                pair = []
        for m in range(1, nctx):
            share(j, m).start()

    far.onward()
    loads[1].wait()
    acc[...] = nt(dqkv_ref[:, :qw], wq[...])
    mine = pl.ds(pl.multiple_of(me * span, span), span)
    for j in range(blocks):
        total = dkv[j, mine].astype(F32)
        for m in range(1, nctx):
            share(j, m).wait_recv()
            total += land[j, m].astype(F32)
        d_key = total[:, :128]
        d_key = d_key * cos_ref[...] - swap_halves(d_key) * sin_ref[...]
        dqkv_ref[:, qw + 128 * j : qw + 128 * (j + 1)] = d_key.astype(BF)
        dqkv_ref[:, qw + kvw + 128 * j : qw + kvw + 128 * (j + 1)] = total[:, 128:].astype(BF)
    loads[2].wait()
    loads[3].wait()
    front_ref[...] = (
        acc[...] + nt(dqkv_ref[:, qw : qw + kvw], wk[...]) + nt(dqkv_ref[:, qw + kvw :], wv[...])
    ).astype(BF)
    for j in range(blocks):
        for m in range(1, nctx):
            share(j, m).wait_send()
    for copy in spreads:
        copy.wait()
    far.wait_recv()
    far.finish()


def back(where, q, kv, low, lse, cosine, sine, wq, wk, wv, wo, lowp, n_all, ndp, nctx):
    span, qw = q.shape
    length = kv.shape[0]
    kvw = kv.shape[1] // 2
    width = low.shape[1]
    dma = pltpu.SemaphoreType.DMA
    return pl.pallas_call(
        functools.partial(back_kernel, ndp, nctx, qw // kvw),
        in_specs=[SMEM_SPEC] + [VMEM_SPEC] * 6 + [HBM_SPEC] * 6,
        out_specs=[VMEM_SPEC] * 2 + [HBM_SPEC] * 2,
        out_shape=[
            jax.ShapeDtypeStruct((span, qw + 2 * kvw), BF),
            jax.ShapeDtypeStruct((span, width), BF),
            jax.ShapeDtypeStruct((nctx, span, width // nctx), BF),
            jax.ShapeDtypeStruct((span, width), BF),
        ],
        scratch_shapes=[
            pltpu.VMEM((width, qw), BF),
            pltpu.VMEM((width, kvw), BF),
            pltpu.VMEM((width, kvw), BF),
            pltpu.VMEM((qw, width), BF),
            pltpu.VMEM((span, qw), BF),
            pltpu.VMEM((length, span), F32),
            pltpu.VMEM((kvw // 128, length, 256), BF),
            pltpu.VMEM((kvw // 128, nctx, span, 256), BF),
            pltpu.VMEM((span, width), F32),
            dma((4,)),
            dma((2, nctx)),
            dma((2, 2)),
            dma((2, kvw // 128, nctx)),
        ],
        compiler_params=own(2),
        cost_estimate=cost(4 * 10 * length * span * qw, 4 * width * (qw + kvw)),
        name="back",
    )(where, q, kv, low, lse, cosine, sine, wq, wk, wv, wo, lowp, n_all)


def grads_kernel(
    ndp, nctx, chunk, rows,
    n_own, n_near, n_far, g_own, g_near, wg_hbm, wu_hbm, wd_hbm,
    dqkv_hbm, n1_own, n1_near, low_own, low_near, att_own, att_near, front_hbm, out_hbm,
    down_z, gate_z, up_z, att_z, front_got, out_got, g_far,
    n_all, g_all, wg_buf, wu_buf, wd_buf, act, d_gate, d_up,
    give, take, x_give, x_take, x_keep, left1, left2, right1, right2, prod,
    in_sem, l_sem, w_sem, r_sem, core_sem, x_sem, zz_sem, z_own, att_sem, y_sem, far_sem,
):
    z, me, y = lax.axis_index("dp"), lax.axis_index("ctx"), lax.axis_index("tensor")
    tokens, width = n_all.shape
    span = tokens // ndp
    units = act.shape[1]
    core, xpos = me % 2, me // 2
    part = width // (ndp * nctx)
    start = z * units
    peers = [{"dp": lax.rem(z + s, ndp)} for s in range(1, ndp)]

    def block_load(r, own_ref, near, far, dst, sem):
        block = lax.rem(jnp.where(z < ndp // 2, z + r, z + ndp - r), ndp)
        at = dst.at[pl.ds(r * span, span)]
        if r == 0:
            return [(None, pltpu.make_async_copy(own_ref, at, sem))]
        if r < ndp - 1:
            return [(None, pltpu.make_async_copy(near.at[block], at, sem))]
        end = (z == 0) | (z == ndp - 1)
        return [
            (end, pltpu.make_async_copy(far, at, sem)),
            (jnp.logical_not(end), pltpu.make_async_copy(near.at[block], at, sem)),
        ]

    def go(copies):
        for ok, copy in copies:
            if ok is None:
                copy.start()
            else:
                pl.when(ok)(lambda copy=copy: copy.start())

    def done(copies):
        copies[0][1].wait()

    n_loads = [block_load(r, n_own, n_near, n_far, n_all, in_sem.at[0, r]) for r in range(ndp)]
    g_loads = [block_load(r, g_own, g_near, g_far, g_all, in_sem.at[1, r]) for r in range(ndp)]

    def ctx_load(p, own_ref, near, dst, sem):
        at = dst.at[pl.ds(p * span, span)]
        mine = me == p
        return [
            (mine, pltpu.make_async_copy(own_ref, at, sem)),
            (jnp.logical_not(mine), pltpu.make_async_copy(near.at[p], at, sem)),
        ]

    l_loads = []
    for p in range(nctx):
        l_loads.append(ctx_load(p, low_own.at[p], low_near, left2, l_sem.at[0, p]))
        l_loads.append(ctx_load(p, att_own, att_near, right2, l_sem.at[1, p]))
        l_loads.append(ctx_load(p, n1_own.at[p], n1_near, left1, l_sem.at[2, p]))

    def weights(j, slot):
        at = pl.multiple_of(start + j * chunk, chunk)
        return (
            pltpu.make_async_copy(wg_hbm.at[:, pl.ds(at, chunk)], wg_buf.at[slot], w_sem.at[slot, 0]),
            pltpu.make_async_copy(wu_hbm.at[:, pl.ds(at, chunk)], wu_buf.at[slot], w_sem.at[slot, 1]),
            pltpu.make_async_copy(wd_hbm.at[pl.ds(at, chunk)], wd_buf.at[slot], w_sem.at[slot, 2]),
        )

    for copies in l_loads[:]:
        go(copies)
    for copies in n_loads + g_loads[: ndp - 1]:
        go(copies)
    for copy in weights(0, 0):
        copy.start()

    far = Far(z, y, g_near, g_far, far_sem)
    mate = {"tensor": 1 - y}
    y_copies = [
        remote(front_hbm, front_got, y_sem.at[0, 0], y_sem.at[1, 0], mate),
        remote(out_hbm, out_got, y_sem.at[0, 1], y_sem.at[1, 1], mate),
    ]
    mine = pl.ds(pl.multiple_of(me * span, span), span)
    cross = pl.ds(pl.multiple_of((me ^ 2) * span, span), span)
    r_own = pltpu.make_async_copy(dqkv_hbm, right1.at[mine], r_sem.at[0, 3])
    r_x = remote(dqkv_hbm, right1.at[mine], r_sem.at[0, 0], r_sem.at[1, 0], {"ctx": me ^ 2})
    r_core = remote(dqkv_hbm, right1.at[mine], r_sem.at[0, 1], r_sem.at[1, 1], {"ctx": me ^ 1})
    r_onward = remote(
        right1.at[cross], right1.at[cross], r_sem.at[0, 2], r_sem.at[1, 2], {"ctx": me ^ 1}
    )
    enter(peers + mates(me, y))
    far.start()
    r_x.start()
    r_core.start()
    r_own.start()
    for copy in y_copies:
        copy.start()

    nq = right1.shape[1]

    def z_rows(k):
        return pl.ds(pl.multiple_of(k * part, part), part)

    def att_copies(w, cols):
        return [
            remote(
                prod.at[z_rows(lax.rem(z + s, ndp)), cols],
                att_z.at[z, :, cols],
                att_sem.at[0, w, s],
                att_sem.at[1, w, s],
                peers[s - 1],
            )
            for s in range(1, ndp)
        ]

    def att_own_copy(w, cols):
        return pltpu.make_async_copy(
            prod.at[z_rows(z), cols], att_z.at[z, :, cols], att_sem.at[0, w, 0]
        )

    out_cols = slice(nq, prod.shape[1])
    qkv_cols = slice(0, nq)
    for copies in l_loads:
        done(copies)
    prod[:, out_cols] = tn(left2[...], right2[...]).astype(BF)
    for copy in att_copies(1, out_cols):
        copy.start()
    att_own_copy(1, out_cols).start()

    count = units // chunk
    for copies in n_loads + g_loads[: ndp - 1]:
        done(copies)

    def activations(j, first, size):
        slot = j % 2
        for copy in weights(j, slot):
            copy.wait()

        @pl.when(j + 1 < count)
        def _():
            for copy in weights(j + 1, 1 - slot):
                copy.start()

        cols = pl.ds(pl.multiple_of(j * chunk, chunk), chunk)

        @pl.loop(0, size // rows)
        def _(i):
            some = pl.ds(pl.multiple_of(first + i * rows, rows), rows)
            gate = nn(n_all[some], wg_buf[slot])
            up = nn(n_all[some], wu_buf[slot])
            d_act = nt(g_all[some], wd_buf[slot])
            a, dg, du = gate_parts(gate, up, d_act)
            act[some, cols] = a
            d_gate[some, cols] = dg
            d_up[some, cols] = du

    @pl.loop(0, count)
    def _(j):
        activations(j, 0, tokens - span)

        @pl.when(j == count - 1)
        def _():
            far.onward()
            r_x.wait_recv()
            r_onward.start()
            for copy in weights(0, 0):
                copy.start()

    r_own.wait()
    r_core.wait_recv()
    r_onward.wait_recv()
    prod[:, qkv_cols] = tn(left1[...], right1[...]).astype(BF)
    for copy in att_copies(0, qkv_cols):
        copy.start()
    att_own_copy(0, qkv_cols).start()
    far.wait_recv()
    go(g_loads[ndp - 1])
    done(g_loads[ndp - 1])

    @pl.loop(0, count)
    def _(j):
        activations(j, tokens - span, span)

    terms = ((g_all, act), (n_all, d_gate), (n_all, d_up))
    nx = nctx // 2

    def product(w, x, c):
        left, right = terms[w]
        block = jnp.concatenate(
            [
                left[:, pl.ds(pl.multiple_of((k * nctx + x * 2 + c) * part, part), part)]
                for k in range(ndp)
            ],
            axis=1,
        )
        return tn(block, right[...])

    core_copies = [
        remote(give.at[w], take.at[w], core_sem.at[0, w], core_sem.at[1, w], {"ctx": me ^ 1})
        for w in range(3)
    ]
    x_copies = [
        remote(x_give.at[w], x_take.at[w], x_sem.at[0, w], x_sem.at[1, w], {"ctx": me ^ 2})
        for w in range(3)
    ]

    def hand(w):
        give[w, 0] = product(w, 1 - xpos, 1 - core).astype(BF)
        give[w, 1] = product(w, xpos, 1 - core).astype(BF)
        core_copies[w].start()

    def keep(w):
        there = product(w, 1 - xpos, core)
        core_copies[w].wait()
        x_give[w] = (there + take[w, 0].astype(F32)).astype(BF)
        x_copies[w].start()
        x_keep[w] = (product(w, xpos, core) + take[w, 1].astype(F32)).astype(BF)

    hand(0)
    keep(0)
    hand(1)
    keep(1)
    hand(2)
    keep(2)

    lands = (down_z, gate_z, up_z)

    def z_copies(w):
        return [
            remote(
                x_keep.at[w, z_rows(lax.rem(z + s, ndp))],
                lands[w].at[z],
                zz_sem.at[0, w, s],
                zz_sem.at[1, w, s],
                peers[s - 1],
            )
            for s in range(1, ndp)
        ]

    def z_own_copy(w):
        return pltpu.make_async_copy(x_keep.at[w, z_rows(z)], lands[w].at[z], z_own.at[w])

    for w in range(3):
        x_copies[w].wait()
        x_keep[w] = (x_keep[w].astype(F32) + x_take[w].astype(F32)).astype(BF)
        for copy in z_copies(w):
            copy.start()
        z_own_copy(w).start()
    for copy in y_copies:
        copy.wait()
    r_x.wait_send()
    r_core.wait_send()
    r_onward.wait_send()
    far.finish()
    for w, cols in ((1, out_cols), (0, qkv_cols)):
        for copy in att_copies(w, cols):
            copy.wait()
        att_own_copy(w, cols).wait()
    for w in range(3):
        for copy in z_copies(w):
            copy.wait()
        z_own_copy(w).wait()


def weight_grads(
    n2, n_all, n_far, og, og_all, wg, wu, wd,
    dqkv, n1p, n1_all, lowp, low_all, att, att_all, front_part, out_part,
    ndp, nctx, chunk=256, rows=256,
):
    span, width = n2.shape
    tokens = span * ndp
    length = span * nctx
    units = wg.shape[1] // ndp
    part = width // (ndp * nctx)
    mine = ndp * part
    qkvw, qw = dqkv.shape[1], att.shape[1]
    dma = pltpu.SemaphoreType.DMA
    side = jax.ShapeDtypeStruct((ndp, part, units), BF)
    row = jax.ShapeDtypeStruct((span, width), BF)
    return pl.pallas_call(
        functools.partial(grads_kernel, ndp, nctx, chunk, rows),
        in_specs=[HBM_SPEC] * 17,
        out_specs=[HBM_SPEC] * 7,
        out_shape=[
            side, side, side, jax.ShapeDtypeStruct((ndp, part, qkvw + qw), BF), row, row, row,
        ],
        scratch_shapes=[
            pltpu.VMEM((tokens, width), BF),
            pltpu.VMEM((tokens, width), BF),
            pltpu.VMEM((2, width, chunk), BF),
            pltpu.VMEM((2, width, chunk), BF),
            pltpu.VMEM((2, chunk, width), BF),
            pltpu.VMEM((tokens, units), BF),
            pltpu.VMEM((tokens, units), BF),
            pltpu.VMEM((tokens, units), BF),
            pltpu.VMEM((3, 2, mine, units), BF),
            pltpu.VMEM((3, 2, mine, units), BF),
            pltpu.VMEM((3, mine, units), BF),
            pltpu.VMEM((3, mine, units), BF),
            pltpu.VMEM((3, mine, units), BF),
            pltpu.VMEM((length, width // nctx), BF),
            pltpu.VMEM((length, width // nctx), BF),
            pltpu.VMEM((length, qkvw), BF),
            pltpu.VMEM((length, qw), BF),
            pltpu.VMEM((mine, qkvw + qw), BF),
            dma((2, ndp)),
            dma((3, nctx)),
            dma((2, 3)),
            dma((2, 4)),
            dma((2, 3)),
            dma((2, 3)),
            dma((2, 3, ndp)),
            dma((3,)),
            dma((2, 2, ndp)),
            dma((2, 2)),
            dma((2, 2)),
        ],
        compiler_params=pltpu.CompilerParams(
            vmem_limit_bytes=63 * 1024 * 1024, collective_id=3, has_side_effects=True
        ),
        cost_estimate=cost(12 * tokens * width * units, 4 * tokens * width),
        name="weight_grads",
    )(
        n2, n_all, n_far, og, og_all, wg, wu, wd,
        dqkv, n1p, n1_all, lowp, low_all, att, att_all, front_part, out_part,
    )


def dot_plain(left, right):
    return jnp.dot(left, right, preferred_element_type=F32)


def dot_right(left, right):
    return lax.dot_general(left, right, (((1,), (1,)), ((), ())), preferred_element_type=F32)


def dot_left(left, right):
    return lax.dot_general(left, right, (((0,), (0,)), ((), ())), preferred_element_type=F32)


def normed(v, gain):
    return v * lax.rsqrt(jnp.mean(v * v, axis=-1, keepdims=True) + EPS) * gain


def norm_back(v, gain, grad):
    factor = lax.rsqrt(jnp.mean(v * v, axis=-1, keepdims=True) + EPS)
    unit = v * factor
    d_unit = grad * gain
    d_gain = jnp.sum(grad * unit, axis=0)
    d_v = factor * (d_unit - unit * jnp.mean(d_unit * unit, axis=-1, keepdims=True))
    return (d_v, d_gain)


def rotate(t, cosine, sine):
    half = t.shape[-1] // 2
    first, second = (t[..., :half], t[..., half:])
    return jnp.concatenate(
        [first * cosine - second * sine, second * cosine + first * sine], axis=-1
    )


def rotate_back(t, cosine, sine):
    half = t.shape[-1] // 2
    first, second = (t[..., :half], t[..., half:])
    return jnp.concatenate(
        [first * cosine + second * sine, second * cosine - first * sine], axis=-1
    )


def score_block(query5, key_all, allowed):
    scores = jnp.einsum(
        "scngd,slnd->sngcl", query5, key_all, preferred_element_type=F32
    ) * HD ** (-0.5)
    return jnp.where(allowed[:, None, None], scores, NEG)


def build(ndp, nctx, nten):
    def pull(v, axis, n, s):
        return lax.ppermute(v, axis, [((i + s) % n, i) for i in range(n)])

    def flip(v, axis, n, bit):
        return lax.ppermute(v, axis, [(i, i ^ bit) for i in range(n)])

    def tensor_sum(v):
        low = v.astype(BF)
        if nten == 2:
            return low.astype(F32) + flip(low, "tensor", 2, 1).astype(F32)
        return lax.psum(low, "tensor").astype(F32)

    def gather_dp(v):
        rows = v.shape[0] // nten
        part = lax.dynamic_slice_in_dim(v, lax.axis_index("tensor") * rows, rows, 0)
        pieces = [v]
        for s in range(1, ndp):
            got = pull(part, "dp", ndp, s)
            pieces.append(got)
            for t in range(1, nten):
                pieces.append(pull(got, "tensor", nten, t))
        return jnp.concatenate(pieces, axis=0)

    def ctx_sum(full):
        r = full.shape[0] // (ndp * nctx)
        me = lax.axis_index("ctx")
        work = full.reshape(ndp, nctx, r, full.shape[1])
        bit = 1
        while bit < nctx:
            left = work.shape[1] // 2
            work = work.reshape(ndp, left, 2, r, full.shape[1])
            mine = (me // bit) % 2
            keep = lax.dynamic_index_in_dim(work, mine, 2, keepdims=False)
            give = lax.dynamic_index_in_dim(work, 1 - mine, 2, keepdims=False)
            got = flip(give, "ctx", nctx, bit)
            work = (keep.astype(F32) + got.astype(F32)).astype(BF)
            bit *= 2
        return work.reshape(ndp, r, full.shape[1])

    def finish_slices(full):
        got = lax.all_to_all(ctx_sum(full), "dp", 0, 0, tiled=True)
        return jnp.swapaxes(got, 0, 1).reshape(got.shape[1], -1).astype(F32)

    def finish_sum(full):
        got = lax.all_to_all(ctx_sum(full), "dp", 0, 0, tiled=True)
        return jnp.sum(got.astype(F32), axis=0)

    def local(
        layer_input,
        output_grad,
        prefix,
        attn_gain,
        w_query,
        w_key,
        w_value,
        w_out,
        mlp_gain,
        w_gate,
        w_up,
        w_down,
    ):
        seqs, span, width = layer_input.shape
        q_heads = w_query.shape[1] // HD
        kv_heads = w_key.shape[1] // HD
        group = q_heads // kv_heads
        zi = lax.axis_index("dp")
        rows = layer_input.astype(F32).reshape(seqs * span, width)
        grad_low = output_grad.reshape(seqs * span, width)
        grad_rows = grad_low.astype(F32)
        grad_all = gather_dp(grad_low)

        first = lax.axis_index("ctx") * span
        position = (first + jnp.arange(span)).astype(F32)
        frequency = ROPE_BASE ** (-jnp.arange(HD // 2).astype(F32) * 2.0 / HD)
        angle = position[:, None] * frequency[None, :]
        cosine = jnp.cos(angle)[None, :, None, :]
        sine = jnp.sin(angle)[None, :, None, :]
        normed1 = normed(rows, attn_gain).astype(BF)
        query = rotate(
            dot_plain(normed1, w_query).reshape(seqs, span, q_heads, HD), cosine, sine
        ).astype(BF)
        keyed = rotate(
            dot_plain(normed1, w_key).reshape(seqs, span, kv_heads, HD), cosine, sine
        ).astype(BF)
        valued = dot_plain(normed1, w_value).astype(BF).reshape(seqs, span, kv_heads * HD)
        key_all, value_all = (
            lax.all_gather(
                keyed.reshape(seqs, span, kv_heads * HD), "ctx", axis=1, tiled=True
            ),
            lax.all_gather(valued, "ctx", axis=1, tiled=True),
        )
        length = key_all.shape[1]
        key_all = key_all.reshape(seqs, length, kv_heads, HD)
        value_all = value_all.reshape(seqs, length, kv_heads, HD)
        query5 = query.reshape(seqs, span, kv_heads, group, HD)
        query_pos = first + jnp.arange(span)
        key_pos = jnp.arange(length)
        allowed = (key_pos[None, None, :] <= query_pos[None, :, None]) | (
            key_pos[None, None, :] < prefix[:, None, None]
        )
        scores = score_block(query5, key_all, allowed)
        top = jnp.max(scores, axis=-1, keepdims=True)
        exponent = jnp.exp(scores - top)
        total = jnp.sum(exponent, axis=-1, keepdims=True)
        log_total = top + jnp.log(total)
        probs_low = (exponent / total).astype(BF)
        attended = jnp.einsum(
            "sngcl,slnd->scngd", probs_low, value_all, preferred_element_type=F32
        )
        attended = attended.astype(BF).reshape(seqs * span, q_heads * HD)
        resid = rows + tensor_sum(dot_plain(attended, w_out))
        normed2 = normed(resid, mlp_gain).astype(BF)
        normed2_all = gather_dp(normed2)
        gate = dot_plain(normed2, w_gate)
        up = dot_plain(normed2, w_up)
        act = (jax.nn.silu(gate) * up).astype(BF)

        def mlp_back(gate, up, d_act):
            sigmoid_gate = jax.nn.sigmoid(gate)
            d_gate_pre = (
                d_act * up * sigmoid_gate * (1.0 + gate * (1.0 - sigmoid_gate))
            ).astype(BF)
            d_up_pre = (d_act * gate * sigmoid_gate).astype(BF)
            return d_gate_pre, d_up_pre

        d_act = dot_right(grad_low, w_down)
        d_gate_pre, d_up_pre = mlp_back(gate, up, d_act)
        back_terms = dot_right(d_gate_pre, w_gate) + dot_right(d_up_pre, w_up)
        d_normed2 = tensor_sum(back_terms)
        output = (resid + tensor_sum(dot_plain(act, w_down))).astype(BF)
        output = output.reshape(seqs, span, width)

        units = w_gate.shape[1] // ndp
        wg = lax.dynamic_slice_in_dim(w_gate, zi * units, units, 1)
        wu = lax.dynamic_slice_in_dim(w_up, zi * units, units, 1)
        wd = lax.dynamic_slice_in_dim(w_down, zi * units, units, 0)
        gate_s = dot_plain(normed2_all, wg)
        up_s = dot_plain(normed2_all, wu)
        d_act_s = dot_right(grad_all, wd)
        act_s = (jax.nn.silu(gate_s) * up_s).astype(BF)
        d_gate_s, d_up_s = mlp_back(gate_s, up_s, d_act_s)
        s_down = finish_slices(dot_left(grad_all, act_s).astype(BF)).T
        s_gate = finish_slices(dot_left(normed2_all, d_gate_s).astype(BF))
        s_up = finish_slices(dot_left(normed2_all, d_up_s).astype(BF))

        d_resid_norm, g_mlp_gain = norm_back(resid, mlp_gain, d_normed2)
        d_resid = grad_rows + d_resid_norm
        d_resid_low = d_resid.astype(BF)
        s_out = finish_sum(dot_left(d_resid_low, attended).astype(BF)).T
        d_attended = dot_right(d_resid_low, w_out).astype(BF).reshape(query5.shape)
        scores = score_block(query5, key_all, allowed)
        probs = jnp.exp(scores - log_total)
        probs_low = probs.astype(BF)
        d_probs = jnp.einsum(
            "scngd,slnd->sngcl", d_attended, value_all, preferred_element_type=F32
        )
        delta = jnp.sum(probs * d_probs, axis=-1, keepdims=True)
        d_scores = (probs * (d_probs - delta)).astype(BF)
        scale = HD ** (-0.5)
        d_query = (
            jnp.einsum("sngcl,slnd->scngd", d_scores, key_all, preferred_element_type=F32) * scale
        )
        d_key_all = (
            jnp.einsum("sngcl,scngd->slnd", d_scores, query5, preferred_element_type=F32) * scale
        )
        d_value_all = jnp.einsum(
            "sngcl,scngd->slnd", probs_low, d_attended, preferred_element_type=F32
        )
        d_kv = jnp.concatenate(
            [
                d_key_all.reshape(length, kv_heads * HD).astype(BF),
                d_value_all.reshape(length, kv_heads * HD).astype(BF),
            ],
            axis=1,
        )
        d_kv = lax.psum_scatter(d_kv, "ctx", scatter_dimension=0, tiled=True).astype(F32)
        d_key, d_val = d_kv[:, : kv_heads * HD], d_kv[:, kv_heads * HD :]
        d_qp = (
            rotate_back(d_query.reshape(seqs, span, q_heads, HD), cosine, sine)
            .astype(BF)
            .reshape(seqs * span, q_heads * HD)
        )
        d_kp = (
            rotate_back(d_key.reshape(seqs, span, kv_heads, HD), cosine, sine)
            .astype(BF)
            .reshape(seqs * span, kv_heads * HD)
        )
        d_vp = d_val.astype(BF).reshape(seqs * span, kv_heads * HD)
        front_terms = dot_right(d_qp, w_query) + dot_right(d_kp, w_key) + dot_right(d_vp, w_value)
        d_normed1 = tensor_sum(front_terms)
        d_rows_norm, g_attn_gain = norm_back(rows, attn_gain, d_normed1)
        d_input = d_resid + d_rows_norm
        d_input = d_input.reshape(seqs, span, width)
        s_qkv = finish_sum(
            dot_left(normed1, jnp.concatenate([d_qp, d_kp, d_vp], axis=1)).astype(BF)
        )
        nq, nk = q_heads * HD, kv_heads * HD
        s_query, s_key, s_value = s_qkv[:, :nq], s_qkv[:, nq : nq + nk], s_qkv[:, nq + nk :]
        gains = jnp.stack([g_attn_gain, g_mlp_gain])
        gains = lax.psum_scatter(gains, ("dp", "ctx"), scatter_dimension=1, tiled=True)
        return (
            output,
            d_input,
            gains[0],
            s_query,
            s_key,
            s_value,
            s_out,
            gains[1],
            s_gate,
            s_up,
            s_down,
        )

    return local


def suits(ndp, nctx, nten, layer_input, output_grad, prefix, attn_gain, w_query, w_key, w_value, w_out, mlp_gain, w_gate, w_up, w_down):
    seqs, span, width = layer_input.shape
    return (
        seqs == 1
        and (ndp, nctx, nten) == (4, 4, 2)
        and span == 256
        and width % (128 * ndp * nctx) == 0
        and w_key.shape[1] % 128 == 0
        and w_query.shape[1] % 256 == 0
        and w_gate.shape[1] % (512 * ndp) == 0
    )


def build_fast(ndp, nctx, nten):
    def local(
        layer_input,
        output_grad,
        prefix,
        attn_gain,
        w_query,
        w_key,
        w_value,
        w_out,
        mlp_gain,
        w_gate,
        w_up,
        w_down,
    ):
        seqs, span, width = layer_input.shape
        kvw, nq = w_key.shape[1], w_query.shape[1]
        low = layer_input.reshape(span, width)
        grad_low = output_grad.reshape(span, width)
        first = lax.axis_index("ctx") * span
        where = jnp.stack([first, prefix[0]]).astype(jnp.int32)
        cosine, sine = rope_tables(first, span)
        n1p, query, kv, attended, lse, resid, normed2, grad_all = front(
            where, low, attn_gain, w_query, w_key, w_value, w_out, cosine, sine, mlp_gain, grad_low, ndp, nctx
        )
        out_part, d_resid, low_d, low_dp, g_mlp_gain, n_all, n1_all, att_all = middle(
            normed2, grad_low, w_gate, w_up, w_down, resid, mlp_gain, n1p, attended, ndp, nctx
        )
        dqkv, front_part, low_all, n_far = back(
            where, query, kv, low_d, lse, cosine, sine, w_query, w_key, w_value, w_out, low_dp, n_all, ndp, nctx
        )
        down_z, gate_z, up_z, att_z, front_got, out_got, _ = weight_grads(
            normed2, n_all, n_far, grad_low, grad_all, w_gate, w_up, w_down,
            dqkv, n1p, n1_all, low_dp, low_all, attended, att_all, front_part, out_part, ndp, nctx,
        )
        output = resid + (out_part.astype(F32) + out_got.astype(F32))
        output = output.astype(BF).reshape(seqs, span, width)
        s_down = jnp.swapaxes(down_z, 1, 2).reshape(w_down.shape[0], -1).astype(F32)
        s_gate, s_up = (
            jnp.swapaxes(g, 0, 1).reshape(g.shape[1], -1).astype(F32) for g in (gate_z, up_z)
        )
        s_att = jnp.sum(att_z.astype(F32), axis=0)
        s_query, s_key = s_att[:, :nq], s_att[:, nq : nq + kvw]
        s_value, s_out = s_att[:, nq + kvw : nq + 2 * kvw], s_att[:, nq + 2 * kvw :].T
        d_normed1 = front_part.astype(F32) + front_got.astype(F32)
        d_rows_norm, g_attn_gain = norm_back(low.astype(F32), attn_gain, d_normed1)
        d_input = (d_resid + d_rows_norm).reshape(seqs, span, width)
        gains = jnp.stack([g_attn_gain, g_mlp_gain[0]])
        gains = jnp.swapaxes(gains.reshape(2, ndp * nctx, -1), 0, 1)
        gains = lax.all_to_all(gains, ("dp", "ctx"), 0, 0, tiled=True)
        gains = jnp.sum(gains, axis=0)
        return (
            output,
            d_input,
            gains[0],
            s_query,
            s_key,
            s_value,
            s_out,
            gains[1],
            s_gate,
            s_up,
            s_down,
        )

    return local


def solution(mesh):
    sizes = mesh.shape["dp"], mesh.shape["ctx"], mesh.shape["tensor"]
    plain, fast = build(*sizes), build_fast(*sizes)

    def local(*args):
        return (fast if suits(*sizes, *args) else plain)(*args)

    return jax.shard_map(
        local,
        mesh=mesh,
        in_specs=(
            P("dp", "ctx", None),
            P("dp", "ctx", None),
            P("dp"),
            P(),
            P(None, "tensor"),
            P(None, "tensor"),
            P(None, "tensor"),
            P("tensor", None),
            P(),
            P(None, "tensor"),
            P(None, "tensor"),
            P("tensor", None),
        ),
        out_specs=(
            P("dp", "ctx", None),
            P("dp", "ctx", None),
            P(("dp", "ctx")),
            P(("dp", "ctx"), "tensor"),
            P(("dp", "ctx"), "tensor"),
            P(("dp", "ctx"), "tensor"),
            P("tensor", ("dp", "ctx")),
            P(("dp", "ctx")),
            P(("dp", "ctx"), "tensor"),
            P(("dp", "ctx"), "tensor"),
            P("tensor", ("dp", "ctx")),
        ),
        check_vma=False,
    )
```

```python
import functools
import jax
import jax.numpy as jnp
from jax import lax
from jax.experimental import pallas as pl
from jax.experimental.pallas import tpu as pltpu
from jax.sharding import PartitionSpec as P

HD = 64
EPS = 1e-05
ROPE_BASE = 500000.0
NEG = -1e30
BF = jnp.bfloat16
F32 = jnp.float32
VMEM_MOST = 60 * 1024 * 1024


def cost(flops, nbytes, trans=0):
    return pl.CostEstimate(flops=int(flops), bytes_accessed=int(nbytes), transcendentals=int(trans))


def nt(a, b):
    return lax.dot_general(a, b, (((1,), (1,)), ((), ())), preferred_element_type=F32)


def tn(a, b):
    return lax.dot_general(a, b, (((0,), (0,)), ((), ())), preferred_element_type=F32)


def nn(a, b):
    return jnp.dot(a, b, preferred_element_type=F32)


def swap_halves(t):
    lane = lax.broadcasted_iota(jnp.int32, t.shape, 1) % HD
    n = t.shape[1]
    return jnp.where(
        lane < HD // 2, pltpu.roll(t, n - HD // 2, 1), pltpu.roll(t, HD // 2, 1)
    )


def rope_tables(first, span):
    position = (first + jnp.arange(span)).astype(F32)
    frequency = ROPE_BASE ** (-jnp.arange(HD // 2).astype(F32) * 2.0 / HD)
    angle = position[:, None] * frequency[None, :]
    cosine, sine = jnp.cos(angle), jnp.sin(angle)
    return (
        jnp.concatenate([cosine, cosine, cosine, cosine], axis=1),
        jnp.concatenate([-sine, sine, -sine, sine], axis=1),
    )


def mask_bias(first, prefix, length, span):
    key = lax.broadcasted_iota(jnp.int32, (length, span), 0)
    query = lax.broadcasted_iota(jnp.int32, (length, span), 1) + first
    return jnp.where((key <= query) | (key < prefix), 0.0, NEG).astype(F32)


def gate_parts(gate, up, d_act):
    sig = 1.0 / (1.0 + jnp.exp(-gate))
    silu = gate * sig
    return (
        (silu * up).astype(BF),
        (d_act * up * (sig + silu * (1.0 - sig))).astype(BF),
        (d_act * silu).astype(BF),
    )


MESH = pl.DeviceIdType.MESH


def remote(src, dst, send, recv, to):
    return pltpu.make_async_remote_copy(
        src_ref=src, dst_ref=dst, send_sem=send, recv_sem=recv, device_id=to, device_id_type=MESH
    )


def enter(devices):
    barrier = pltpu.get_barrier_semaphore()
    for to in devices:
        pl.semaphore_signal(barrier, inc=1, device_id=to, device_id_type=MESH)
    pl.semaphore_wait(barrier, len(devices))


def around(z, ndp):
    return [{"dp": lax.rem(z + 1, ndp)}, {"dp": lax.rem(z + ndp - 1, ndp)}]


def mates(me, y):
    return [{"ctx": me ^ 1}, {"ctx": me ^ 2}, {"ctx": me ^ 3}, {"tensor": 1 - y}]


class Relay:
    def __init__(self, z, ndp, hop, own, blocks, sems):
        self.z, self.ndp, self.hop = z, ndp, hop
        self.own, self.blocks, self.sems = own, blocks, sems

    def copy(self, way, block, to):
        src = self.own if self.hop == 1 else self.blocks.at[block]
        at = 0 if way > 0 else 1
        return remote(
            src, self.blocks.at[block], self.sems.at[0, at], self.sems.at[1, at], {"dp": to}
        )

    def each(self, act, incoming):
        z, hop = self.z, self.hop
        for way in (1, -1):
            if incoming:
                block = z - way * hop
                ok = block >= 0 if way > 0 else block < self.ndp
            else:
                block = z - way * (hop - 1)
                ok = (block >= 0) & (z < self.ndp - 1) if way > 0 else (block < self.ndp) & (z > 0)

            @pl.when(ok)
            def _(way=way, block=block):
                act(self.copy(way, block, z if incoming else z + way))

    def start(self):
        self.each(lambda c: c.start(), False)

    def wait_recv(self):
        self.each(lambda c: c.wait_recv(), True)

    def wait_send(self):
        self.each(lambda c: c.wait_send(), False)


def rope_parts(t, cosine, sine):
    pieces = []
    for i in range(t.shape[1] // 128):
        part = t[:, 128 * i : 128 * (i + 1)]
        pieces.append((part * cosine + swap_halves(part) * sine).astype(BF))
    return pieces


def front_kernel(
    ndp, nctx, group,
    where_ref, x_ref, gain1_ref, wq_hbm, wk_hbm, wv_hbm, wo_hbm, cos_ref, sin_ref, gain2_ref, og_hbm,
    n1_ref, q_ref, kv_out, att_ref, lse_ref, resid_ref, n2_ref, og_all,
    n1_buf, wq, wk, wv, wo, kv, bias_ref, part, part_got,
    w_sem, kv_sem, kv_out_sem, part_sem, z_sem,
):
    z, me, y = lax.axis_index("dp"), lax.axis_index("ctx"), lax.axis_index("tensor")
    span, width = x_ref.shape
    length = kv.shape[0]
    kvw = wk.shape[1]
    loads = [
        pltpu.make_async_copy(src, dst, w_sem.at[i])
        for i, (src, dst) in enumerate(((wk_hbm, wk), (wv_hbm, wv), (wq_hbm, wq), (wo_hbm, wo)))
    ]
    for copy in loads:
        copy.start()
    hop1 = Relay(z, ndp, 1, og_hbm, og_all, z_sem.at[0])
    hop2 = Relay(z, ndp, 2, og_hbm, og_all, z_sem.at[1])
    enter(around(z, ndp) + mates(me, y))
    hop1.start()
    v = x_ref[...].astype(F32)
    factor = lax.rsqrt(jnp.mean(v * v, axis=-1, keepdims=True) + EPS)
    n1_buf[...] = (v * factor * gain1_ref[...]).astype(BF)
    cosine, sine = cos_ref[...], sin_ref[...]
    mine = pl.ds(pl.multiple_of(me * span, span), span)
    loads[0].wait()
    for i, piece in enumerate(rope_parts(nn(n1_buf[...], wk[...]), cosine, sine)):
        kv[mine, 128 * i : 128 * (i + 1)] = piece
    loads[1].wait()
    kv[mine, kvw:] = nn(n1_buf[...], wv[...]).astype(BF)

    def kv_copy(which, block, mask):
        rows = pl.ds(pl.multiple_of(block * span, span), span)
        return remote(kv.at[rows], kv.at[rows], kv_sem.at[0, which], kv_sem.at[1, which], {"ctx": me ^ mask})

    to_x = kv_copy(0, me, 2)
    to_core = kv_copy(1, me, 1)
    onward = kv_copy(2, me ^ 2, 1)
    to_x.start()
    to_core.start()
    loads[2].wait()
    for i, piece in enumerate(rope_parts(nn(n1_buf[...], wq[...]), cosine, sine)):
        q_ref[:, 128 * i : 128 * (i + 1)] = piece
    part_width = width // (ndp * nctx)
    for p in range(nctx):
        for b in range(ndp):
            at = (b * nctx + p) * part_width
            n1_ref[p, :, b * part_width : (b + 1) * part_width] = n1_buf[:, at : at + part_width]
    bias_ref[...] = mask_bias(where_ref[0], where_ref[1], length, span)
    to_x.wait_recv()
    onward.start()
    to_core.wait_recv()
    onward.wait_recv()
    to_x.wait_send()
    to_core.wait_send()
    onward.wait_send()
    save_kv = pltpu.make_async_copy(kv, kv_out, kv_out_sem)
    save_kv.start()

    wide = 128 * group
    heads = wide // HD

    @pl.loop(0, kvw // 128)
    def _(j):
        lanes = pl.ds(pl.multiple_of(j * wide, 128), wide)
        queries = q_ref[:, lanes] * jnp.asarray(HD**-0.5, BF)
        keys = kv[:, pl.ds(pl.multiple_of(j * 128, 128), 128)]
        values = kv[:, pl.ds(pl.multiple_of(kvw + j * 128, 128), 128)]
        rows, outs = [], []
        for h in range(heads):
            at = slice(HD * (h // group), HD * (h // group + 1))
            scores = nt(keys[:, at], queries[:, HD * h : HD * (h + 1)]) + bias_ref[...]
            top = jnp.max(scores, axis=0, keepdims=True)
            exponent = jnp.exp(scores - top)
            total = jnp.sum(exponent, axis=0, keepdims=True)
            rows.append(top + jnp.log(total))
            outs.append(tn(values[:, at], exponent.astype(BF)) / total)
            if h % 2:
                both = jnp.concatenate(outs, axis=0).T.astype(BF)
                att_ref[:, pl.ds(pl.multiple_of(j * wide + HD * (h - 1), 128), 128)] = both
                outs = []
        lse_ref[pl.ds(pl.multiple_of(j * heads, heads), heads), :] = jnp.concatenate(rows, axis=0)

    hop1.wait_recv()
    hop2.start()
    save_kv.wait()
    loads[3].wait()
    count, _, cols = part.shape
    copies = [
        remote(part.at[c], part_got.at[c], part_sem.at[0, c], part_sem.at[1, c], {"tensor": 1 - y})
        for c in range(count)
    ]
    for c in range(count):
        part[c] = nn(att_ref[...], wo[:, c * cols : (c + 1) * cols]).astype(BF)
        copies[c].start()
    square = jnp.zeros((span, 1), F32)
    for c in range(count):
        at = slice(c * cols, (c + 1) * cols)
        copies[c].wait_recv()
        r = x_ref[:, at].astype(F32) + (part[c].astype(F32) + part_got[c].astype(F32))
        resid_ref[:, at] = r
        square += jnp.sum(r * r, axis=-1, keepdims=True)
    factor = lax.rsqrt(square / width + EPS)
    for c in range(count):
        at = slice(c * cols, (c + 1) * cols)
        n2_ref[:, at] = (resid_ref[:, at] * factor * gain2_ref[:, at]).astype(BF)
    for copy in copies:
        copy.wait_send()
    hop1.wait_send()
    hop2.wait_recv()
    hop2.wait_send()


HBM_SPEC = pl.BlockSpec(memory_space=pl.ANY)
VMEM_SPEC = pl.BlockSpec(memory_space=pltpu.VMEM)
SMEM_SPEC = pl.BlockSpec(memory_space=pltpu.SMEM)


def own(number):
    return pltpu.CompilerParams(
        vmem_limit_bytes=VMEM_MOST, collective_id=number, has_side_effects=True
    )


def front(where, x, gain1, wq, wk, wv, wo, cosine, sine, gain2, og, ndp, nctx):
    span, width = x.shape
    qw, kvw = wq.shape[1], wk.shape[1]
    group = qw // kvw
    length = span * nctx
    chunks = 4
    dma = pltpu.SemaphoreType.DMA
    return pl.pallas_call(
        functools.partial(front_kernel, ndp, nctx, group),
        in_specs=[SMEM_SPEC, VMEM_SPEC, VMEM_SPEC] + [HBM_SPEC] * 4 + [VMEM_SPEC] * 3 + [HBM_SPEC],
        out_specs=[VMEM_SPEC, VMEM_SPEC, HBM_SPEC] + [VMEM_SPEC] * 4 + [HBM_SPEC],
        out_shape=[
            jax.ShapeDtypeStruct((nctx, span, width // nctx), BF),
            jax.ShapeDtypeStruct((span, qw), BF),
            jax.ShapeDtypeStruct((length, 2 * kvw), BF),
            jax.ShapeDtypeStruct((span, qw), BF),
            jax.ShapeDtypeStruct((qw // HD, span), F32),
            jax.ShapeDtypeStruct((span, width), F32),
            jax.ShapeDtypeStruct((span, width), BF),
            jax.ShapeDtypeStruct((ndp, span, width), BF),
        ],
        scratch_shapes=[
            pltpu.VMEM((span, width), BF),
            pltpu.VMEM((width, qw), BF),
            pltpu.VMEM((width, kvw), BF),
            pltpu.VMEM((width, kvw), BF),
            pltpu.VMEM((qw, width), BF),
            pltpu.VMEM((length, 2 * kvw), BF),
            pltpu.VMEM((length, span), F32),
            pltpu.VMEM((chunks, span, width // chunks), BF),
            pltpu.VMEM((chunks, span, width // chunks), BF),
            dma((4,)),
            dma((2, 3)),
            dma,
            dma((2, chunks)),
            dma((2, 2, 2)),
        ],
        compiler_params=own(0),
        cost_estimate=cost(2 * span * width * (2 * qw + 2 * kvw), 4 * width * (qw + kvw)),
        name="front",
    )(where, x, gain1.reshape(1, width), wq, wk, wv, wo, cosine, sine, gain2.reshape(1, width), og)


def halves(y, span):
    return pl.ds(pl.multiple_of(y * (span // 2), span // 2), span // 2)


class Far:
    def __init__(self, z, y, blocks, far, sems):
        self.z, self.far = z, far
        rows = halves(y, far.shape[0])
        block = jnp.where(z == 1, 3, 0)
        to = jnp.where(z == 1, 0, 3)
        self.over = remote(
            blocks.at[block, rows], far.at[rows], sems.at[0, 0], sems.at[1, 0], {"dp": to}
        )
        self.swap = remote(
            far.at[rows], far.at[rows], sems.at[0, 1], sems.at[1, 1], {"tensor": 1 - y}
        )
        self.gives = (z == 1) | (z == 2)
        self.takes = (z == 0) | (z == 3)

    def start(self):
        pl.when(self.gives)(lambda: self.over.start())

    def onward(self):
        @pl.when(self.takes)
        def _():
            self.over.wait_recv()
            self.swap.start()

    def wait_recv(self):
        pl.when(self.takes)(lambda: self.swap.wait_recv())

    def finish(self):
        pl.when(self.takes)(lambda: self.swap.wait_send())
        pl.when(self.gives)(lambda: self.over.wait_send())


class Gather:
    def __init__(self, z, y, ndp, own, blocks, sems, swaps):
        self.z, self.y, self.ndp = z, y, ndp
        self.own, self.blocks, self.sems, self.swaps = own, blocks, sems, swaps
        self.rows = halves(y, own.shape[0])

    def over(self, way, hop, block, to):
        src = self.own.at[self.rows] if hop == 1 else self.blocks.at[block, self.rows]
        at = 0 if way > 0 else 1
        return remote(
            src, self.blocks.at[block, self.rows],
            self.sems.at[hop - 1, 0, at], self.sems.at[hop - 1, 1, at], {"dp": to},
        )

    def swap(self, way, hop, block):
        at = 0 if way > 0 else 1
        part = self.blocks.at[block, self.rows]
        return remote(
            part, part, self.swaps.at[hop - 1, 0, at], self.swaps.at[hop - 1, 1, at],
            {"tensor": 1 - self.y},
        )

    def comes(self, way, hop):
        block = self.z - way * hop
        return block, (block >= 0 if way > 0 else block < self.ndp)

    def leaves(self, way, hop):
        block = self.z - way * (hop - 1)
        if way > 0:
            return block, (block >= 0) & (self.z < self.ndp - 1)
        return block, (block < self.ndp) & (self.z > 0)

    def send(self, hop):
        for way in (1, -1):
            block, ok = self.leaves(way, hop)

            @pl.when(ok)
            def _(way=way, block=block):
                self.over(way, hop, block, self.z + way).start()

    def step(self, hop):
        for way in (1, -1):
            block, ok = self.comes(way, hop)

            @pl.when(ok)
            def _(way=way, block=block):
                self.over(way, hop, block, self.z).wait_recv()
                self.swap(way, hop, block).start()

        if hop < self.ndp - 1:
            self.send(hop + 1)

    def finish(self):
        for hop in range(1, self.ndp):
            for way in (1, -1):
                block, ok = self.comes(way, hop)

                @pl.when(ok)
                def _(way=way, block=block, hop=hop):
                    self.swap(way, hop, block).wait()

                block, ok = self.leaves(way, hop)

                @pl.when(ok)
                def _(way=way, block=block, hop=hop):
                    self.over(way, hop, block, self.z + way).wait_send()


def middle_kernel(
    ndp, nctx,
    n_ref, g_ref, wg_ref, wu_ref, wd_ref, n_hbm, n1_hbm, att_hbm, g_near,
    o_ref, dn_ref, n_all, n1_all, att_all, g_far,
    o_acc, dn_acc,
    z_sem, swap_sem, n1_sem, att_sem, far_sem,
):
    z, me, y = lax.axis_index("dp"), lax.axis_index("ctx"), lax.axis_index("tensor")
    j = pl.program_id(0)
    last = pl.num_programs(0) - 1
    gather = Gather(z, y, ndp, n_hbm, n_all, z_sem, swap_sem)
    far = Far(z, y, g_near, g_far, far_sem)
    spreads = []
    for m in range(1, nctx):
        spreads.append(
            remote(n1_hbm.at[me ^ m], n1_all.at[me], n1_sem.at[0, m], n1_sem.at[1, m], {"ctx": me ^ m})
        )
        spreads.append(
            remote(att_hbm, att_all.at[me], att_sem.at[0, m], att_sem.at[1, m], {"ctx": me ^ m})
        )

    @pl.when(j == 0)
    def _():
        enter(around(z, ndp) + mates(me, y))
        gather.send(1)
        far.start()
        for copy in spreads:
            copy.start()

    normed2, grad = n_ref[...], g_ref[...]
    gate = nn(normed2, wg_ref[...])
    up = nn(normed2, wu_ref[...])
    d_act = nt(grad, wd_ref[...])
    act, d_gate, d_up = gate_parts(gate, up, d_act)

    @pl.when(j == 0)
    def _():
        o_acc[...] = nn(act, wd_ref[...])
        dn_acc[...] = nt(d_gate, wg_ref[...]) + nt(d_up, wu_ref[...])

    @pl.when(j > 0)
    def _():
        o_acc[...] += nn(act, wd_ref[...])
        dn_acc[...] += nt(d_gate, wg_ref[...]) + nt(d_up, wu_ref[...])

    @pl.when(j == 3)
    def _():
        gather.step(1)

    @pl.when(j == 5)
    def _():
        gather.step(2)
        far.onward()

    @pl.when(j == last)
    def _():
        gather.step(3)
        o_ref[...] = o_acc[...].astype(BF)
        dn_ref[...] = dn_acc[...].astype(BF)
        for copy in spreads:
            copy.wait()
        far.wait_recv()
        far.finish()
        gather.finish()


def middle(n2, og, wg, wu, wd, n1p, att, og_all, ndp, nctx, step=512):
    span, width = n2.shape
    units = wg.shape[1]
    dma = pltpu.SemaphoreType.DMA
    whole = pl.BlockSpec((span, width), lambda j: (0, 0))
    cols = pl.BlockSpec((width, step), lambda j: (0, j))
    return pl.pallas_call(
        functools.partial(middle_kernel, ndp, nctx),
        grid=(units // step,),
        in_specs=[
            whole, whole, cols, cols, pl.BlockSpec((step, width), lambda j: (j, 0)),
            HBM_SPEC, HBM_SPEC, HBM_SPEC, HBM_SPEC,
        ],
        out_specs=[whole, whole, HBM_SPEC, HBM_SPEC, HBM_SPEC, HBM_SPEC],
        out_shape=[
            jax.ShapeDtypeStruct((span, width), BF),
            jax.ShapeDtypeStruct((span, width), BF),
            jax.ShapeDtypeStruct((ndp, span, width), BF),
            jax.ShapeDtypeStruct((nctx, span, width // nctx), BF),
            jax.ShapeDtypeStruct((nctx,) + att.shape, BF),
            jax.ShapeDtypeStruct((span, width), BF),
        ],
        scratch_shapes=[
            pltpu.VMEM((span, width), F32),
            pltpu.VMEM((span, width), F32),
            dma((ndp - 1, 2, 2)),
            dma((ndp - 1, 2, 2)),
            dma((2, nctx)),
            dma((2, nctx)),
            dma((2, 2)),
        ],
        compiler_params=own(1),
        cost_estimate=cost(12 * span * width * units, 6 * width * units),
        name="middle",
    )(n2, og, wg, wu, wd, n2, n1p, att, og_all)


def rear_kernel(
    ndp, nctx, group, chunk, rows,
    where_ref, q_ref, kv_ref, lse_ref, cos_ref, sin_ref, gain_ref, dn_ref,
    n_own, n_near, g_own, g_near, g_far, wg_hbm, wu_hbm, wd_hbm, wq_hbm, wk_hbm, wv_hbm, wo_hbm,
    resid_hbm, n1_own, n1_near, att_own, att_near, out_hbm,
    down_z, gate_z, up_z, att_z, front_out, front_got, out_got, dr_out, gain_grad_ref,
    n_all, g_all, acts, wg_buf, wu_buf, wd_buf, give, take, x_give, x_take, x_keep,
    left1, left2, right1, right2, prod, low, d_att, bias_ref, dkv, land, acc,
    in_sem, l_sem, w_sem, back_sem, dn_sem, low_sem, dkv_sem, r_sem, core_sem, x_sem, zz_sem, z_own,
    att_sem, y_sem, save_sem,
):
    z, me, y = lax.axis_index("dp"), lax.axis_index("ctx"), lax.axis_index("tensor")
    tokens, width = n_all.shape
    span, qw = q_ref.shape
    length = kv_ref.shape[0]
    kvw = kv_ref.shape[1] // 2
    units = acts.shape[1]
    core, xpos = me % 2, me // 2
    part = width // (ndp * nctx)
    start = z * units
    peers = [{"dp": lax.rem(z + s, ndp)} for s in range(1, ndp)]
    mate = {"tensor": 1 - y}
    mine = pl.ds(pl.multiple_of(me * span, span), span)
    cross = pl.ds(pl.multiple_of((me ^ 2) * span, span), span)

    def block_load(r, own_ref, near, far, dst, sem):
        block = lax.rem(jnp.where(z < ndp // 2, z + r, z + ndp - r), ndp)
        at = dst.at[pl.ds(r * span, span)]
        if r == 0:
            return [(None, pltpu.make_async_copy(own_ref, at, sem))]
        if r < ndp - 1 or far is None:
            return [(None, pltpu.make_async_copy(near.at[block], at, sem))]
        end = (z == 0) | (z == ndp - 1)
        return [
            (end, pltpu.make_async_copy(far, at, sem)),
            (jnp.logical_not(end), pltpu.make_async_copy(near.at[block], at, sem)),
        ]

    def go(copies):
        for ok, copy in copies:
            if ok is None:
                copy.start()
            else:
                pl.when(ok)(lambda copy=copy: copy.start())

    def done(copies):
        copies[0][1].wait()

    n_loads = [block_load(r, n_own, n_near, None, n_all, in_sem.at[0, r]) for r in range(ndp)]
    g_loads = [block_load(r, g_own, g_near, g_far, g_all, in_sem.at[1, r]) for r in range(ndp)]

    def ctx_load(p, own_ref, near, dst, sem):
        at = dst.at[pl.ds(p * span, span)]
        here = me == p
        return [
            (here, pltpu.make_async_copy(own_ref, at, sem)),
            (jnp.logical_not(here), pltpu.make_async_copy(near.at[p], at, sem)),
        ]

    l_loads = []
    for p in range(nctx):
        l_loads.append(ctx_load(p, att_own, att_near, right2, l_sem.at[0, p]))
        l_loads.append(ctx_load(p, n1_own.at[p], n1_near, left1, l_sem.at[1, p]))

    def weights(j, slot):
        at = pl.multiple_of(start + j * chunk, chunk)
        return (
            pltpu.make_async_copy(wg_hbm.at[:, pl.ds(at, chunk)], wg_buf.at[slot], w_sem.at[slot, 0]),
            pltpu.make_async_copy(wu_hbm.at[:, pl.ds(at, chunk)], wu_buf.at[slot], w_sem.at[slot, 1]),
            pltpu.make_async_copy(wd_hbm.at[pl.ds(at, chunk)], wd_buf.at[slot], w_sem.at[slot, 2]),
        )

    for copies in n_loads + g_loads:
        go(copies)
    for copy in weights(0, 0):
        copy.start()
    resid_load = pltpu.make_async_copy(resid_hbm, acc, save_sem.at[0])
    resid_load.start()
    for copies in l_loads:
        go(copies)
    dn_got = [x_take.at[2, pl.ds(h * span, span)] for h in range(2)]
    half = width // 2
    dn_copies = [
        remote(
            dn_ref.at[:, pl.ds(h * half, half)], dn_got[h], dn_sem.at[0, h], dn_sem.at[1, h], mate
        )
        for h in range(2)
    ]
    enter(peers + mates(me, y))
    for copy in dn_copies:
        copy.start()

    count = units // chunk
    for copies in n_loads + g_loads:
        done(copies)

    @pl.loop(0, count)
    def _(j):
        slot = j % 2
        for copy in weights(j, slot):
            copy.wait()

        @pl.when(j + 1 < count)
        def _():
            for copy in weights(j + 1, 1 - slot):
                copy.start()

        cols = pl.ds(pl.multiple_of(j * chunk, chunk), chunk)

        @pl.loop(0, tokens // rows)
        def _(i):
            some = pl.ds(pl.multiple_of(i * rows, rows), rows)
            gate = nn(n_all[some], wg_buf[slot])
            up = nn(n_all[some], wu_buf[slot])
            d_act = nt(g_all[some], wd_buf[slot])
            for w, value in enumerate(gate_parts(gate, up, d_act)):
                acts[pl.ds(pl.multiple_of(w * tokens + i * rows, rows), rows), cols] = value

    lefts = (g_all, n_all, n_all)

    def product(w, x, c):
        left = lefts[w]
        block = jnp.concatenate(
            [
                left[:, pl.ds(pl.multiple_of((k * nctx + x * 2 + c) * part, part), part)]
                for k in range(ndp)
            ],
            axis=1,
        )
        return tn(block, acts[w * tokens : (w + 1) * tokens])

    core_copies = [
        remote(give.at[w % 2], take.at[w % 2], core_sem.at[0, w], core_sem.at[1, w], {"ctx": me ^ 1})
        for w in range(3)
    ]
    x_copies = [
        remote(x_give.at[w], x_take.at[w], x_sem.at[0, w], x_sem.at[1, w], {"ctx": me ^ 2})
        for w in range(3)
    ]

    def hand(w):
        give[w % 2, 0] = product(w, 1 - xpos, 1 - core).astype(BF)
        give[w % 2, 1] = product(w, xpos, 1 - core).astype(BF)
        core_copies[w].start()

    def keep(w):
        there = product(w, 1 - xpos, core)
        core_copies[w].wait()
        x_give[w] = (there + take[w % 2, 0].astype(F32)).astype(BF)
        if w < 2:
            x_copies[w].start()
        x_keep[w] = (product(w, xpos, core) + take[w % 2, 1].astype(F32)).astype(BF)

    hand(0)
    keep(0)
    hand(1)
    keep(1)
    hand(2)
    keep(2)

    def z_rows(k):
        return pl.ds(pl.multiple_of(k * part, part), part)

    z_units = pl.ds(pl.multiple_of(start, units), units)

    def landing(w):
        return down_z.at[z] if w == 0 else (gate_z, up_z)[w - 1].at[:, z_units]

    def z_copies(w):
        return [
            remote(
                x_keep.at[w, z_rows(lax.rem(z + s, ndp))],
                landing(w),
                zz_sem.at[0, w, s],
                zz_sem.at[1, w, s],
                peers[s - 1],
            )
            for s in range(1, ndp)
        ]

    def z_own_copy(w):
        return pltpu.make_async_copy(x_keep.at[w, z_rows(z)], landing(w), z_own.at[w])

    def serve(w):
        x_copies[w].wait()
        x_keep[w] = (x_keep[w].astype(F32) + x_take[w].astype(F32)).astype(BF)
        for copy in z_copies(w):
            copy.start()
        z_own_copy(w).start()

    wo, wq = n_all, acts.at[pl.ds(0, width)]
    wk, wv = wg_buf.at[0], wu_buf.at[0]
    loads = [
        pltpu.make_async_copy(src, dst, back_sem.at[i])
        for i, (src, dst) in enumerate(((wo_hbm, wo), (wq_hbm, wq), (wk_hbm, wk), (wv_hbm, wv)))
    ]
    for copy in loads:
        copy.start()
    bias_ref[...] = mask_bias(where_ref[0], where_ref[1], length, span)
    resid_load.wait()
    v = acc[...]
    factor = lax.rsqrt(jnp.mean(v * v, axis=-1, keepdims=True) + EPS)
    for copy in dn_copies:
        copy.wait()
    y_out = remote(out_hbm, out_got, y_sem.at[0, 1], y_sem.at[1, 1], mate)
    y_out.start()
    cols = width // 4

    def dn_part(c):
        return dn_got[c // 2][:, (c % 2) * cols : (c % 2 + 1) * cols]

    dots = jnp.zeros((span, 1), F32)
    for c in range(4):
        at = slice(c * cols, (c + 1) * cols)
        unit = acc[:, at] * factor
        back = dn_ref[:, at].astype(F32) + dn_part(c).astype(F32)
        term = back * unit
        gain_grad_ref[:, at] = jnp.sum(term, axis=0, keepdims=True)
        dots += jnp.sum(term * gain_ref[:, at], axis=-1, keepdims=True)
    dots = dots / width
    for c in range(4):
        at = slice(c * cols, (c + 1) * cols)
        unit = acc[:, at] * factor
        back = dn_ref[:, at].astype(F32) + dn_part(c).astype(F32)
        total = g_all[:span, at].astype(F32) + factor * (back * gain_ref[:, at] - unit * dots)
        acc[:, at] = total
        low[:, at] = total.astype(BF)
    dr_save = pltpu.make_async_copy(acc, dr_out, save_sem.at[1])
    dr_save.start()

    spread = width // nctx

    def low_rows(p):
        return pl.ds(pl.multiple_of(p // 2 * span, span), span)

    def low_cols(p):
        return pl.ds(pl.multiple_of(p % 2 * spread, spread), spread)

    for p in range(nctx):
        for b in range(ndp):
            at = (b * nctx + p) * part
            to = p % 2 * spread + b * part
            give[0, 0, p // 2 * span : (p // 2 + 1) * span, to : to + part] = low[:, at : at + part]
    spreads = [
        remote(
            give.at[0, 0, low_rows(me ^ m), low_cols(me ^ m)],
            left2.at[mine],
            low_sem.at[0, m],
            low_sem.at[1, m],
            {"ctx": me ^ m},
        )
        for m in range(1, nctx)
    ]
    for copy in spreads:
        copy.start()
    left2[mine, :] = give[0, 0, low_rows(me), low_cols(me)]
    loads[0].wait()
    d_att[...] = nt(low[...], wo[...]).astype(BF)
    wide = 128 * group
    heads = wide // HD
    blocks = kvw // 128
    scale = jnp.asarray(HD**-0.5, BF)

    def share(j, m):
        some = pl.ds(pl.multiple_of((me ^ m) * span, span), span)
        return remote(
            dkv.at[j, some], land.at[j, m], dkv_sem.at[0, j, m], dkv_sem.at[1, j, m], {"ctx": me ^ m}
        )

    @pl.loop(0, blocks)
    def _(j):
        lanes = pl.ds(pl.multiple_of(j * wide, 128), wide)
        queries = q_ref[:, lanes] * scale
        grads = d_att[:, lanes]
        keys = kv_ref[:, pl.ds(pl.multiple_of(j * 128, 128), 128)]
        values = kv_ref[:, pl.ds(pl.multiple_of(kvw + j * 128, 128), 128)]
        lse = lse_ref[pl.ds(pl.multiple_of(j * heads, heads), heads), :]
        pair = []
        for h in range(heads):
            at = slice(HD * (h // group), HD * (h // group + 1))
            key, value = keys[:, at], values[:, at]
            query = queries[:, HD * h : HD * (h + 1)]
            grad = grads[:, HD * h : HD * (h + 1)]
            probs = jnp.exp(nt(key, query) + (bias_ref[...] - lse[h : h + 1, :]))
            d_probs = nt(value, grad)
            delta = jnp.sum(probs * d_probs, axis=0, keepdims=True)
            d_scores = (probs * (d_probs - delta)).astype(BF)
            d_value = nn(probs.astype(BF), grad)
            d_key = nn(d_scores, query)
            if h % group == 0:
                sum_key, sum_value = d_key, d_value
            else:
                sum_key, sum_value = sum_key + d_key, sum_value + d_value
            if h % group == group - 1:
                dkv[j, :, at] = sum_key.astype(BF)
                dkv[j, :, slice(128 + at.start, 128 + at.stop)] = sum_value.astype(BF)
            pair.append(tn(key * scale, d_scores))
            if h % 2:
                both = jnp.concatenate(pair, axis=0).T
                turned = both * cos_ref[...] - swap_halves(both) * sin_ref[...]
                right1[mine, pl.ds(pl.multiple_of(j * wide + HD * (h - 1), 128), 128)] = turned.astype(BF)
                pair = []
        for m in range(1, nctx):
            share(j, m).start()

        @pl.when(j == 0)
        def _():
            serve(0)

    loads[1].wait()
    dr_save.wait()
    acc[...] = nt(right1[mine, :qw], wq[...])
    serve(1)
    for j in range(blocks):
        total = dkv[j, mine].astype(F32)
        for m in range(1, nctx):
            share(j, m).wait_recv()
            total += land[j, m].astype(F32)
        d_key = total[:, :128]
        d_key = d_key * cos_ref[...] - swap_halves(d_key) * sin_ref[...]
        right1[mine, qw + 128 * j : qw + 128 * (j + 1)] = d_key.astype(BF)
        right1[mine, qw + kvw + 128 * j : qw + kvw + 128 * (j + 1)] = total[:, 128:].astype(BF)
    own_rows = right1.at[mine]
    r_x = remote(own_rows, own_rows, r_sem.at[0, 0], r_sem.at[1, 0], {"ctx": me ^ 2})
    r_core = remote(own_rows, own_rows, r_sem.at[0, 1], r_sem.at[1, 1], {"ctx": me ^ 1})
    r_onward = remote(
        right1.at[cross], right1.at[cross], r_sem.at[0, 2], r_sem.at[1, 2], {"ctx": me ^ 1}
    )
    r_x.start()
    r_core.start()
    x_copies[2].start()
    loads[2].wait()
    loads[3].wait()
    low[...] = (
        acc[...]
        + nt(right1[mine, qw : qw + kvw], wk[...])
        + nt(right1[mine, qw + kvw :], wv[...])
    ).astype(BF)
    front_save = pltpu.make_async_copy(low, front_out, save_sem.at[2])
    y_front = remote(low, front_got, y_sem.at[0, 0], y_sem.at[1, 0], mate)
    front_save.start()
    y_front.start()

    nq = right1.shape[1]

    def att_copies(w, at):
        return [
            remote(
                prod.at[z_rows(lax.rem(z + s, ndp)), at],
                att_z.at[z, :, at],
                att_sem.at[0, w, s],
                att_sem.at[1, w, s],
                peers[s - 1],
            )
            for s in range(1, ndp)
        ]

    def att_own_copy(w, at):
        return pltpu.make_async_copy(
            prod.at[z_rows(z), at], att_z.at[z, :, at], att_sem.at[0, w, 0]
        )

    out_cols = slice(nq, prod.shape[1])
    qkv_cols = slice(0, nq)
    for copies in l_loads:
        done(copies)
    for copy in spreads:
        copy.wait()
    prod[:, out_cols] = tn(left2[...], right2[...]).astype(BF)
    for copy in att_copies(1, out_cols):
        copy.start()
    att_own_copy(1, out_cols).start()
    r_x.wait_recv()
    r_onward.start()
    r_core.wait_recv()
    r_onward.wait_recv()
    prod[:, qkv_cols] = tn(left1[...], right1[...]).astype(BF)
    for copy in att_copies(0, qkv_cols):
        copy.start()
    att_own_copy(0, qkv_cols).start()
    serve(2)
    for j in range(blocks):
        for m in range(1, nctx):
            share(j, m).wait_send()
    y_out.wait()
    y_front.wait()
    front_save.wait()
    r_x.wait_send()
    r_core.wait_send()
    r_onward.wait_send()
    for w, at in ((1, out_cols), (0, qkv_cols)):
        for copy in att_copies(w, at):
            copy.wait()
        att_own_copy(w, at).wait()
    for w in range(3):
        for copy in z_copies(w):
            copy.wait()
        z_own_copy(w).wait()


def rear(
    where, q, kv, lse, cosine, sine, gain, dn, n2, n_all, og, og_all, og_far, wg, wu, wd,
    wq, wk, wv, wo, resid, n1p, n1_all, att, att_all, out_part, ndp, nctx, chunk=256, rows=256,
):
    span, width = n2.shape
    tokens, length = span * ndp, span * nctx
    units = wg.shape[1] // ndp
    part = width // (ndp * nctx)
    mine = ndp * part
    qw, kvw = wq.shape[1], wk.shape[1]
    qkvw = qw + 2 * kvw
    dma = pltpu.SemaphoreType.DMA
    flat = jax.ShapeDtypeStruct((part, ndp * units), BF)
    row = jax.ShapeDtypeStruct((span, width), BF)
    return pl.pallas_call(
        functools.partial(rear_kernel, ndp, nctx, qw // kvw, chunk, rows),
        in_specs=[SMEM_SPEC] + [VMEM_SPEC] * 7 + [HBM_SPEC] * 18,
        out_specs=[HBM_SPEC] * 8 + [VMEM_SPEC],
        out_shape=[
            jax.ShapeDtypeStruct((ndp, part, units), BF),
            flat,
            flat,
            jax.ShapeDtypeStruct((ndp, part, qkvw + qw), BF),
            row,
            row,
            row,
            jax.ShapeDtypeStruct((span, width), F32),
            jax.ShapeDtypeStruct((1, width), F32),
        ],
        scratch_shapes=[
            pltpu.VMEM((tokens, width), BF),
            pltpu.VMEM((tokens, width), BF),
            pltpu.VMEM((3 * tokens, units), BF),
            pltpu.VMEM((2, width, chunk), BF),
            pltpu.VMEM((2, width, chunk), BF),
            pltpu.VMEM((2, chunk, width), BF),
            pltpu.VMEM((2, 2, mine, units), BF),
            pltpu.VMEM((2, 2, mine, units), BF),
            pltpu.VMEM((3, mine, units), BF),
            pltpu.VMEM((3, mine, units), BF),
            pltpu.VMEM((3, mine, units), BF),
            pltpu.VMEM((length, width // nctx), BF),
            pltpu.VMEM((length, width // nctx), BF),
            pltpu.VMEM((length, qkvw), BF),
            pltpu.VMEM((length, qw), BF),
            pltpu.VMEM((mine, qkvw + qw), BF),
            pltpu.VMEM((span, width), BF),
            pltpu.VMEM((span, qw), BF),
            pltpu.VMEM((length, span), F32),
            pltpu.VMEM((kvw // 128, length, 256), BF),
            pltpu.VMEM((kvw // 128, nctx, span, 256), BF),
            pltpu.VMEM((span, width), F32),
            dma((2, ndp)),
            dma((2, nctx)),
            dma((2, 3)),
            dma((4,)),
            dma((2, 2)),
            dma((2, nctx)),
            dma((2, kvw // 128, nctx)),
            dma((2, 3)),
            dma((2, 3)),
            dma((2, 3)),
            dma((2, 3, ndp)),
            dma((3,)),
            dma((2, 2, ndp)),
            dma((2, 2)),
            dma((3,)),
        ],
        compiler_params=pltpu.CompilerParams(
            vmem_limit_bytes=63 * 1024 * 1024, collective_id=2, has_side_effects=True
        ),
        cost_estimate=cost(12 * tokens * width * units, 4 * tokens * width),
        name="rear",
    )(
        where, q, kv, lse, cosine, sine, gain.reshape(1, width), dn,
        n2, n_all, og, og_all, og_far, wg, wu, wd, wq, wk, wv, wo,
        resid, n1p, n1_all, att, att_all, out_part,
    )


def dot_plain(left, right):
    return jnp.dot(left, right, preferred_element_type=F32)


def dot_right(left, right):
    return lax.dot_general(left, right, (((1,), (1,)), ((), ())), preferred_element_type=F32)


def dot_left(left, right):
    return lax.dot_general(left, right, (((0,), (0,)), ((), ())), preferred_element_type=F32)


def normed(v, gain):
    return v * lax.rsqrt(jnp.mean(v * v, axis=-1, keepdims=True) + EPS) * gain


def norm_back(v, gain, grad):
    factor = lax.rsqrt(jnp.mean(v * v, axis=-1, keepdims=True) + EPS)
    unit = v * factor
    d_unit = grad * gain
    d_gain = jnp.sum(grad * unit, axis=0)
    d_v = factor * (d_unit - unit * jnp.mean(d_unit * unit, axis=-1, keepdims=True))
    return (d_v, d_gain)


def rotate(t, cosine, sine):
    half = t.shape[-1] // 2
    first, second = (t[..., :half], t[..., half:])
    return jnp.concatenate(
        [first * cosine - second * sine, second * cosine + first * sine], axis=-1
    )


def rotate_back(t, cosine, sine):
    half = t.shape[-1] // 2
    first, second = (t[..., :half], t[..., half:])
    return jnp.concatenate(
        [first * cosine + second * sine, second * cosine - first * sine], axis=-1
    )


def score_block(query5, key_all, allowed):
    scores = jnp.einsum(
        "scngd,slnd->sngcl", query5, key_all, preferred_element_type=F32
    ) * HD ** (-0.5)
    return jnp.where(allowed[:, None, None], scores, NEG)


def build(ndp, nctx, nten):
    def pull(v, axis, n, s):
        return lax.ppermute(v, axis, [((i + s) % n, i) for i in range(n)])

    def flip(v, axis, n, bit):
        return lax.ppermute(v, axis, [(i, i ^ bit) for i in range(n)])

    def tensor_sum(v):
        low = v.astype(BF)
        if nten == 2:
            return low.astype(F32) + flip(low, "tensor", 2, 1).astype(F32)
        return lax.psum(low, "tensor").astype(F32)

    def gather_dp(v):
        rows = v.shape[0] // nten
        part = lax.dynamic_slice_in_dim(v, lax.axis_index("tensor") * rows, rows, 0)
        pieces = [v]
        for s in range(1, ndp):
            got = pull(part, "dp", ndp, s)
            pieces.append(got)
            for t in range(1, nten):
                pieces.append(pull(got, "tensor", nten, t))
        return jnp.concatenate(pieces, axis=0)

    def ctx_sum(full):
        r = full.shape[0] // (ndp * nctx)
        me = lax.axis_index("ctx")
        work = full.reshape(ndp, nctx, r, full.shape[1])
        bit = 1
        while bit < nctx:
            left = work.shape[1] // 2
            work = work.reshape(ndp, left, 2, r, full.shape[1])
            mine = (me // bit) % 2
            keep = lax.dynamic_index_in_dim(work, mine, 2, keepdims=False)
            give = lax.dynamic_index_in_dim(work, 1 - mine, 2, keepdims=False)
            got = flip(give, "ctx", nctx, bit)
            work = (keep.astype(F32) + got.astype(F32)).astype(BF)
            bit *= 2
        return work.reshape(ndp, r, full.shape[1])

    def finish_slices(full):
        got = lax.all_to_all(ctx_sum(full), "dp", 0, 0, tiled=True)
        return jnp.swapaxes(got, 0, 1).reshape(got.shape[1], -1).astype(F32)

    def finish_sum(full):
        got = lax.all_to_all(ctx_sum(full), "dp", 0, 0, tiled=True)
        return jnp.sum(got.astype(F32), axis=0)

    def local(
        layer_input,
        output_grad,
        prefix,
        attn_gain,
        w_query,
        w_key,
        w_value,
        w_out,
        mlp_gain,
        w_gate,
        w_up,
        w_down,
    ):
        seqs, span, width = layer_input.shape
        q_heads = w_query.shape[1] // HD
        kv_heads = w_key.shape[1] // HD
        group = q_heads // kv_heads
        zi = lax.axis_index("dp")
        rows = layer_input.astype(F32).reshape(seqs * span, width)
        grad_low = output_grad.reshape(seqs * span, width)
        grad_rows = grad_low.astype(F32)
        grad_all = gather_dp(grad_low)

        first = lax.axis_index("ctx") * span
        position = (first + jnp.arange(span)).astype(F32)
        frequency = ROPE_BASE ** (-jnp.arange(HD // 2).astype(F32) * 2.0 / HD)
        angle = position[:, None] * frequency[None, :]
        cosine = jnp.cos(angle)[None, :, None, :]
        sine = jnp.sin(angle)[None, :, None, :]
        normed1 = normed(rows, attn_gain).astype(BF)
        query = rotate(
            dot_plain(normed1, w_query).reshape(seqs, span, q_heads, HD), cosine, sine
        ).astype(BF)
        keyed = rotate(
            dot_plain(normed1, w_key).reshape(seqs, span, kv_heads, HD), cosine, sine
        ).astype(BF)
        valued = dot_plain(normed1, w_value).astype(BF).reshape(seqs, span, kv_heads * HD)
        key_all, value_all = (
            lax.all_gather(
                keyed.reshape(seqs, span, kv_heads * HD), "ctx", axis=1, tiled=True
            ),
            lax.all_gather(valued, "ctx", axis=1, tiled=True),
        )
        length = key_all.shape[1]
        key_all = key_all.reshape(seqs, length, kv_heads, HD)
        value_all = value_all.reshape(seqs, length, kv_heads, HD)
        query5 = query.reshape(seqs, span, kv_heads, group, HD)
        query_pos = first + jnp.arange(span)
        key_pos = jnp.arange(length)
        allowed = (key_pos[None, None, :] <= query_pos[None, :, None]) | (
            key_pos[None, None, :] < prefix[:, None, None]
        )
        scores = score_block(query5, key_all, allowed)
        top = jnp.max(scores, axis=-1, keepdims=True)
        exponent = jnp.exp(scores - top)
        total = jnp.sum(exponent, axis=-1, keepdims=True)
        log_total = top + jnp.log(total)
        probs_low = (exponent / total).astype(BF)
        attended = jnp.einsum(
            "sngcl,slnd->scngd", probs_low, value_all, preferred_element_type=F32
        )
        attended = attended.astype(BF).reshape(seqs * span, q_heads * HD)
        resid = rows + tensor_sum(dot_plain(attended, w_out))
        normed2 = normed(resid, mlp_gain).astype(BF)
        normed2_all = gather_dp(normed2)
        gate = dot_plain(normed2, w_gate)
        up = dot_plain(normed2, w_up)
        act = (jax.nn.silu(gate) * up).astype(BF)

        def mlp_back(gate, up, d_act):
            sigmoid_gate = jax.nn.sigmoid(gate)
            d_gate_pre = (
                d_act * up * sigmoid_gate * (1.0 + gate * (1.0 - sigmoid_gate))
            ).astype(BF)
            d_up_pre = (d_act * gate * sigmoid_gate).astype(BF)
            return d_gate_pre, d_up_pre

        d_act = dot_right(grad_low, w_down)
        d_gate_pre, d_up_pre = mlp_back(gate, up, d_act)
        back_terms = dot_right(d_gate_pre, w_gate) + dot_right(d_up_pre, w_up)
        d_normed2 = tensor_sum(back_terms)
        output = (resid + tensor_sum(dot_plain(act, w_down))).astype(BF)
        output = output.reshape(seqs, span, width)

        units = w_gate.shape[1] // ndp
        wg = lax.dynamic_slice_in_dim(w_gate, zi * units, units, 1)
        wu = lax.dynamic_slice_in_dim(w_up, zi * units, units, 1)
        wd = lax.dynamic_slice_in_dim(w_down, zi * units, units, 0)
        gate_s = dot_plain(normed2_all, wg)
        up_s = dot_plain(normed2_all, wu)
        d_act_s = dot_right(grad_all, wd)
        act_s = (jax.nn.silu(gate_s) * up_s).astype(BF)
        d_gate_s, d_up_s = mlp_back(gate_s, up_s, d_act_s)
        s_down = finish_slices(dot_left(grad_all, act_s).astype(BF)).T
        s_gate = finish_slices(dot_left(normed2_all, d_gate_s).astype(BF))
        s_up = finish_slices(dot_left(normed2_all, d_up_s).astype(BF))

        d_resid_norm, g_mlp_gain = norm_back(resid, mlp_gain, d_normed2)
        d_resid = grad_rows + d_resid_norm
        d_resid_low = d_resid.astype(BF)
        s_out = finish_sum(dot_left(d_resid_low, attended).astype(BF)).T
        d_attended = dot_right(d_resid_low, w_out).astype(BF).reshape(query5.shape)
        scores = score_block(query5, key_all, allowed)
        probs = jnp.exp(scores - log_total)
        probs_low = probs.astype(BF)
        d_probs = jnp.einsum(
            "scngd,slnd->sngcl", d_attended, value_all, preferred_element_type=F32
        )
        delta = jnp.sum(probs * d_probs, axis=-1, keepdims=True)
        d_scores = (probs * (d_probs - delta)).astype(BF)
        scale = HD ** (-0.5)
        d_query = (
            jnp.einsum("sngcl,slnd->scngd", d_scores, key_all, preferred_element_type=F32) * scale
        )
        d_key_all = (
            jnp.einsum("sngcl,scngd->slnd", d_scores, query5, preferred_element_type=F32) * scale
        )
        d_value_all = jnp.einsum(
            "sngcl,scngd->slnd", probs_low, d_attended, preferred_element_type=F32
        )
        d_kv = jnp.concatenate(
            [
                d_key_all.reshape(length, kv_heads * HD).astype(BF),
                d_value_all.reshape(length, kv_heads * HD).astype(BF),
            ],
            axis=1,
        )
        d_kv = lax.psum_scatter(d_kv, "ctx", scatter_dimension=0, tiled=True).astype(F32)
        d_key, d_val = d_kv[:, : kv_heads * HD], d_kv[:, kv_heads * HD :]
        d_qp = (
            rotate_back(d_query.reshape(seqs, span, q_heads, HD), cosine, sine)
            .astype(BF)
            .reshape(seqs * span, q_heads * HD)
        )
        d_kp = (
            rotate_back(d_key.reshape(seqs, span, kv_heads, HD), cosine, sine)
            .astype(BF)
            .reshape(seqs * span, kv_heads * HD)
        )
        d_vp = d_val.astype(BF).reshape(seqs * span, kv_heads * HD)
        front_terms = dot_right(d_qp, w_query) + dot_right(d_kp, w_key) + dot_right(d_vp, w_value)
        d_normed1 = tensor_sum(front_terms)
        d_rows_norm, g_attn_gain = norm_back(rows, attn_gain, d_normed1)
        d_input = d_resid + d_rows_norm
        d_input = d_input.reshape(seqs, span, width)
        s_qkv = finish_sum(
            dot_left(normed1, jnp.concatenate([d_qp, d_kp, d_vp], axis=1)).astype(BF)
        )
        nq, nk = q_heads * HD, kv_heads * HD
        s_query, s_key, s_value = s_qkv[:, :nq], s_qkv[:, nq : nq + nk], s_qkv[:, nq + nk :]
        gains = jnp.stack([g_attn_gain, g_mlp_gain])
        gains = lax.psum_scatter(gains, ("dp", "ctx"), scatter_dimension=1, tiled=True)
        return (
            output,
            d_input,
            gains[0],
            s_query,
            s_key,
            s_value,
            s_out,
            gains[1],
            s_gate,
            s_up,
            s_down,
        )

    return local


def suits(ndp, nctx, nten, layer_input, output_grad, prefix, attn_gain, w_query, w_key, w_value, w_out, mlp_gain, w_gate, w_up, w_down):
    seqs, span, width = layer_input.shape
    return (
        seqs == 1
        and (ndp, nctx, nten) == (4, 4, 2)
        and (span, width) == (256, 2048)
        and (w_query.shape[1], w_key.shape[1], w_gate.shape[1]) == (1024, 256, 4096)
    )


def build_fast(ndp, nctx, nten):
    def local(
        layer_input,
        output_grad,
        prefix,
        attn_gain,
        w_query,
        w_key,
        w_value,
        w_out,
        mlp_gain,
        w_gate,
        w_up,
        w_down,
    ):
        seqs, span, width = layer_input.shape
        kvw, nq = w_key.shape[1], w_query.shape[1]
        low = layer_input.reshape(span, width)
        grad_low = output_grad.reshape(span, width)
        first = lax.axis_index("ctx") * span
        where = jnp.stack([first, prefix[0]]).astype(jnp.int32)
        cosine, sine = rope_tables(first, span)
        n1p, query, kv, attended, lse, resid, normed2, grad_all = front(
            where, low, attn_gain, w_query, w_key, w_value, w_out, cosine, sine, mlp_gain, grad_low, ndp, nctx
        )
        out_part, dn, n_all, n1_all, att_all, grad_far = middle(
            normed2, grad_low, w_gate, w_up, w_down, n1p, attended, grad_all, ndp, nctx
        )
        down_z, gate_z, up_z, att_z, front_part, front_got, out_got, d_resid, g_mlp_gain = rear(
            where, query, kv, lse, cosine, sine, mlp_gain, dn, normed2, n_all, grad_low, grad_all, grad_far,
            w_gate, w_up, w_down, w_query, w_key, w_value, w_out, resid, n1p, n1_all, attended, att_all,
            out_part, ndp, nctx,
        )
        output = resid + (out_part.astype(F32) + out_got.astype(F32))
        output = output.astype(BF).reshape(seqs, span, width)
        s_down = jnp.swapaxes(down_z, 1, 2).reshape(w_down.shape[0], -1).astype(F32)
        s_gate, s_up = gate_z.astype(F32), up_z.astype(F32)
        s_att = jnp.sum(att_z.astype(F32), axis=0)
        s_query, s_key = s_att[:, :nq], s_att[:, nq : nq + kvw]
        s_value, s_out = s_att[:, nq + kvw : nq + 2 * kvw], s_att[:, nq + 2 * kvw :].T
        d_normed1 = front_part.astype(F32) + front_got.astype(F32)
        d_rows_norm, g_attn_gain = norm_back(low.astype(F32), attn_gain, d_normed1)
        d_input = (d_resid + d_rows_norm).reshape(seqs, span, width)
        gains = jnp.stack([g_attn_gain, g_mlp_gain[0]])
        gains = jnp.swapaxes(gains.reshape(2, ndp * nctx, -1), 0, 1)
        gains = lax.all_to_all(gains, ("dp", "ctx"), 0, 0, tiled=True)
        gains = jnp.sum(gains, axis=0)
        return (
            output,
            d_input,
            gains[0],
            s_query,
            s_key,
            s_value,
            s_out,
            gains[1],
            s_gate,
            s_up,
            s_down,
        )

    return local


def solution(mesh):
    sizes = mesh.shape["dp"], mesh.shape["ctx"], mesh.shape["tensor"]
    plain, fast = build(*sizes), build_fast(*sizes)

    def local(*args):
        return (fast if suits(*sizes, *args) else plain)(*args)

    return jax.shard_map(
        local,
        mesh=mesh,
        in_specs=(
            P("dp", "ctx", None),
            P("dp", "ctx", None),
            P("dp"),
            P(),
            P(None, "tensor"),
            P(None, "tensor"),
            P(None, "tensor"),
            P("tensor", None),
            P(),
            P(None, "tensor"),
            P(None, "tensor"),
            P("tensor", None),
        ),
        out_specs=(
            P("dp", "ctx", None),
            P("dp", "ctx", None),
            P(("dp", "ctx")),
            P(("dp", "ctx"), "tensor"),
            P(("dp", "ctx"), "tensor"),
            P(("dp", "ctx"), "tensor"),
            P("tensor", ("dp", "ctx")),
            P(("dp", "ctx")),
            P(("dp", "ctx"), "tensor"),
            P(("dp", "ctx"), "tensor"),
            P("tensor", ("dp", "ctx")),
        ),
        check_vma=False,
    )
```

```python
import functools
import jax
import jax.numpy as jnp
from jax import lax
from jax.experimental import pallas as pl
from jax.experimental.pallas import tpu as pltpu
from jax.sharding import PartitionSpec as P

HD = 64
EPS = 1e-05
ROPE_BASE = 500000.0
NEG = -1e30
BF = jnp.bfloat16
F32 = jnp.float32
VMEM_MOST = 60 * 1024 * 1024


def cost(flops, nbytes, trans=0):
    return pl.CostEstimate(flops=int(flops), bytes_accessed=int(nbytes), transcendentals=int(trans))


def nt(a, b):
    return lax.dot_general(a, b, (((1,), (1,)), ((), ())), preferred_element_type=F32)


def tn(a, b):
    return lax.dot_general(a, b, (((0,), (0,)), ((), ())), preferred_element_type=F32)


def nn(a, b):
    return jnp.dot(a, b, preferred_element_type=F32)


def swap_halves(t):
    lane = lax.broadcasted_iota(jnp.int32, t.shape, 1) % HD
    n = t.shape[1]
    return jnp.where(
        lane < HD // 2, pltpu.roll(t, n - HD // 2, 1), pltpu.roll(t, HD // 2, 1)
    )


def rope_tables(first, span):
    position = (first + jnp.arange(span)).astype(F32)
    frequency = ROPE_BASE ** (-jnp.arange(HD // 2).astype(F32) * 2.0 / HD)
    angle = position[:, None] * frequency[None, :]
    cosine, sine = jnp.cos(angle), jnp.sin(angle)
    return (
        jnp.concatenate([cosine, cosine, cosine, cosine], axis=1),
        jnp.concatenate([-sine, sine, -sine, sine], axis=1),
    )


def mask_bias(first, prefix, length, span):
    key = lax.broadcasted_iota(jnp.int32, (length, span), 0)
    query = lax.broadcasted_iota(jnp.int32, (length, span), 1) + first
    return jnp.where((key <= query) | (key < prefix), 0.0, NEG).astype(F32)


def gate_parts(gate, up, d_act):
    sig = 1.0 / (1.0 + jnp.exp(-gate))
    silu = gate * sig
    return (
        (silu * up).astype(BF),
        (d_act * up * (sig + silu * (1.0 - sig))).astype(BF),
        (d_act * silu).astype(BF),
    )


MESH = pl.DeviceIdType.MESH


def remote(src, dst, send, recv, to):
    return pltpu.make_async_remote_copy(
        src_ref=src, dst_ref=dst, send_sem=send, recv_sem=recv, device_id=to, device_id_type=MESH
    )


def enter(devices):
    barrier = pltpu.get_barrier_semaphore()
    for to in devices:
        pl.semaphore_signal(barrier, inc=1, device_id=to, device_id_type=MESH)
    pl.semaphore_wait(barrier, len(devices))


def around(z, ndp):
    return [{"dp": lax.rem(z + 1, ndp)}, {"dp": lax.rem(z + ndp - 1, ndp)}]


def mates(me, y):
    return [{"ctx": me ^ 1}, {"ctx": me ^ 2}, {"ctx": me ^ 3}, {"tensor": 1 - y}]


class Relay:
    def __init__(self, z, ndp, hop, own, blocks, sems):
        self.z, self.ndp, self.hop = z, ndp, hop
        self.own, self.blocks, self.sems = own, blocks, sems

    def copy(self, way, block, to):
        src = self.own if self.hop == 1 else self.blocks.at[block]
        at = 0 if way > 0 else 1
        return remote(
            src, self.blocks.at[block], self.sems.at[0, at], self.sems.at[1, at], {"dp": to}
        )

    def each(self, act, incoming):
        z, hop = self.z, self.hop
        for way in (1, -1):
            if incoming:
                block = z - way * hop
                ok = block >= 0 if way > 0 else block < self.ndp
            else:
                block = z - way * (hop - 1)
                ok = (block >= 0) & (z < self.ndp - 1) if way > 0 else (block < self.ndp) & (z > 0)

            @pl.when(ok)
            def _(way=way, block=block):
                act(self.copy(way, block, z if incoming else z + way))

    def start(self):
        self.each(lambda c: c.start(), False)

    def wait_recv(self):
        self.each(lambda c: c.wait_recv(), True)

    def wait_send(self):
        self.each(lambda c: c.wait_send(), False)


def rope_parts(t, cosine, sine):
    pieces = []
    for i in range(t.shape[1] // 128):
        part = t[:, 128 * i : 128 * (i + 1)]
        pieces.append((part * cosine + swap_halves(part) * sine).astype(BF))
    return pieces


def front_kernel(
    ndp, nctx, group,
    where_ref, x_ref, gain1_ref, wq_hbm, wk_hbm, wv_hbm, wo_hbm, cos_ref, sin_ref, gain2_ref, og_hbm,
    n1_ref, q_ref, kv_out, att_ref, lse_ref, resid_ref, n2_ref, og_all,
    n1_buf, wq, wk, wv, wo, kv, bias_ref, part, part_got,
    w_sem, kv_sem, kv_out_sem, part_sem, z_sem,
):
    z, me, y = lax.axis_index("dp"), lax.axis_index("ctx"), lax.axis_index("tensor")
    span, width = x_ref.shape
    length = kv.shape[0]
    kvw = wk.shape[1]
    loads = [
        pltpu.make_async_copy(src, dst, w_sem.at[i])
        for i, (src, dst) in enumerate(((wk_hbm, wk), (wv_hbm, wv), (wq_hbm, wq), (wo_hbm, wo)))
    ]
    for copy in loads:
        copy.start()
    hop1 = Relay(z, ndp, 1, og_hbm, og_all, z_sem.at[0])
    hop2 = Relay(z, ndp, 2, og_hbm, og_all, z_sem.at[1])
    enter(around(z, ndp) + mates(me, y))
    hop1.start()
    v = x_ref[...].astype(F32)
    factor = lax.rsqrt(jnp.mean(v * v, axis=-1, keepdims=True) + EPS)
    n1_buf[...] = (v * factor * gain1_ref[...]).astype(BF)
    cosine, sine = cos_ref[...], sin_ref[...]
    mine = pl.ds(pl.multiple_of(me * span, span), span)
    loads[0].wait()
    for i, piece in enumerate(rope_parts(nn(n1_buf[...], wk[...]), cosine, sine)):
        kv[mine, 128 * i : 128 * (i + 1)] = piece
    loads[1].wait()
    kv[mine, kvw:] = nn(n1_buf[...], wv[...]).astype(BF)

    def kv_copy(which, block, mask):
        rows = pl.ds(pl.multiple_of(block * span, span), span)
        return remote(kv.at[rows], kv.at[rows], kv_sem.at[0, which], kv_sem.at[1, which], {"ctx": me ^ mask})

    to_x = kv_copy(0, me, 2)
    to_core = kv_copy(1, me, 1)
    onward = kv_copy(2, me ^ 2, 1)
    to_x.start()
    to_core.start()
    loads[2].wait()
    for i, piece in enumerate(rope_parts(nn(n1_buf[...], wq[...]), cosine, sine)):
        q_ref[:, 128 * i : 128 * (i + 1)] = piece
    part_width = width // (ndp * nctx)
    for p in range(nctx):
        for b in range(ndp):
            at = (b * nctx + p) * part_width
            n1_ref[p, :, b * part_width : (b + 1) * part_width] = n1_buf[:, at : at + part_width]
    bias_ref[...] = mask_bias(where_ref[0], where_ref[1], length, span)
    to_x.wait_recv()
    onward.start()
    to_core.wait_recv()
    onward.wait_recv()
    to_x.wait_send()
    to_core.wait_send()
    onward.wait_send()
    save_kv = pltpu.make_async_copy(kv, kv_out, kv_out_sem)
    save_kv.start()

    wide = 128 * group
    heads = wide // HD

    @pl.loop(0, kvw // 128)
    def _(j):
        lanes = pl.ds(pl.multiple_of(j * wide, 128), wide)
        queries = q_ref[:, lanes] * jnp.asarray(HD**-0.5, BF)
        keys = kv[:, pl.ds(pl.multiple_of(j * 128, 128), 128)]
        values = kv[:, pl.ds(pl.multiple_of(kvw + j * 128, 128), 128)]
        rows, outs = [], []
        for h in range(heads):
            at = slice(HD * (h // group), HD * (h // group + 1))
            scores = nt(keys[:, at], queries[:, HD * h : HD * (h + 1)]) + bias_ref[...]
            top = jnp.max(scores, axis=0, keepdims=True)
            exponent = jnp.exp(scores - top)
            total = jnp.sum(exponent, axis=0, keepdims=True)
            rows.append(top + jnp.log(total))
            outs.append(tn(values[:, at], exponent.astype(BF)) / total)
            if h % 2:
                both = jnp.concatenate(outs, axis=0).T.astype(BF)
                att_ref[:, pl.ds(pl.multiple_of(j * wide + HD * (h - 1), 128), 128)] = both
                outs = []
        lse_ref[pl.ds(pl.multiple_of(j * heads, heads), heads), :] = jnp.concatenate(rows, axis=0)

    hop1.wait_recv()
    hop2.start()
    save_kv.wait()
    loads[3].wait()
    count, _, cols = part.shape
    copies = [
        remote(part.at[c], part_got.at[c], part_sem.at[0, c], part_sem.at[1, c], {"tensor": 1 - y})
        for c in range(count)
    ]
    for c in range(count):
        part[c] = nn(att_ref[...], wo[:, c * cols : (c + 1) * cols]).astype(BF)
        copies[c].start()
    square = jnp.zeros((span, 1), F32)
    for c in range(count):
        at = slice(c * cols, (c + 1) * cols)
        copies[c].wait_recv()
        r = x_ref[:, at].astype(F32) + (part[c].astype(F32) + part_got[c].astype(F32))
        resid_ref[:, at] = r
        square += jnp.sum(r * r, axis=-1, keepdims=True)
    factor = lax.rsqrt(square / width + EPS)
    for c in range(count):
        at = slice(c * cols, (c + 1) * cols)
        n2_ref[:, at] = (resid_ref[:, at] * factor * gain2_ref[:, at]).astype(BF)
    for copy in copies:
        copy.wait_send()
    hop1.wait_send()
    hop2.wait_recv()
    hop2.wait_send()


HBM_SPEC = pl.BlockSpec(memory_space=pl.ANY)
VMEM_SPEC = pl.BlockSpec(memory_space=pltpu.VMEM)
SMEM_SPEC = pl.BlockSpec(memory_space=pltpu.SMEM)


def own(number):
    return pltpu.CompilerParams(
        vmem_limit_bytes=VMEM_MOST, collective_id=number, has_side_effects=True
    )


def front(where, x, gain1, wq, wk, wv, wo, cosine, sine, gain2, og, ndp, nctx):
    span, width = x.shape
    qw, kvw = wq.shape[1], wk.shape[1]
    group = qw // kvw
    length = span * nctx
    chunks = 4
    dma = pltpu.SemaphoreType.DMA
    return pl.pallas_call(
        functools.partial(front_kernel, ndp, nctx, group),
        in_specs=[SMEM_SPEC, VMEM_SPEC, VMEM_SPEC] + [HBM_SPEC] * 4 + [VMEM_SPEC] * 3 + [HBM_SPEC],
        out_specs=[VMEM_SPEC, VMEM_SPEC, HBM_SPEC] + [VMEM_SPEC] * 4 + [HBM_SPEC],
        out_shape=[
            jax.ShapeDtypeStruct((nctx, span, width // nctx), BF),
            jax.ShapeDtypeStruct((span, qw), BF),
            jax.ShapeDtypeStruct((length, 2 * kvw), BF),
            jax.ShapeDtypeStruct((span, qw), BF),
            jax.ShapeDtypeStruct((qw // HD, span), F32),
            jax.ShapeDtypeStruct((span, width), F32),
            jax.ShapeDtypeStruct((span, width), BF),
            jax.ShapeDtypeStruct((ndp, span, width), BF),
        ],
        scratch_shapes=[
            pltpu.VMEM((span, width), BF),
            pltpu.VMEM((width, qw), BF),
            pltpu.VMEM((width, kvw), BF),
            pltpu.VMEM((width, kvw), BF),
            pltpu.VMEM((qw, width), BF),
            pltpu.VMEM((length, 2 * kvw), BF),
            pltpu.VMEM((length, span), F32),
            pltpu.VMEM((chunks, span, width // chunks), BF),
            pltpu.VMEM((chunks, span, width // chunks), BF),
            dma((4,)),
            dma((2, 3)),
            dma,
            dma((2, chunks)),
            dma((2, 2, 2)),
        ],
        compiler_params=own(0),
        cost_estimate=cost(2 * span * width * (2 * qw + 2 * kvw), 4 * width * (qw + kvw)),
        name="front",
    )(where, x, gain1.reshape(1, width), wq, wk, wv, wo, cosine, sine, gain2.reshape(1, width), og)


def halves(y, span):
    return pl.ds(pl.multiple_of(y * (span // 2), span // 2), span // 2)


class Far:
    def __init__(self, z, y, blocks, far, sems):
        rows = halves(y, far.shape[0])
        block = jnp.where(z == 1, 3, 0)
        to = jnp.where(z == 1, 0, 3)
        self.over = remote(blocks.at[block, rows], far.at[rows], sems.at[0], sems.at[1], {"dp": to})
        self.gives = (z == 1) | (z == 2)
        self.takes = (z == 0) | (z == 3)

    def start(self):
        pl.when(self.gives)(lambda: self.over.start())

    def finish(self):
        pl.when(self.takes)(lambda: self.over.wait_recv())
        pl.when(self.gives)(lambda: self.over.wait_send())


class Gather:
    def __init__(self, z, y, ndp, own, blocks, sems, swaps):
        self.z, self.y, self.ndp = z, y, ndp
        self.own, self.blocks, self.sems, self.swaps = own, blocks, sems, swaps
        self.rows = halves(y, own.shape[0])

    def over(self, way, hop, block, to):
        src = self.own.at[self.rows] if hop == 1 else self.blocks.at[block, self.rows]
        at = 0 if way > 0 else 1
        return remote(
            src, self.blocks.at[block, self.rows],
            self.sems.at[hop - 1, 0, at], self.sems.at[hop - 1, 1, at], {"dp": to},
        )

    def swap(self, way, hop, block):
        at = 0 if way > 0 else 1
        part = self.blocks.at[block, self.rows]
        return remote(
            part, part, self.swaps.at[hop - 1, 0, at], self.swaps.at[hop - 1, 1, at],
            {"tensor": 1 - self.y},
        )

    def comes(self, way, hop):
        block = self.z - way * hop
        return block, (block >= 0 if way > 0 else block < self.ndp)

    def leaves(self, way, hop):
        block = self.z - way * (hop - 1)
        if way > 0:
            return block, (block >= 0) & (self.z < self.ndp - 1)
        return block, (block < self.ndp) & (self.z > 0)

    def send(self, hop):
        for way in (1, -1):
            block, ok = self.leaves(way, hop)

            @pl.when(ok)
            def _(way=way, block=block):
                self.over(way, hop, block, self.z + way).start()

    def step(self, hop):
        for way in (1, -1):
            block, ok = self.comes(way, hop)

            @pl.when(ok)
            def _(way=way, block=block):
                self.over(way, hop, block, self.z).wait_recv()
                self.swap(way, hop, block).start()

        if hop < self.ndp - 1:
            self.send(hop + 1)

    def finish(self):
        for hop in range(1, self.ndp):
            for way in (1, -1):
                block, ok = self.comes(way, hop)

                @pl.when(ok)
                def _(way=way, block=block, hop=hop):
                    self.swap(way, hop, block).wait()

                block, ok = self.leaves(way, hop)

                @pl.when(ok)
                def _(way=way, block=block, hop=hop):
                    self.over(way, hop, block, self.z + way).wait_send()


def middle_kernel(
    ndp, nctx,
    n_ref, g_ref, wg_ref, wu_ref, wd_ref, n_hbm, n1_hbm, att_hbm, g_near,
    o_ref, dn_ref, n_all, n1_all, att_all, g_far,
    o_acc, dn_acc,
    z_sem, swap_sem, n1_sem, att_sem, far_sem,
):
    z, me, y = lax.axis_index("dp"), lax.axis_index("ctx"), lax.axis_index("tensor")
    j = pl.program_id(0)
    last = pl.num_programs(0) - 1
    gather = Gather(z, y, ndp, n_hbm, n_all, z_sem, swap_sem)
    far = Far(z, y, g_near, g_far, far_sem)
    spreads = []
    for m in range(1, nctx):
        spreads.append(
            remote(n1_hbm.at[me ^ m], n1_all.at[me], n1_sem.at[0, m], n1_sem.at[1, m], {"ctx": me ^ m})
        )
        spreads.append(
            remote(att_hbm, att_all.at[me], att_sem.at[0, m], att_sem.at[1, m], {"ctx": me ^ m})
        )

    @pl.when(j == 0)
    def _():
        enter(around(z, ndp) + mates(me, y))
        gather.send(1)
        for copy in spreads:
            copy.start()

    normed2, grad = n_ref[...], g_ref[...]
    gate = nn(normed2, wg_ref[...])
    up = nn(normed2, wu_ref[...])
    d_act = nt(grad, wd_ref[...])
    act, d_gate, d_up = gate_parts(gate, up, d_act)

    @pl.when(j == 0)
    def _():
        o_acc[...] = nn(act, wd_ref[...])
        dn_acc[...] = nt(d_gate, wg_ref[...]) + nt(d_up, wu_ref[...])

    @pl.when(j > 0)
    def _():
        o_acc[...] += nn(act, wd_ref[...])
        dn_acc[...] += nt(d_gate, wg_ref[...]) + nt(d_up, wu_ref[...])

    @pl.when(j == 3)
    def _():
        gather.step(1)

    @pl.when(j == 5)
    def _():
        gather.step(2)
        far.start()

    @pl.when(j == last)
    def _():
        gather.step(3)
        o_ref[...] = o_acc[...].astype(BF)
        dn_ref[...] = dn_acc[...].astype(BF)
        for copy in spreads:
            copy.wait()
        far.finish()
        gather.finish()


def middle(n2, og, wg, wu, wd, n1p, att, og_all, ndp, nctx, step=512):
    span, width = n2.shape
    units = wg.shape[1]
    dma = pltpu.SemaphoreType.DMA
    whole = pl.BlockSpec((span, width), lambda j: (0, 0))
    cols = pl.BlockSpec((width, step), lambda j: (0, j))
    return pl.pallas_call(
        functools.partial(middle_kernel, ndp, nctx),
        grid=(units // step,),
        in_specs=[
            whole, whole, cols, cols, pl.BlockSpec((step, width), lambda j: (j, 0)),
            HBM_SPEC, HBM_SPEC, HBM_SPEC, HBM_SPEC,
        ],
        out_specs=[whole, whole, HBM_SPEC, HBM_SPEC, HBM_SPEC, HBM_SPEC],
        out_shape=[
            jax.ShapeDtypeStruct((span, width), BF),
            jax.ShapeDtypeStruct((span, width), BF),
            jax.ShapeDtypeStruct((ndp, span, width), BF),
            jax.ShapeDtypeStruct((nctx, span, width // nctx), BF),
            jax.ShapeDtypeStruct((nctx,) + att.shape, BF),
            jax.ShapeDtypeStruct((span, width), BF),
        ],
        scratch_shapes=[
            pltpu.VMEM((span, width), F32),
            pltpu.VMEM((span, width), F32),
            dma((ndp - 1, 2, 2)),
            dma((ndp - 1, 2, 2)),
            dma((2, nctx)),
            dma((2, nctx)),
            dma((2,)),
        ],
        compiler_params=own(1),
        cost_estimate=cost(12 * span * width * units, 6 * width * units),
        name="middle",
    )(n2, og, wg, wu, wd, n2, n1p, att, og_all)


def rear_kernel(
    ndp, nctx, group, chunk, rows,
    where_ref, q_ref, kv_ref, lse_ref, cos_ref, sin_ref, gain_ref, dn_ref,
    n_own, n_near, g_own, g_near, g_far, wg_hbm, wu_hbm, wd_hbm, wq_hbm, wk_hbm, wv_hbm, wo_hbm,
    resid_hbm, n1_own, n1_near, att_own, att_near, out_hbm,
    down_z, gate_z, up_z, att_z, front_out, front_got, out_got, dr_out, gain_grad_ref,
    n_all, g_all, acts, wg_buf, wu_buf, wd_buf, give, take, x_give, x_take, x_keep,
    left1, left2, right1, right2, prod, low, d_att, bias_ref, dkv, land, acc,
    in_sem, l_sem, w_sem, back_sem, dn_sem, low_sem, dkv_sem, r_sem, core_sem, x_sem, zz_sem, z_own,
    att_sem, y_sem, save_sem, far_sem,
):
    z, me, y = lax.axis_index("dp"), lax.axis_index("ctx"), lax.axis_index("tensor")
    tokens, width = n_all.shape
    span, qw = q_ref.shape
    length = kv_ref.shape[0]
    kvw = kv_ref.shape[1] // 2
    units = acts.shape[1]
    core, xpos = me % 2, me // 2
    part = width // (ndp * nctx)
    start = z * units
    peers = [{"dp": lax.rem(z + s, ndp)} for s in range(1, ndp)]
    mate = {"tensor": 1 - y}
    mine = pl.ds(pl.multiple_of(me * span, span), span)
    cross = pl.ds(pl.multiple_of((me ^ 2) * span, span), span)

    def block_load(r, own_ref, near, dst, sem):
        block = lax.rem(jnp.where(z < ndp // 2, z + r, z + ndp - r), ndp)
        at = dst.at[pl.ds(r * span, span)]
        return pltpu.make_async_copy(own_ref if r == 0 else near.at[block], at, sem)

    def go(copies):
        for ok, copy in copies:
            if ok is None:
                copy.start()
            else:
                pl.when(ok)(lambda copy=copy: copy.start())

    def done(copies):
        copies[0][1].wait()

    n_loads = [block_load(r, n_own, n_near, n_all, in_sem.at[0, r]) for r in range(ndp)]
    g_loads = [block_load(r, g_own, g_near, g_all, in_sem.at[1, r]) for r in range(ndp)]
    end = (z == 0) | (z == ndp - 1)
    tail = ndp - 1
    half_rows = halves(y, span)
    half_at = g_all.at[pl.ds(pl.multiple_of(tail * span + y * (span // 2), span // 2), span // 2)]
    half_load = pltpu.make_async_copy(g_far.at[half_rows], half_at, in_sem.at[1, tail])
    half_swap = remote(g_far.at[half_rows], half_at, far_sem.at[0], far_sem.at[1], mate)

    def ctx_load(p, own_ref, near, dst, sem):
        at = dst.at[pl.ds(p * span, span)]
        here = me == p
        return [
            (here, pltpu.make_async_copy(own_ref, at, sem)),
            (jnp.logical_not(here), pltpu.make_async_copy(near.at[p], at, sem)),
        ]

    l_loads = []
    for p in range(nctx):
        l_loads.append(ctx_load(p, att_own, att_near, right2, l_sem.at[0, p]))
        l_loads.append(ctx_load(p, n1_own.at[p], n1_near, left1, l_sem.at[1, p]))

    def weights(j, slot):
        at = pl.multiple_of(start + j * chunk, chunk)
        return (
            pltpu.make_async_copy(wg_hbm.at[:, pl.ds(at, chunk)], wg_buf.at[slot], w_sem.at[slot, 0]),
            pltpu.make_async_copy(wu_hbm.at[:, pl.ds(at, chunk)], wu_buf.at[slot], w_sem.at[slot, 1]),
            pltpu.make_async_copy(wd_hbm.at[pl.ds(at, chunk)], wd_buf.at[slot], w_sem.at[slot, 2]),
        )

    for copy in n_loads + g_loads[:tail]:
        copy.start()
    pl.when(end)(lambda: half_load.start())
    pl.when(jnp.logical_not(end))(lambda: g_loads[tail].start())
    for copy in weights(0, 0):
        copy.start()
    resid_load = pltpu.make_async_copy(resid_hbm, acc, save_sem.at[0])
    resid_load.start()
    for copies in l_loads:
        go(copies)
    dn_got = [x_take.at[2, pl.ds(h * span, span)] for h in range(2)]
    half = width // 2
    dn_copies = [
        remote(
            dn_ref.at[:, pl.ds(h * half, half)], dn_got[h], dn_sem.at[0, h], dn_sem.at[1, h], mate
        )
        for h in range(2)
    ]
    enter(peers + mates(me, y))
    pl.when(end)(lambda: half_swap.start())
    for copy in dn_copies:
        copy.start()

    count = units // chunk
    for copy in n_loads + g_loads[:tail]:
        copy.wait()

    @pl.loop(0, count)
    def _(j):
        slot = j % 2
        for copy in weights(j, slot):
            copy.wait()

        @pl.when(j + 1 < count)
        def _():
            for copy in weights(j + 1, 1 - slot):
                copy.start()

        cols = pl.ds(pl.multiple_of(j * chunk, chunk), chunk)

        @pl.loop(0, tokens // rows)
        def _(i):
            @pl.when((j == 0) & (i == tail))
            def _():
                pl.when(jnp.logical_not(end))(lambda: g_loads[tail].wait())

                @pl.when(end)
                def _():
                    half_load.wait()
                    half_swap.wait()

            some = pl.ds(pl.multiple_of(i * rows, rows), rows)
            gate = nn(n_all[some], wg_buf[slot])
            up = nn(n_all[some], wu_buf[slot])
            d_act = nt(g_all[some], wd_buf[slot])
            for w, value in enumerate(gate_parts(gate, up, d_act)):
                acts[pl.ds(pl.multiple_of(w * tokens + i * rows, rows), rows), cols] = value

    lefts = (g_all, n_all, n_all)

    def product(w, x, c):
        left = lefts[w]
        block = jnp.concatenate(
            [
                left[:, pl.ds(pl.multiple_of((k * nctx + x * 2 + c) * part, part), part)]
                for k in range(ndp)
            ],
            axis=1,
        )
        return tn(block, acts[w * tokens : (w + 1) * tokens])

    core_copies = [
        remote(give.at[w % 2], take.at[w % 2], core_sem.at[0, w], core_sem.at[1, w], {"ctx": me ^ 1})
        for w in range(3)
    ]
    x_copies = [
        remote(x_give.at[w], x_take.at[w], x_sem.at[0, w], x_sem.at[1, w], {"ctx": me ^ 2})
        for w in range(3)
    ]

    def hand(w):
        give[w % 2, 0] = product(w, 1 - xpos, 1 - core).astype(BF)
        give[w % 2, 1] = product(w, xpos, 1 - core).astype(BF)
        core_copies[w].start()

    def keep(w):
        there = product(w, 1 - xpos, core)
        core_copies[w].wait()
        x_give[w] = (there + take[w % 2, 0].astype(F32)).astype(BF)
        if w < 2:
            x_copies[w].start()
        x_keep[w] = (product(w, xpos, core) + take[w % 2, 1].astype(F32)).astype(BF)

    hand(0)
    keep(0)
    hand(1)
    keep(1)
    hand(2)
    keep(2)

    def z_rows(k):
        return pl.ds(pl.multiple_of(k * part, part), part)

    z_units = pl.ds(pl.multiple_of(start, units), units)

    def landing(w):
        return down_z.at[z] if w == 0 else (gate_z, up_z)[w - 1].at[:, z_units]

    def z_copies(w):
        return [
            remote(
                x_keep.at[w, z_rows(lax.rem(z + s, ndp))],
                landing(w),
                zz_sem.at[0, w, s],
                zz_sem.at[1, w, s],
                peers[s - 1],
            )
            for s in range(1, ndp)
        ]

    def z_own_copy(w):
        return pltpu.make_async_copy(x_keep.at[w, z_rows(z)], landing(w), z_own.at[w])

    def serve(w):
        x_copies[w].wait()
        x_keep[w] = (x_keep[w].astype(F32) + x_take[w].astype(F32)).astype(BF)
        for copy in z_copies(w):
            copy.start()
        z_own_copy(w).start()

    wo, wq = n_all, acts.at[pl.ds(0, width)]
    wk, wv = wg_buf.at[0], wu_buf.at[0]
    loads = [
        pltpu.make_async_copy(src, dst, back_sem.at[i])
        for i, (src, dst) in enumerate(((wo_hbm, wo), (wq_hbm, wq), (wk_hbm, wk), (wv_hbm, wv)))
    ]
    for copy in loads:
        copy.start()
    bias_ref[...] = mask_bias(where_ref[0], where_ref[1], length, span)
    resid_load.wait()
    v = acc[...]
    factor = lax.rsqrt(jnp.mean(v * v, axis=-1, keepdims=True) + EPS)
    for copy in dn_copies:
        copy.wait()
    y_out = remote(out_hbm, out_got, y_sem.at[0, 1], y_sem.at[1, 1], mate)
    y_out.start()
    cols = width // 4

    def dn_part(c):
        return dn_got[c // 2][:, (c % 2) * cols : (c % 2 + 1) * cols]

    dots = jnp.zeros((span, 1), F32)
    for c in range(4):
        at = slice(c * cols, (c + 1) * cols)
        unit = acc[:, at] * factor
        back = dn_ref[:, at].astype(F32) + dn_part(c).astype(F32)
        term = back * unit
        gain_grad_ref[:, at] = jnp.sum(term, axis=0, keepdims=True)
        dots += jnp.sum(term * gain_ref[:, at], axis=-1, keepdims=True)
    dots = dots / width
    for c in range(4):
        at = slice(c * cols, (c + 1) * cols)
        unit = acc[:, at] * factor
        back = dn_ref[:, at].astype(F32) + dn_part(c).astype(F32)
        total = g_all[:span, at].astype(F32) + factor * (back * gain_ref[:, at] - unit * dots)
        acc[:, at] = total
        low[:, at] = total.astype(BF)
    dr_save = pltpu.make_async_copy(acc, dr_out, save_sem.at[1])
    dr_save.start()

    spread = width // nctx

    def low_rows(p):
        return pl.ds(pl.multiple_of(p // 2 * span, span), span)

    def low_cols(p):
        return pl.ds(pl.multiple_of(p % 2 * spread, spread), spread)

    for p in range(nctx):
        for b in range(ndp):
            at = (b * nctx + p) * part
            to = p % 2 * spread + b * part
            give[0, 0, p // 2 * span : (p // 2 + 1) * span, to : to + part] = low[:, at : at + part]
    spreads = [
        remote(
            give.at[0, 0, low_rows(me ^ m), low_cols(me ^ m)],
            left2.at[mine],
            low_sem.at[0, m],
            low_sem.at[1, m],
            {"ctx": me ^ m},
        )
        for m in range(1, nctx)
    ]
    for copy in spreads:
        copy.start()
    left2[mine, :] = give[0, 0, low_rows(me), low_cols(me)]
    loads[0].wait()
    d_att[...] = nt(low[...], wo[...]).astype(BF)
    wide = 128 * group
    heads = wide // HD
    blocks = kvw // 128
    scale = jnp.asarray(HD**-0.5, BF)

    def share(j, m):
        some = pl.ds(pl.multiple_of((me ^ m) * span, span), span)
        return remote(
            dkv.at[j, some], land.at[j, m], dkv_sem.at[0, j, m], dkv_sem.at[1, j, m], {"ctx": me ^ m}
        )

    @pl.loop(0, blocks)
    def _(j):
        lanes = pl.ds(pl.multiple_of(j * wide, 128), wide)
        queries = q_ref[:, lanes] * scale
        grads = d_att[:, lanes]
        keys = kv_ref[:, pl.ds(pl.multiple_of(j * 128, 128), 128)]
        values = kv_ref[:, pl.ds(pl.multiple_of(kvw + j * 128, 128), 128)]
        lse = lse_ref[pl.ds(pl.multiple_of(j * heads, heads), heads), :]
        pair = []
        for h in range(heads):
            at = slice(HD * (h // group), HD * (h // group + 1))
            key, value = keys[:, at], values[:, at]
            query = queries[:, HD * h : HD * (h + 1)]
            grad = grads[:, HD * h : HD * (h + 1)]
            probs = jnp.exp(nt(key, query) + (bias_ref[...] - lse[h : h + 1, :]))
            d_probs = nt(value, grad)
            delta = jnp.sum(probs * d_probs, axis=0, keepdims=True)
            d_scores = (probs * (d_probs - delta)).astype(BF)
            d_value = nn(probs.astype(BF), grad)
            d_key = nn(d_scores, query)
            if h % group == 0:
                sum_key, sum_value = d_key, d_value
            else:
                sum_key, sum_value = sum_key + d_key, sum_value + d_value
            if h % group == group - 1:
                dkv[j, :, at] = sum_key.astype(BF)
                dkv[j, :, slice(128 + at.start, 128 + at.stop)] = sum_value.astype(BF)
            pair.append(tn(key * scale, d_scores))
            if h % 2:
                both = jnp.concatenate(pair, axis=0).T
                turned = both * cos_ref[...] - swap_halves(both) * sin_ref[...]
                right1[mine, pl.ds(pl.multiple_of(j * wide + HD * (h - 1), 128), 128)] = turned.astype(BF)
                pair = []
        for m in range(1, nctx):
            share(j, m).start()

        @pl.when(j == 0)
        def _():
            serve(0)

    loads[1].wait()
    dr_save.wait()
    acc[...] = nt(right1[mine, :qw], wq[...])
    serve(1)
    for j in range(blocks):
        total = dkv[j, mine].astype(F32)
        for m in range(1, nctx):
            share(j, m).wait_recv()
            total += land[j, m].astype(F32)
        d_key = total[:, :128]
        d_key = d_key * cos_ref[...] - swap_halves(d_key) * sin_ref[...]
        right1[mine, qw + 128 * j : qw + 128 * (j + 1)] = d_key.astype(BF)
        right1[mine, qw + kvw + 128 * j : qw + kvw + 128 * (j + 1)] = total[:, 128:].astype(BF)
    own_rows = right1.at[mine]
    r_x = remote(own_rows, own_rows, r_sem.at[0, 0], r_sem.at[1, 0], {"ctx": me ^ 2})
    r_core = remote(own_rows, own_rows, r_sem.at[0, 1], r_sem.at[1, 1], {"ctx": me ^ 1})
    r_onward = remote(
        right1.at[cross], right1.at[cross], r_sem.at[0, 2], r_sem.at[1, 2], {"ctx": me ^ 1}
    )
    r_x.start()
    r_core.start()
    x_copies[2].start()
    loads[2].wait()
    loads[3].wait()
    low[...] = (
        acc[...]
        + nt(right1[mine, qw : qw + kvw], wk[...])
        + nt(right1[mine, qw + kvw :], wv[...])
    ).astype(BF)
    front_save = pltpu.make_async_copy(low, front_out, save_sem.at[2])
    y_front = remote(low, front_got, y_sem.at[0, 0], y_sem.at[1, 0], mate)
    front_save.start()
    y_front.start()

    nq = right1.shape[1]

    def att_copies(w, at):
        return [
            remote(
                prod.at[z_rows(lax.rem(z + s, ndp)), at],
                att_z.at[z, :, at],
                att_sem.at[0, w, s],
                att_sem.at[1, w, s],
                peers[s - 1],
            )
            for s in range(1, ndp)
        ]

    def att_own_copy(w, at):
        return pltpu.make_async_copy(
            prod.at[z_rows(z), at], att_z.at[z, :, at], att_sem.at[0, w, 0]
        )

    out_cols = slice(nq, prod.shape[1])
    qkv_cols = slice(0, nq)
    for copies in l_loads:
        done(copies)
    for copy in spreads:
        copy.wait()
    prod[:, out_cols] = tn(left2[...], right2[...]).astype(BF)
    for copy in att_copies(1, out_cols):
        copy.start()
    att_own_copy(1, out_cols).start()
    r_x.wait_recv()
    r_onward.start()
    r_core.wait_recv()
    r_onward.wait_recv()
    prod[:, qkv_cols] = tn(left1[...], right1[...]).astype(BF)
    for copy in att_copies(0, qkv_cols):
        copy.start()
    att_own_copy(0, qkv_cols).start()
    serve(2)
    for j in range(blocks):
        for m in range(1, nctx):
            share(j, m).wait_send()
    y_out.wait()
    y_front.wait()
    front_save.wait()
    r_x.wait_send()
    r_core.wait_send()
    r_onward.wait_send()
    for w, at in ((1, out_cols), (0, qkv_cols)):
        for copy in att_copies(w, at):
            copy.wait()
        att_own_copy(w, at).wait()
    for w in range(3):
        for copy in z_copies(w):
            copy.wait()
        z_own_copy(w).wait()


def rear(
    where, q, kv, lse, cosine, sine, gain, dn, n2, n_all, og, og_all, og_far, wg, wu, wd,
    wq, wk, wv, wo, resid, n1p, n1_all, att, att_all, out_part, ndp, nctx, chunk=256, rows=256,
):
    span, width = n2.shape
    tokens, length = span * ndp, span * nctx
    units = wg.shape[1] // ndp
    part = width // (ndp * nctx)
    mine = ndp * part
    qw, kvw = wq.shape[1], wk.shape[1]
    qkvw = qw + 2 * kvw
    dma = pltpu.SemaphoreType.DMA
    flat = jax.ShapeDtypeStruct((part, ndp * units), BF)
    row = jax.ShapeDtypeStruct((span, width), BF)
    return pl.pallas_call(
        functools.partial(rear_kernel, ndp, nctx, qw // kvw, chunk, rows),
        in_specs=[SMEM_SPEC] + [VMEM_SPEC] * 7 + [HBM_SPEC] * 18,
        out_specs=[HBM_SPEC] * 8 + [VMEM_SPEC],
        out_shape=[
            jax.ShapeDtypeStruct((ndp, part, units), BF),
            flat,
            flat,
            jax.ShapeDtypeStruct((ndp, part, qkvw + qw), BF),
            row,
            row,
            row,
            jax.ShapeDtypeStruct((span, width), F32),
            jax.ShapeDtypeStruct((1, width), F32),
        ],
        scratch_shapes=[
            pltpu.VMEM((tokens, width), BF),
            pltpu.VMEM((tokens, width), BF),
            pltpu.VMEM((3 * tokens, units), BF),
            pltpu.VMEM((2, width, chunk), BF),
            pltpu.VMEM((2, width, chunk), BF),
            pltpu.VMEM((2, chunk, width), BF),
            pltpu.VMEM((2, 2, mine, units), BF),
            pltpu.VMEM((2, 2, mine, units), BF),
            pltpu.VMEM((3, mine, units), BF),
            pltpu.VMEM((3, mine, units), BF),
            pltpu.VMEM((3, mine, units), BF),
            pltpu.VMEM((length, width // nctx), BF),
            pltpu.VMEM((length, width // nctx), BF),
            pltpu.VMEM((length, qkvw), BF),
            pltpu.VMEM((length, qw), BF),
            pltpu.VMEM((mine, qkvw + qw), BF),
            pltpu.VMEM((span, width), BF),
            pltpu.VMEM((span, qw), BF),
            pltpu.VMEM((length, span), F32),
            pltpu.VMEM((kvw // 128, length, 256), BF),
            pltpu.VMEM((kvw // 128, nctx, span, 256), BF),
            pltpu.VMEM((span, width), F32),
            dma((2, ndp)),
            dma((2, nctx)),
            dma((2, 3)),
            dma((4,)),
            dma((2, 2)),
            dma((2, nctx)),
            dma((2, kvw // 128, nctx)),
            dma((2, 3)),
            dma((2, 3)),
            dma((2, 3)),
            dma((2, 3, ndp)),
            dma((3,)),
            dma((2, 2, ndp)),
            dma((2, 2)),
            dma((3,)),
            dma((2,)),
        ],
        compiler_params=pltpu.CompilerParams(
            vmem_limit_bytes=63 * 1024 * 1024, collective_id=2, has_side_effects=True
        ),
        cost_estimate=cost(12 * tokens * width * units, 4 * tokens * width),
        name="rear",
    )(
        where, q, kv, lse, cosine, sine, gain.reshape(1, width), dn,
        n2, n_all, og, og_all, og_far, wg, wu, wd, wq, wk, wv, wo,
        resid, n1p, n1_all, att, att_all, out_part,
    )


def dot_plain(left, right):
    return jnp.dot(left, right, preferred_element_type=F32)


def dot_right(left, right):
    return lax.dot_general(left, right, (((1,), (1,)), ((), ())), preferred_element_type=F32)


def dot_left(left, right):
    return lax.dot_general(left, right, (((0,), (0,)), ((), ())), preferred_element_type=F32)


def normed(v, gain):
    return v * lax.rsqrt(jnp.mean(v * v, axis=-1, keepdims=True) + EPS) * gain


def norm_back(v, gain, grad):
    factor = lax.rsqrt(jnp.mean(v * v, axis=-1, keepdims=True) + EPS)
    unit = v * factor
    d_unit = grad * gain
    d_gain = jnp.sum(grad * unit, axis=0)
    d_v = factor * (d_unit - unit * jnp.mean(d_unit * unit, axis=-1, keepdims=True))
    return (d_v, d_gain)


def rotate(t, cosine, sine):
    half = t.shape[-1] // 2
    first, second = (t[..., :half], t[..., half:])
    return jnp.concatenate(
        [first * cosine - second * sine, second * cosine + first * sine], axis=-1
    )


def rotate_back(t, cosine, sine):
    half = t.shape[-1] // 2
    first, second = (t[..., :half], t[..., half:])
    return jnp.concatenate(
        [first * cosine + second * sine, second * cosine - first * sine], axis=-1
    )


def score_block(query5, key_all, allowed):
    scores = jnp.einsum(
        "scngd,slnd->sngcl", query5, key_all, preferred_element_type=F32
    ) * HD ** (-0.5)
    return jnp.where(allowed[:, None, None], scores, NEG)


def build(ndp, nctx, nten):
    def pull(v, axis, n, s):
        return lax.ppermute(v, axis, [((i + s) % n, i) for i in range(n)])

    def flip(v, axis, n, bit):
        return lax.ppermute(v, axis, [(i, i ^ bit) for i in range(n)])

    def tensor_sum(v):
        low = v.astype(BF)
        if nten == 2:
            return low.astype(F32) + flip(low, "tensor", 2, 1).astype(F32)
        return lax.psum(low, "tensor").astype(F32)

    def gather_dp(v):
        rows = v.shape[0] // nten
        part = lax.dynamic_slice_in_dim(v, lax.axis_index("tensor") * rows, rows, 0)
        pieces = [v]
        for s in range(1, ndp):
            got = pull(part, "dp", ndp, s)
            pieces.append(got)
            for t in range(1, nten):
                pieces.append(pull(got, "tensor", nten, t))
        return jnp.concatenate(pieces, axis=0)

    def ctx_sum(full):
        r = full.shape[0] // (ndp * nctx)
        me = lax.axis_index("ctx")
        work = full.reshape(ndp, nctx, r, full.shape[1])
        bit = 1
        while bit < nctx:
            left = work.shape[1] // 2
            work = work.reshape(ndp, left, 2, r, full.shape[1])
            mine = (me // bit) % 2
            keep = lax.dynamic_index_in_dim(work, mine, 2, keepdims=False)
            give = lax.dynamic_index_in_dim(work, 1 - mine, 2, keepdims=False)
            got = flip(give, "ctx", nctx, bit)
            work = (keep.astype(F32) + got.astype(F32)).astype(BF)
            bit *= 2
        return work.reshape(ndp, r, full.shape[1])

    def finish_slices(full):
        got = lax.all_to_all(ctx_sum(full), "dp", 0, 0, tiled=True)
        return jnp.swapaxes(got, 0, 1).reshape(got.shape[1], -1).astype(F32)

    def finish_sum(full):
        got = lax.all_to_all(ctx_sum(full), "dp", 0, 0, tiled=True)
        return jnp.sum(got.astype(F32), axis=0)

    def local(
        layer_input,
        output_grad,
        prefix,
        attn_gain,
        w_query,
        w_key,
        w_value,
        w_out,
        mlp_gain,
        w_gate,
        w_up,
        w_down,
    ):
        seqs, span, width = layer_input.shape
        q_heads = w_query.shape[1] // HD
        kv_heads = w_key.shape[1] // HD
        group = q_heads // kv_heads
        zi = lax.axis_index("dp")
        rows = layer_input.astype(F32).reshape(seqs * span, width)
        grad_low = output_grad.reshape(seqs * span, width)
        grad_rows = grad_low.astype(F32)
        grad_all = gather_dp(grad_low)

        first = lax.axis_index("ctx") * span
        position = (first + jnp.arange(span)).astype(F32)
        frequency = ROPE_BASE ** (-jnp.arange(HD // 2).astype(F32) * 2.0 / HD)
        angle = position[:, None] * frequency[None, :]
        cosine = jnp.cos(angle)[None, :, None, :]
        sine = jnp.sin(angle)[None, :, None, :]
        normed1 = normed(rows, attn_gain).astype(BF)
        query = rotate(
            dot_plain(normed1, w_query).reshape(seqs, span, q_heads, HD), cosine, sine
        ).astype(BF)
        keyed = rotate(
            dot_plain(normed1, w_key).reshape(seqs, span, kv_heads, HD), cosine, sine
        ).astype(BF)
        valued = dot_plain(normed1, w_value).astype(BF).reshape(seqs, span, kv_heads * HD)
        key_all, value_all = (
            lax.all_gather(
                keyed.reshape(seqs, span, kv_heads * HD), "ctx", axis=1, tiled=True
            ),
            lax.all_gather(valued, "ctx", axis=1, tiled=True),
        )
        length = key_all.shape[1]
        key_all = key_all.reshape(seqs, length, kv_heads, HD)
        value_all = value_all.reshape(seqs, length, kv_heads, HD)
        query5 = query.reshape(seqs, span, kv_heads, group, HD)
        query_pos = first + jnp.arange(span)
        key_pos = jnp.arange(length)
        allowed = (key_pos[None, None, :] <= query_pos[None, :, None]) | (
            key_pos[None, None, :] < prefix[:, None, None]
        )
        scores = score_block(query5, key_all, allowed)
        top = jnp.max(scores, axis=-1, keepdims=True)
        exponent = jnp.exp(scores - top)
        total = jnp.sum(exponent, axis=-1, keepdims=True)
        log_total = top + jnp.log(total)
        probs_low = (exponent / total).astype(BF)
        attended = jnp.einsum(
            "sngcl,slnd->scngd", probs_low, value_all, preferred_element_type=F32
        )
        attended = attended.astype(BF).reshape(seqs * span, q_heads * HD)
        resid = rows + tensor_sum(dot_plain(attended, w_out))
        normed2 = normed(resid, mlp_gain).astype(BF)
        normed2_all = gather_dp(normed2)
        gate = dot_plain(normed2, w_gate)
        up = dot_plain(normed2, w_up)
        act = (jax.nn.silu(gate) * up).astype(BF)

        def mlp_back(gate, up, d_act):
            sigmoid_gate = jax.nn.sigmoid(gate)
            d_gate_pre = (
                d_act * up * sigmoid_gate * (1.0 + gate * (1.0 - sigmoid_gate))
            ).astype(BF)
            d_up_pre = (d_act * gate * sigmoid_gate).astype(BF)
            return d_gate_pre, d_up_pre

        d_act = dot_right(grad_low, w_down)
        d_gate_pre, d_up_pre = mlp_back(gate, up, d_act)
        back_terms = dot_right(d_gate_pre, w_gate) + dot_right(d_up_pre, w_up)
        d_normed2 = tensor_sum(back_terms)
        output = (resid + tensor_sum(dot_plain(act, w_down))).astype(BF)
        output = output.reshape(seqs, span, width)

        units = w_gate.shape[1] // ndp
        wg = lax.dynamic_slice_in_dim(w_gate, zi * units, units, 1)
        wu = lax.dynamic_slice_in_dim(w_up, zi * units, units, 1)
        wd = lax.dynamic_slice_in_dim(w_down, zi * units, units, 0)
        gate_s = dot_plain(normed2_all, wg)
        up_s = dot_plain(normed2_all, wu)
        d_act_s = dot_right(grad_all, wd)
        act_s = (jax.nn.silu(gate_s) * up_s).astype(BF)
        d_gate_s, d_up_s = mlp_back(gate_s, up_s, d_act_s)
        s_down = finish_slices(dot_left(grad_all, act_s).astype(BF)).T
        s_gate = finish_slices(dot_left(normed2_all, d_gate_s).astype(BF))
        s_up = finish_slices(dot_left(normed2_all, d_up_s).astype(BF))

        d_resid_norm, g_mlp_gain = norm_back(resid, mlp_gain, d_normed2)
        d_resid = grad_rows + d_resid_norm
        d_resid_low = d_resid.astype(BF)
        s_out = finish_sum(dot_left(d_resid_low, attended).astype(BF)).T
        d_attended = dot_right(d_resid_low, w_out).astype(BF).reshape(query5.shape)
        scores = score_block(query5, key_all, allowed)
        probs = jnp.exp(scores - log_total)
        probs_low = probs.astype(BF)
        d_probs = jnp.einsum(
            "scngd,slnd->sngcl", d_attended, value_all, preferred_element_type=F32
        )
        delta = jnp.sum(probs * d_probs, axis=-1, keepdims=True)
        d_scores = (probs * (d_probs - delta)).astype(BF)
        scale = HD ** (-0.5)
        d_query = (
            jnp.einsum("sngcl,slnd->scngd", d_scores, key_all, preferred_element_type=F32) * scale
        )
        d_key_all = (
            jnp.einsum("sngcl,scngd->slnd", d_scores, query5, preferred_element_type=F32) * scale
        )
        d_value_all = jnp.einsum(
            "sngcl,scngd->slnd", probs_low, d_attended, preferred_element_type=F32
        )
        d_kv = jnp.concatenate(
            [
                d_key_all.reshape(length, kv_heads * HD).astype(BF),
                d_value_all.reshape(length, kv_heads * HD).astype(BF),
            ],
            axis=1,
        )
        d_kv = lax.psum_scatter(d_kv, "ctx", scatter_dimension=0, tiled=True).astype(F32)
        d_key, d_val = d_kv[:, : kv_heads * HD], d_kv[:, kv_heads * HD :]
        d_qp = (
            rotate_back(d_query.reshape(seqs, span, q_heads, HD), cosine, sine)
            .astype(BF)
            .reshape(seqs * span, q_heads * HD)
        )
        d_kp = (
            rotate_back(d_key.reshape(seqs, span, kv_heads, HD), cosine, sine)
            .astype(BF)
            .reshape(seqs * span, kv_heads * HD)
        )
        d_vp = d_val.astype(BF).reshape(seqs * span, kv_heads * HD)
        front_terms = dot_right(d_qp, w_query) + dot_right(d_kp, w_key) + dot_right(d_vp, w_value)
        d_normed1 = tensor_sum(front_terms)
        d_rows_norm, g_attn_gain = norm_back(rows, attn_gain, d_normed1)
        d_input = d_resid + d_rows_norm
        d_input = d_input.reshape(seqs, span, width)
        s_qkv = finish_sum(
            dot_left(normed1, jnp.concatenate([d_qp, d_kp, d_vp], axis=1)).astype(BF)
        )
        nq, nk = q_heads * HD, kv_heads * HD
        s_query, s_key, s_value = s_qkv[:, :nq], s_qkv[:, nq : nq + nk], s_qkv[:, nq + nk :]
        gains = jnp.stack([g_attn_gain, g_mlp_gain])
        gains = lax.psum_scatter(gains, ("dp", "ctx"), scatter_dimension=1, tiled=True)
        return (
            output,
            d_input,
            gains[0],
            s_query,
            s_key,
            s_value,
            s_out,
            gains[1],
            s_gate,
            s_up,
            s_down,
        )

    return local


def suits(ndp, nctx, nten, layer_input, output_grad, prefix, attn_gain, w_query, w_key, w_value, w_out, mlp_gain, w_gate, w_up, w_down):
    seqs, span, width = layer_input.shape
    return (
        seqs == 1
        and (ndp, nctx, nten) == (4, 4, 2)
        and (span, width) == (256, 2048)
        and (w_query.shape[1], w_key.shape[1], w_gate.shape[1]) == (1024, 256, 4096)
    )


def build_fast(ndp, nctx, nten):
    def local(
        layer_input,
        output_grad,
        prefix,
        attn_gain,
        w_query,
        w_key,
        w_value,
        w_out,
        mlp_gain,
        w_gate,
        w_up,
        w_down,
    ):
        seqs, span, width = layer_input.shape
        kvw, nq = w_key.shape[1], w_query.shape[1]
        low = layer_input.reshape(span, width)
        grad_low = output_grad.reshape(span, width)
        first = lax.axis_index("ctx") * span
        where = jnp.stack([first, prefix[0]]).astype(jnp.int32)
        cosine, sine = rope_tables(first, span)
        n1p, query, kv, attended, lse, resid, normed2, grad_all = front(
            where, low, attn_gain, w_query, w_key, w_value, w_out, cosine, sine, mlp_gain, grad_low, ndp, nctx
        )
        out_part, dn, n_all, n1_all, att_all, grad_far = middle(
            normed2, grad_low, w_gate, w_up, w_down, n1p, attended, grad_all, ndp, nctx
        )
        down_z, gate_z, up_z, att_z, front_part, front_got, out_got, d_resid, g_mlp_gain = rear(
            where, query, kv, lse, cosine, sine, mlp_gain, dn, normed2, n_all, grad_low, grad_all, grad_far,
            w_gate, w_up, w_down, w_query, w_key, w_value, w_out, resid, n1p, n1_all, attended, att_all,
            out_part, ndp, nctx,
        )
        output = resid + (out_part.astype(F32) + out_got.astype(F32))
        output = output.astype(BF).reshape(seqs, span, width)
        s_down = jnp.swapaxes(down_z, 1, 2).reshape(w_down.shape[0], -1).astype(F32)
        s_gate, s_up = gate_z.astype(F32), up_z.astype(F32)
        s_att = jnp.sum(att_z.astype(F32), axis=0)
        s_query, s_key = s_att[:, :nq], s_att[:, nq : nq + kvw]
        s_value, s_out = s_att[:, nq + kvw : nq + 2 * kvw], s_att[:, nq + 2 * kvw :].T
        d_normed1 = front_part.astype(F32) + front_got.astype(F32)
        d_rows_norm, g_attn_gain = norm_back(low.astype(F32), attn_gain, d_normed1)
        d_input = (d_resid + d_rows_norm).reshape(seqs, span, width)
        gains = jnp.stack([g_attn_gain, g_mlp_gain[0]])
        gains = jnp.swapaxes(gains.reshape(2, ndp * nctx, -1), 0, 1)
        gains = lax.all_to_all(gains, ("dp", "ctx"), 0, 0, tiled=True)
        gains = jnp.sum(gains, axis=0)
        return (
            output,
            d_input,
            gains[0],
            s_query,
            s_key,
            s_value,
            s_out,
            gains[1],
            s_gate,
            s_up,
            s_down,
        )

    return local


def solution(mesh):
    sizes = mesh.shape["dp"], mesh.shape["ctx"], mesh.shape["tensor"]
    plain, fast = build(*sizes), build_fast(*sizes)

    def local(*args):
        return (fast if suits(*sizes, *args) else plain)(*args)

    return jax.shard_map(
        local,
        mesh=mesh,
        in_specs=(
            P("dp", "ctx", None),
            P("dp", "ctx", None),
            P("dp"),
            P(),
            P(None, "tensor"),
            P(None, "tensor"),
            P(None, "tensor"),
            P("tensor", None),
            P(),
            P(None, "tensor"),
            P(None, "tensor"),
            P("tensor", None),
        ),
        out_specs=(
            P("dp", "ctx", None),
            P("dp", "ctx", None),
            P(("dp", "ctx")),
            P(("dp", "ctx"), "tensor"),
            P(("dp", "ctx"), "tensor"),
            P(("dp", "ctx"), "tensor"),
            P("tensor", ("dp", "ctx")),
            P(("dp", "ctx")),
            P(("dp", "ctx"), "tensor"),
            P(("dp", "ctx"), "tensor"),
            P("tensor", ("dp", "ctx")),
        ),
        check_vma=False,
    )
```

```python
import functools
import jax
import jax.numpy as jnp
from jax import lax
from jax.experimental import pallas as pl
from jax.experimental.pallas import tpu as pltpu
from jax.sharding import PartitionSpec as P

HD = 64
EPS = 1e-05
ROPE_BASE = 500000.0
NEG = -1e30
BF = jnp.bfloat16
F32 = jnp.float32
VMEM_MOST = 60 * 1024 * 1024


def cost(flops, nbytes, trans=0):
    return pl.CostEstimate(flops=int(flops), bytes_accessed=int(nbytes), transcendentals=int(trans))


def nt(a, b):
    return lax.dot_general(a, b, (((1,), (1,)), ((), ())), preferred_element_type=F32)


def tn(a, b):
    return lax.dot_general(a, b, (((0,), (0,)), ((), ())), preferred_element_type=F32)


def nn(a, b):
    return jnp.dot(a, b, preferred_element_type=F32)


def swap_halves(t):
    lane = lax.broadcasted_iota(jnp.int32, t.shape, 1) % HD
    n = t.shape[1]
    return jnp.where(
        lane < HD // 2, pltpu.roll(t, n - HD // 2, 1), pltpu.roll(t, HD // 2, 1)
    )


def rope_tables(first, span):
    position = (first + jnp.arange(span)).astype(F32)
    frequency = ROPE_BASE ** (-jnp.arange(HD // 2).astype(F32) * 2.0 / HD)
    angle = position[:, None] * frequency[None, :]
    cosine, sine = jnp.cos(angle), jnp.sin(angle)
    return (
        jnp.concatenate([cosine, cosine, cosine, cosine], axis=1),
        jnp.concatenate([-sine, sine, -sine, sine], axis=1),
    )


def mask_bias(first, prefix, length, span):
    key = lax.broadcasted_iota(jnp.int32, (length, span), 0)
    query = lax.broadcasted_iota(jnp.int32, (length, span), 1) + first
    return jnp.where((key <= query) | (key < prefix), 0.0, NEG).astype(F32)


def gate_parts(gate, up, d_act):
    sig = 1.0 / (1.0 + jnp.exp(-gate))
    silu = gate * sig
    return (
        (silu * up).astype(BF),
        (d_act * up * (sig + silu * (1.0 - sig))).astype(BF),
        (d_act * silu).astype(BF),
    )


MESH = pl.DeviceIdType.MESH


def remote(src, dst, send, recv, to):
    return pltpu.make_async_remote_copy(
        src_ref=src, dst_ref=dst, send_sem=send, recv_sem=recv, device_id=to, device_id_type=MESH
    )


def enter(devices):
    barrier = pltpu.get_barrier_semaphore()
    for to in devices:
        pl.semaphore_signal(barrier, inc=1, device_id=to, device_id_type=MESH)
    pl.semaphore_wait(barrier, len(devices))


def around(z, ndp):
    return [{"dp": lax.rem(z + 1, ndp)}, {"dp": lax.rem(z + ndp - 1, ndp)}]


def mates(me, y):
    return [{"ctx": me ^ 1}, {"ctx": me ^ 2}, {"ctx": me ^ 3}, {"tensor": 1 - y}]


class Relay:
    def __init__(self, z, ndp, hop, own, blocks, sems):
        self.z, self.ndp, self.hop = z, ndp, hop
        self.own, self.blocks, self.sems = own, blocks, sems

    def copy(self, way, block, to):
        src = self.own if self.hop == 1 else self.blocks.at[block]
        at = 0 if way > 0 else 1
        return remote(
            src, self.blocks.at[block], self.sems.at[0, at], self.sems.at[1, at], {"dp": to}
        )

    def each(self, act, incoming):
        z, hop = self.z, self.hop
        for way in (1, -1):
            if incoming:
                block = z - way * hop
                ok = block >= 0 if way > 0 else block < self.ndp
            else:
                block = z - way * (hop - 1)
                ok = (block >= 0) & (z < self.ndp - 1) if way > 0 else (block < self.ndp) & (z > 0)

            @pl.when(ok)
            def _(way=way, block=block):
                act(self.copy(way, block, z if incoming else z + way))

    def start(self):
        self.each(lambda c: c.start(), False)

    def wait_recv(self):
        self.each(lambda c: c.wait_recv(), True)

    def wait_send(self):
        self.each(lambda c: c.wait_send(), False)


def rope_parts(t, cosine, sine):
    pieces = []
    for i in range(t.shape[1] // 128):
        part = t[:, 128 * i : 128 * (i + 1)]
        pieces.append((part * cosine + swap_halves(part) * sine).astype(BF))
    return pieces


def front_kernel(
    ndp, nctx, group,
    where_ref, x_ref, gain1_ref, wq_hbm, wk_hbm, wv_hbm, wo_hbm, cos_ref, sin_ref, gain2_ref, og_hbm,
    n1_ref, q_ref, kv_out, att_ref, lse_ref, resid_ref, n2_ref, og_all,
    n1_buf, wq, wk, wv, wo, kv, bias_ref, part, part_got,
    w_sem, kv_sem, kv_out_sem, part_sem, z_sem,
):
    z, me, y = lax.axis_index("dp"), lax.axis_index("ctx"), lax.axis_index("tensor")
    span, width = x_ref.shape
    length = kv.shape[0]
    kvw = wk.shape[1]
    loads = [
        pltpu.make_async_copy(src, dst, w_sem.at[i])
        for i, (src, dst) in enumerate(((wk_hbm, wk), (wv_hbm, wv), (wq_hbm, wq), (wo_hbm, wo)))
    ]
    for copy in loads:
        copy.start()
    hop1 = Relay(z, ndp, 1, og_hbm, og_all, z_sem.at[0])
    hop2 = Relay(z, ndp, 2, og_hbm, og_all, z_sem.at[1])
    enter(around(z, ndp) + mates(me, y))
    hop1.start()
    v = x_ref[...].astype(F32)
    factor = lax.rsqrt(jnp.mean(v * v, axis=-1, keepdims=True) + EPS)
    n1_buf[...] = (v * factor * gain1_ref[...]).astype(BF)
    cosine, sine = cos_ref[...], sin_ref[...]
    mine = pl.ds(pl.multiple_of(me * span, span), span)
    loads[0].wait()
    for i, piece in enumerate(rope_parts(nn(n1_buf[...], wk[...]), cosine, sine)):
        kv[mine, 128 * i : 128 * (i + 1)] = piece
    loads[1].wait()
    kv[mine, kvw:] = nn(n1_buf[...], wv[...]).astype(BF)

    def kv_copy(which, block, mask):
        rows = pl.ds(pl.multiple_of(block * span, span), span)
        return remote(kv.at[rows], kv.at[rows], kv_sem.at[0, which], kv_sem.at[1, which], {"ctx": me ^ mask})

    to_x = kv_copy(0, me, 2)
    to_core = kv_copy(1, me, 1)
    onward = kv_copy(2, me ^ 2, 1)
    to_x.start()
    to_core.start()
    loads[2].wait()
    for i, piece in enumerate(rope_parts(nn(n1_buf[...], wq[...]), cosine, sine)):
        q_ref[:, 128 * i : 128 * (i + 1)] = piece
    part_width = width // (ndp * nctx)
    for p in range(nctx):
        for b in range(ndp):
            at = (b * nctx + p) * part_width
            n1_ref[p, :, b * part_width : (b + 1) * part_width] = n1_buf[:, at : at + part_width]
    bias_ref[...] = mask_bias(where_ref[0], where_ref[1], length, span)
    to_x.wait_recv()
    onward.start()
    to_core.wait_recv()
    onward.wait_recv()
    to_x.wait_send()
    to_core.wait_send()
    onward.wait_send()
    save_kv = pltpu.make_async_copy(kv, kv_out, kv_out_sem)
    save_kv.start()

    wide = 128 * group
    heads = wide // HD

    @pl.loop(0, kvw // 128)
    def _(j):
        lanes = pl.ds(pl.multiple_of(j * wide, 128), wide)
        queries = q_ref[:, lanes] * jnp.asarray(HD**-0.5, BF)
        keys = kv[:, pl.ds(pl.multiple_of(j * 128, 128), 128)]
        values = kv[:, pl.ds(pl.multiple_of(kvw + j * 128, 128), 128)]
        rows, outs = [], []
        for h in range(heads):
            at = slice(HD * (h // group), HD * (h // group + 1))
            scores = nt(keys[:, at], queries[:, HD * h : HD * (h + 1)]) + bias_ref[...]
            top = jnp.max(scores, axis=0, keepdims=True)
            exponent = jnp.exp(scores - top)
            total = jnp.sum(exponent, axis=0, keepdims=True)
            rows.append(top + jnp.log(total))
            outs.append(tn(values[:, at], exponent.astype(BF)) / total)
            if h % 2:
                both = jnp.concatenate(outs, axis=0).T.astype(BF)
                att_ref[:, pl.ds(pl.multiple_of(j * wide + HD * (h - 1), 128), 128)] = both
                outs = []
        lse_ref[pl.ds(pl.multiple_of(j * heads, heads), heads), :] = jnp.concatenate(rows, axis=0)

    hop1.wait_recv()
    hop2.start()
    save_kv.wait()
    loads[3].wait()
    count, _, cols = part.shape
    copies = [
        remote(part.at[c], part_got.at[c], part_sem.at[0, c], part_sem.at[1, c], {"tensor": 1 - y})
        for c in range(count)
    ]
    for c in range(count):
        part[c] = nn(att_ref[...], wo[:, c * cols : (c + 1) * cols]).astype(BF)
        copies[c].start()
    square = jnp.zeros((span, 1), F32)
    for c in range(count):
        at = slice(c * cols, (c + 1) * cols)
        copies[c].wait_recv()
        r = x_ref[:, at].astype(F32) + (part[c].astype(F32) + part_got[c].astype(F32))
        resid_ref[:, at] = r
        square += jnp.sum(r * r, axis=-1, keepdims=True)
    factor = lax.rsqrt(square / width + EPS)
    for c in range(count):
        at = slice(c * cols, (c + 1) * cols)
        n2_ref[:, at] = (resid_ref[:, at] * factor * gain2_ref[:, at]).astype(BF)
    for copy in copies:
        copy.wait_send()
    hop1.wait_send()
    hop2.wait_recv()
    hop2.wait_send()


HBM_SPEC = pl.BlockSpec(memory_space=pl.ANY)
VMEM_SPEC = pl.BlockSpec(memory_space=pltpu.VMEM)
SMEM_SPEC = pl.BlockSpec(memory_space=pltpu.SMEM)


def own(number):
    return pltpu.CompilerParams(
        vmem_limit_bytes=VMEM_MOST, collective_id=number, has_side_effects=True
    )


def front(where, x, gain1, wq, wk, wv, wo, cosine, sine, gain2, og, ndp, nctx):
    span, width = x.shape
    qw, kvw = wq.shape[1], wk.shape[1]
    group = qw // kvw
    length = span * nctx
    chunks = 4
    dma = pltpu.SemaphoreType.DMA
    return pl.pallas_call(
        functools.partial(front_kernel, ndp, nctx, group),
        in_specs=[SMEM_SPEC, VMEM_SPEC, VMEM_SPEC] + [HBM_SPEC] * 4 + [VMEM_SPEC] * 3 + [HBM_SPEC],
        out_specs=[VMEM_SPEC, VMEM_SPEC, HBM_SPEC] + [VMEM_SPEC] * 4 + [HBM_SPEC],
        out_shape=[
            jax.ShapeDtypeStruct((nctx, span, width // nctx), BF),
            jax.ShapeDtypeStruct((span, qw), BF),
            jax.ShapeDtypeStruct((length, 2 * kvw), BF),
            jax.ShapeDtypeStruct((span, qw), BF),
            jax.ShapeDtypeStruct((qw // HD, span), F32),
            jax.ShapeDtypeStruct((span, width), F32),
            jax.ShapeDtypeStruct((span, width), BF),
            jax.ShapeDtypeStruct((ndp, span, width), BF),
        ],
        scratch_shapes=[
            pltpu.VMEM((span, width), BF),
            pltpu.VMEM((width, qw), BF),
            pltpu.VMEM((width, kvw), BF),
            pltpu.VMEM((width, kvw), BF),
            pltpu.VMEM((qw, width), BF),
            pltpu.VMEM((length, 2 * kvw), BF),
            pltpu.VMEM((length, span), F32),
            pltpu.VMEM((chunks, span, width // chunks), BF),
            pltpu.VMEM((chunks, span, width // chunks), BF),
            dma((4,)),
            dma((2, 3)),
            dma,
            dma((2, chunks)),
            dma((2, 2, 2)),
        ],
        compiler_params=own(0),
        cost_estimate=cost(2 * span * width * (2 * qw + 2 * kvw), 4 * width * (qw + kvw)),
        name="front",
    )(where, x, gain1.reshape(1, width), wq, wk, wv, wo, cosine, sine, gain2.reshape(1, width), og)


def halves(y, span):
    return pl.ds(pl.multiple_of(y * (span // 2), span // 2), span // 2)


class Far:
    def __init__(self, z, y, blocks, far, sems):
        rows = halves(y, far.shape[0])
        block = jnp.where(z == 1, 3, 0)
        to = jnp.where(z == 1, 0, 3)
        self.over = remote(blocks.at[block, rows], far.at[rows], sems.at[0], sems.at[1], {"dp": to})
        self.gives = (z == 1) | (z == 2)
        self.takes = (z == 0) | (z == 3)

    def start(self):
        pl.when(self.gives)(lambda: self.over.start())

    def finish(self):
        pl.when(self.takes)(lambda: self.over.wait_recv())
        pl.when(self.gives)(lambda: self.over.wait_send())


class Gather:
    def __init__(self, z, y, ndp, own, blocks, sems, swaps):
        self.z, self.y, self.ndp = z, y, ndp
        self.own, self.blocks, self.sems, self.swaps = own, blocks, sems, swaps
        self.rows = halves(y, own.shape[0])

    def over(self, way, hop, block, to):
        src = self.own.at[self.rows] if hop == 1 else self.blocks.at[block, self.rows]
        at = 0 if way > 0 else 1
        return remote(
            src, self.blocks.at[block, self.rows],
            self.sems.at[hop - 1, 0, at], self.sems.at[hop - 1, 1, at], {"dp": to},
        )

    def swap(self, way, hop, block):
        at = 0 if way > 0 else 1
        part = self.blocks.at[block, self.rows]
        return remote(
            part, part, self.swaps.at[hop - 1, 0, at], self.swaps.at[hop - 1, 1, at],
            {"tensor": 1 - self.y},
        )

    def comes(self, way, hop):
        block = self.z - way * hop
        return block, (block >= 0 if way > 0 else block < self.ndp)

    def leaves(self, way, hop):
        block = self.z - way * (hop - 1)
        if way > 0:
            return block, (block >= 0) & (self.z < self.ndp - 1)
        return block, (block < self.ndp) & (self.z > 0)

    def send(self, hop):
        for way in (1, -1):
            block, ok = self.leaves(way, hop)

            @pl.when(ok)
            def _(way=way, block=block):
                self.over(way, hop, block, self.z + way).start()

    def step(self, hop):
        for way in (1, -1):
            block, ok = self.comes(way, hop)

            @pl.when(ok)
            def _(way=way, block=block):
                self.over(way, hop, block, self.z).wait_recv()
                self.swap(way, hop, block).start()

        if hop < self.ndp - 1:
            self.send(hop + 1)

    def finish(self):
        for hop in range(1, self.ndp):
            for way in (1, -1):
                block, ok = self.comes(way, hop)

                @pl.when(ok)
                def _(way=way, block=block, hop=hop):
                    self.swap(way, hop, block).wait()

                block, ok = self.leaves(way, hop)

                @pl.when(ok)
                def _(way=way, block=block, hop=hop):
                    self.over(way, hop, block, self.z + way).wait_send()


def middle_kernel(
    ndp, nctx,
    n_ref, g_ref, wg_ref, wu_ref, wd_ref, n_hbm, n1_hbm, att_hbm, g_near,
    o_ref, dn_ref, n_all, n1_all, att_all, g_far,
    o_acc, dn_acc,
    z_sem, swap_sem, n1_sem, att_sem, far_sem,
):
    z, me, y = lax.axis_index("dp"), lax.axis_index("ctx"), lax.axis_index("tensor")
    j = pl.program_id(0)
    last = pl.num_programs(0) - 1
    gather = Gather(z, y, ndp, n_hbm, n_all, z_sem, swap_sem)
    far = Far(z, y, g_near, g_far, far_sem)
    spreads = []
    for m in range(1, nctx):
        spreads.append(
            remote(n1_hbm.at[me ^ m], n1_all.at[me], n1_sem.at[0, m], n1_sem.at[1, m], {"ctx": me ^ m})
        )
        spreads.append(
            remote(att_hbm, att_all.at[me], att_sem.at[0, m], att_sem.at[1, m], {"ctx": me ^ m})
        )

    @pl.when(j == 0)
    def _():
        enter(around(z, ndp) + mates(me, y))
        gather.send(1)
        for copy in spreads:
            copy.start()

    normed2, grad = n_ref[...], g_ref[...]
    gate = nn(normed2, wg_ref[...])
    up = nn(normed2, wu_ref[...])
    d_act = nt(grad, wd_ref[...])
    act, d_gate, d_up = gate_parts(gate, up, d_act)

    @pl.when(j == 0)
    def _():
        o_acc[...] = nn(act, wd_ref[...])
        dn_acc[...] = nt(d_gate, wg_ref[...]) + nt(d_up, wu_ref[...])

    @pl.when(j > 0)
    def _():
        o_acc[...] += nn(act, wd_ref[...])
        dn_acc[...] += nt(d_gate, wg_ref[...]) + nt(d_up, wu_ref[...])

    @pl.when(j == 3)
    def _():
        gather.step(1)

    @pl.when(j == 5)
    def _():
        gather.step(2)
        far.start()

    @pl.when(j == last)
    def _():
        gather.step(3)
        o_ref[...] = o_acc[...].astype(BF)
        dn_ref[...] = dn_acc[...].astype(BF)
        for copy in spreads:
            copy.wait()
        far.finish()
        gather.finish()


def middle(n2, og, wg, wu, wd, n1p, att, og_all, ndp, nctx, step=512):
    span, width = n2.shape
    units = wg.shape[1]
    dma = pltpu.SemaphoreType.DMA
    whole = pl.BlockSpec((span, width), lambda j: (0, 0))
    cols = pl.BlockSpec((width, step), lambda j: (0, j))
    return pl.pallas_call(
        functools.partial(middle_kernel, ndp, nctx),
        grid=(units // step,),
        in_specs=[
            whole, whole, cols, cols, pl.BlockSpec((step, width), lambda j: (j, 0)),
            HBM_SPEC, HBM_SPEC, HBM_SPEC, HBM_SPEC,
        ],
        out_specs=[whole, whole, HBM_SPEC, HBM_SPEC, HBM_SPEC, HBM_SPEC],
        out_shape=[
            jax.ShapeDtypeStruct((span, width), BF),
            jax.ShapeDtypeStruct((span, width), BF),
            jax.ShapeDtypeStruct((ndp, span, width), BF),
            jax.ShapeDtypeStruct((nctx, span, width // nctx), BF),
            jax.ShapeDtypeStruct((nctx,) + att.shape, BF),
            jax.ShapeDtypeStruct((span, width), BF),
        ],
        scratch_shapes=[
            pltpu.VMEM((span, width), F32),
            pltpu.VMEM((span, width), F32),
            dma((ndp - 1, 2, 2)),
            dma((ndp - 1, 2, 2)),
            dma((2, nctx)),
            dma((2, nctx)),
            dma((2,)),
        ],
        compiler_params=own(1),
        cost_estimate=cost(12 * span * width * units, 6 * width * units),
        name="middle",
    )(n2, og, wg, wu, wd, n2, n1p, att, og_all)


def rear_kernel(
    ndp, nctx, group, chunk, rows,
    where_ref, q_ref, kv_ref, lse_ref, cos_ref, sin_ref, gain_ref, gain1_ref, dn_ref,
    n_own, n_near, g_own, g_near, g_far, wg_hbm, wu_hbm, wd_hbm, wq_hbm, wk_hbm, wv_hbm, wo_hbm,
    resid_hbm, n1_own, n1_near, att_own, att_near, out_hbm, x_hbm,
    down_z, gate_z, up_z, att_z, front_got, out_got, dr_out, output, input_grad, gains_ref,
    n_all, g_all, acts, wg_buf, wu_buf, wd_buf, give, take, x_give, x_take, x_keep,
    left1, left2, right1, right2, prod, low, d_att, bias_ref, dkv, land, acc,
    gain_grad_ref, gains, gains_x, gains_z,
    in_sem, l_sem, w_sem, back_sem, dn_sem, low_sem, dkv_sem, r_sem, core_sem, x_sem, zz_sem, z_own,
    att_sem, y_sem, save_sem, far_sem, tail_sem, gx_sem, gz_sem,
):
    z, me, y = lax.axis_index("dp"), lax.axis_index("ctx"), lax.axis_index("tensor")
    tokens, width = n_all.shape
    span, qw = q_ref.shape
    length = kv_ref.shape[0]
    kvw = kv_ref.shape[1] // 2
    units = acts.shape[1]
    core, xpos = me % 2, me // 2
    part = width // (ndp * nctx)
    start = z * units
    peers = [{"dp": lax.rem(z + s, ndp)} for s in range(1, ndp)]
    mate = {"tensor": 1 - y}
    mine = pl.ds(pl.multiple_of(me * span, span), span)
    cross = pl.ds(pl.multiple_of((me ^ 2) * span, span), span)

    def block_load(r, own_ref, near, dst, sem):
        block = lax.rem(jnp.where(z < ndp // 2, z + r, z + ndp - r), ndp)
        at = dst.at[pl.ds(r * span, span)]
        return pltpu.make_async_copy(own_ref if r == 0 else near.at[block], at, sem)

    def go(copies):
        for ok, copy in copies:
            if ok is None:
                copy.start()
            else:
                pl.when(ok)(lambda copy=copy: copy.start())

    def done(copies):
        copies[0][1].wait()

    n_loads = [block_load(r, n_own, n_near, n_all, in_sem.at[0, r]) for r in range(ndp)]
    g_loads = [block_load(r, g_own, g_near, g_all, in_sem.at[1, r]) for r in range(ndp)]
    end = (z == 0) | (z == ndp - 1)
    tail = ndp - 1
    half_rows = halves(y, span)
    half_at = g_all.at[pl.ds(pl.multiple_of(tail * span + y * (span // 2), span // 2), span // 2)]
    half_load = pltpu.make_async_copy(g_far.at[half_rows], half_at, in_sem.at[1, tail])
    half_swap = remote(g_far.at[half_rows], half_at, far_sem.at[0], far_sem.at[1], mate)

    def ctx_load(p, own_ref, near, dst, sem):
        at = dst.at[pl.ds(p * span, span)]
        here = me == p
        return [
            (here, pltpu.make_async_copy(own_ref, at, sem)),
            (jnp.logical_not(here), pltpu.make_async_copy(near.at[p], at, sem)),
        ]

    l_loads = []
    for p in range(nctx):
        l_loads.append(ctx_load(p, att_own, att_near, right2, l_sem.at[0, p]))
        l_loads.append(ctx_load(p, n1_own.at[p], n1_near, left1, l_sem.at[1, p]))

    def weights(j, slot):
        at = pl.multiple_of(start + j * chunk, chunk)
        return (
            pltpu.make_async_copy(wg_hbm.at[:, pl.ds(at, chunk)], wg_buf.at[slot], w_sem.at[slot, 0]),
            pltpu.make_async_copy(wu_hbm.at[:, pl.ds(at, chunk)], wu_buf.at[slot], w_sem.at[slot, 1]),
            pltpu.make_async_copy(wd_hbm.at[pl.ds(at, chunk)], wd_buf.at[slot], w_sem.at[slot, 2]),
        )

    for copy in n_loads + g_loads[:tail]:
        copy.start()
    pl.when(end)(lambda: half_load.start())
    pl.when(jnp.logical_not(end))(lambda: g_loads[tail].start())
    for copy in weights(0, 0):
        copy.start()
    resid_load = pltpu.make_async_copy(resid_hbm, acc, save_sem.at[0])
    resid_load.start()
    for copies in l_loads:
        go(copies)
    dn_got = [x_take.at[2, pl.ds(h * span, span)] for h in range(2)]
    half = width // 2
    dn_copies = [
        remote(
            dn_ref.at[:, pl.ds(h * half, half)], dn_got[h], dn_sem.at[0, h], dn_sem.at[1, h], mate
        )
        for h in range(2)
    ]
    enter(peers + mates(me, y))
    pl.when(end)(lambda: half_swap.start())
    for copy in dn_copies:
        copy.start()

    count = units // chunk
    for copy in n_loads + g_loads[:tail]:
        copy.wait()

    @pl.loop(0, count)
    def _(j):
        slot = j % 2
        for copy in weights(j, slot):
            copy.wait()

        @pl.when(j + 1 < count)
        def _():
            for copy in weights(j + 1, 1 - slot):
                copy.start()

        cols = pl.ds(pl.multiple_of(j * chunk, chunk), chunk)

        @pl.loop(0, tokens // rows)
        def _(i):
            @pl.when((j == 0) & (i == tail))
            def _():
                pl.when(jnp.logical_not(end))(lambda: g_loads[tail].wait())

                @pl.when(end)
                def _():
                    half_load.wait()
                    half_swap.wait()

            some = pl.ds(pl.multiple_of(i * rows, rows), rows)
            gate = nn(n_all[some], wg_buf[slot])
            up = nn(n_all[some], wu_buf[slot])
            d_act = nt(g_all[some], wd_buf[slot])
            for w, value in enumerate(gate_parts(gate, up, d_act)):
                acts[pl.ds(pl.multiple_of(w * tokens + i * rows, rows), rows), cols] = value

    lefts = (g_all, n_all, n_all)

    def product(w, x, c):
        left = lefts[w]
        block = jnp.concatenate(
            [
                left[:, pl.ds(pl.multiple_of((k * nctx + x * 2 + c) * part, part), part)]
                for k in range(ndp)
            ],
            axis=1,
        )
        return tn(block, acts[w * tokens : (w + 1) * tokens])

    core_copies = [
        remote(give.at[w % 2], take.at[w % 2], core_sem.at[0, w], core_sem.at[1, w], {"ctx": me ^ 1})
        for w in range(3)
    ]
    x_copies = [
        remote(x_give.at[w], x_take.at[w], x_sem.at[0, w], x_sem.at[1, w], {"ctx": me ^ 2})
        for w in range(3)
    ]

    def hand(w):
        give[w % 2, 0] = product(w, 1 - xpos, 1 - core).astype(BF)
        give[w % 2, 1] = product(w, xpos, 1 - core).astype(BF)
        core_copies[w].start()

    def keep(w):
        there = product(w, 1 - xpos, core)
        core_copies[w].wait()
        x_give[w] = (there + take[w % 2, 0].astype(F32)).astype(BF)
        if w < 2:
            x_copies[w].start()
        x_keep[w] = (product(w, xpos, core) + take[w % 2, 1].astype(F32)).astype(BF)

    hand(0)
    keep(0)
    hand(1)
    keep(1)
    hand(2)
    keep(2)

    def z_rows(k):
        return pl.ds(pl.multiple_of(k * part, part), part)

    z_units = pl.ds(pl.multiple_of(start, units), units)

    def landing(w):
        return down_z.at[z] if w == 0 else (gate_z, up_z)[w - 1].at[:, z_units]

    def z_copies(w):
        return [
            remote(
                x_keep.at[w, z_rows(lax.rem(z + s, ndp))],
                landing(w),
                zz_sem.at[0, w, s],
                zz_sem.at[1, w, s],
                peers[s - 1],
            )
            for s in range(1, ndp)
        ]

    def z_own_copy(w):
        return pltpu.make_async_copy(x_keep.at[w, z_rows(z)], landing(w), z_own.at[w])

    def serve(w):
        x_copies[w].wait()
        x_keep[w] = (x_keep[w].astype(F32) + x_take[w].astype(F32)).astype(BF)
        for copy in z_copies(w):
            copy.start()
        z_own_copy(w).start()

    wo, wq = n_all, acts.at[pl.ds(0, width)]
    wk, wv = wg_buf.at[0], wu_buf.at[0]
    loads = [
        pltpu.make_async_copy(src, dst, back_sem.at[i])
        for i, (src, dst) in enumerate(((wo_hbm, wo), (wq_hbm, wq), (wk_hbm, wk), (wv_hbm, wv)))
    ]
    for copy in loads:
        copy.start()
    bias_ref[...] = mask_bias(where_ref[0], where_ref[1], length, span)
    resid_load.wait()
    v = acc[...]
    factor = lax.rsqrt(jnp.mean(v * v, axis=-1, keepdims=True) + EPS)
    for copy in dn_copies:
        copy.wait()
    y_out = remote(out_hbm, out_got, y_sem.at[0, 1], y_sem.at[1, 1], mate)
    y_out.start()
    cols = width // 4

    def dn_part(c):
        return dn_got[c // 2][:, (c % 2) * cols : (c % 2 + 1) * cols]

    dots = jnp.zeros((span, 1), F32)
    for c in range(4):
        at = slice(c * cols, (c + 1) * cols)
        unit = acc[:, at] * factor
        back = dn_ref[:, at].astype(F32) + dn_part(c).astype(F32)
        term = back * unit
        gain_grad_ref[:, at] = jnp.sum(term, axis=0, keepdims=True)
        dots += jnp.sum(term * gain_ref[:, at], axis=-1, keepdims=True)
    dots = dots / width
    for c in range(4):
        at = slice(c * cols, (c + 1) * cols)
        unit = acc[:, at] * factor
        back = dn_ref[:, at].astype(F32) + dn_part(c).astype(F32)
        total = g_all[:span, at].astype(F32) + factor * (back * gain_ref[:, at] - unit * dots)
        acc[:, at] = total
        low[:, at] = total.astype(BF)
    dr_save = pltpu.make_async_copy(acc, dr_out, save_sem.at[1])
    dr_save.start()

    spread = width // nctx

    def low_rows(p):
        return pl.ds(pl.multiple_of(p // 2 * span, span), span)

    def low_cols(p):
        return pl.ds(pl.multiple_of(p % 2 * spread, spread), spread)

    for p in range(nctx):
        for b in range(ndp):
            at = (b * nctx + p) * part
            to = p % 2 * spread + b * part
            give[0, 0, p // 2 * span : (p // 2 + 1) * span, to : to + part] = low[:, at : at + part]
    spreads = [
        remote(
            give.at[0, 0, low_rows(me ^ m), low_cols(me ^ m)],
            left2.at[mine],
            low_sem.at[0, m],
            low_sem.at[1, m],
            {"ctx": me ^ m},
        )
        for m in range(1, nctx)
    ]
    for copy in spreads:
        copy.start()
    left2[mine, :] = give[0, 0, low_rows(me), low_cols(me)]
    loads[0].wait()
    d_att[...] = nt(low[...], wo[...]).astype(BF)
    wide = 128 * group
    heads = wide // HD
    blocks = kvw // 128
    scale = jnp.asarray(HD**-0.5, BF)

    def share(j, m):
        some = pl.ds(pl.multiple_of((me ^ m) * span, span), span)
        return remote(
            dkv.at[j, some], land.at[j, m], dkv_sem.at[0, j, m], dkv_sem.at[1, j, m], {"ctx": me ^ m}
        )

    @pl.loop(0, blocks)
    def _(j):
        lanes = pl.ds(pl.multiple_of(j * wide, 128), wide)
        queries = q_ref[:, lanes] * scale
        grads = d_att[:, lanes]
        keys = kv_ref[:, pl.ds(pl.multiple_of(j * 128, 128), 128)]
        values = kv_ref[:, pl.ds(pl.multiple_of(kvw + j * 128, 128), 128)]
        lse = lse_ref[pl.ds(pl.multiple_of(j * heads, heads), heads), :]
        pair = []
        for h in range(heads):
            at = slice(HD * (h // group), HD * (h // group + 1))
            key, value = keys[:, at], values[:, at]
            query = queries[:, HD * h : HD * (h + 1)]
            grad = grads[:, HD * h : HD * (h + 1)]
            probs = jnp.exp(nt(key, query) + (bias_ref[...] - lse[h : h + 1, :]))
            d_probs = nt(value, grad)
            delta = jnp.sum(probs * d_probs, axis=0, keepdims=True)
            d_scores = (probs * (d_probs - delta)).astype(BF)
            d_value = nn(probs.astype(BF), grad)
            d_key = nn(d_scores, query)
            if h % group == 0:
                sum_key, sum_value = d_key, d_value
            else:
                sum_key, sum_value = sum_key + d_key, sum_value + d_value
            if h % group == group - 1:
                dkv[j, :, at] = sum_key.astype(BF)
                dkv[j, :, slice(128 + at.start, 128 + at.stop)] = sum_value.astype(BF)
            pair.append(tn(key * scale, d_scores))
            if h % 2:
                both = jnp.concatenate(pair, axis=0).T
                turned = both * cos_ref[...] - swap_halves(both) * sin_ref[...]
                right1[mine, pl.ds(pl.multiple_of(j * wide + HD * (h - 1), 128), 128)] = turned.astype(BF)
                pair = []
        for m in range(1, nctx):
            share(j, m).start()

        @pl.when(j == 0)
        def _():
            serve(0)

    loads[1].wait()
    dr_save.wait()
    acc[...] = nt(right1[mine, :qw], wq[...])
    serve(1)
    for j in range(blocks):
        total = dkv[j, mine].astype(F32)
        for m in range(1, nctx):
            share(j, m).wait_recv()
            total += land[j, m].astype(F32)
        d_key = total[:, :128]
        d_key = d_key * cos_ref[...] - swap_halves(d_key) * sin_ref[...]
        right1[mine, qw + 128 * j : qw + 128 * (j + 1)] = d_key.astype(BF)
        right1[mine, qw + kvw + 128 * j : qw + kvw + 128 * (j + 1)] = total[:, 128:].astype(BF)
    own_rows = right1.at[mine]
    r_x = remote(own_rows, own_rows, r_sem.at[0, 0], r_sem.at[1, 0], {"ctx": me ^ 2})
    r_core = remote(own_rows, own_rows, r_sem.at[0, 1], r_sem.at[1, 1], {"ctx": me ^ 1})
    r_onward = remote(
        right1.at[cross], right1.at[cross], r_sem.at[0, 2], r_sem.at[1, 2], {"ctx": me ^ 1}
    )
    r_x.start()
    r_core.start()
    x_copies[2].start()
    loads[2].wait()
    loads[3].wait()
    low[...] = (
        acc[...]
        + nt(right1[mine, qw : qw + kvw], wk[...])
        + nt(right1[mine, qw + kvw :], wv[...])
    ).astype(BF)
    y_front = remote(low, front_got, y_sem.at[0, 0], y_sem.at[1, 0], mate)
    y_front.start()

    nq = right1.shape[1]

    def att_copies(w, at):
        return [
            remote(
                prod.at[z_rows(lax.rem(z + s, ndp)), at],
                att_z.at[z, :, at],
                att_sem.at[0, w, s],
                att_sem.at[1, w, s],
                peers[s - 1],
            )
            for s in range(1, ndp)
        ]

    def att_own_copy(w, at):
        return pltpu.make_async_copy(
            prod.at[z_rows(z), at], att_z.at[z, :, at], att_sem.at[0, w, 0]
        )

    out_cols = slice(nq, prod.shape[1])
    qkv_cols = slice(0, nq)
    for copies in l_loads:
        done(copies)
    for copy in spreads:
        copy.wait()
    prod[:, out_cols] = tn(left2[...], right2[...]).astype(BF)
    for copy in att_copies(1, out_cols):
        copy.start()
    att_own_copy(1, out_cols).start()
    r_x.wait_recv()
    r_onward.start()
    r_core.wait_recv()
    r_onward.wait_recv()
    prod[:, qkv_cols] = tn(left1[...], right1[...]).astype(BF)
    for copy in att_copies(0, qkv_cols):
        copy.start()
    att_own_copy(0, qkv_cols).start()

    room = [n_all.at[pl.ds(i * span, span)] for i in range(4)]

    def fetch(src, dst, i):
        return pltpu.make_async_copy(src, dst, tail_sem.at[i])

    first = [fetch(resid_hbm, acc, 0), fetch(out_hbm, room[0], 1), fetch(x_hbm, room[1], 2)]
    for copy in first:
        copy.start()
    y_out.wait()
    got = fetch(out_got, room[2], 3)
    got.start()
    for copy in first + [got]:
        copy.wait()
    g_all[:span] = (
        acc[...] + (n_all[:span].astype(F32) + n_all[2 * span : 3 * span].astype(F32))
    ).astype(BF)
    out_save = pltpu.make_async_copy(g_all.at[pl.ds(0, span)], output, tail_sem.at[4])
    out_save.start()
    y_front.wait()
    last = [fetch(dr_out, acc, 5), fetch(front_got, room[3], 6)]
    for copy in last:
        copy.start()
    for copy in last:
        copy.wait()
    v = n_all[span : 2 * span].astype(F32)
    factor = lax.rsqrt(jnp.mean(v * v, axis=-1, keepdims=True) + EPS)

    def front_part(at):
        x = n_all[span : 2 * span, at].astype(F32)
        return x * factor, low[:, at].astype(F32) + n_all[3 * span :, at].astype(F32)

    gains[...] = jnp.zeros(gains.shape, F32)
    dots = jnp.zeros((span, 1), F32)
    for c in range(ndp):
        at = slice(c * cols, (c + 1) * cols)
        unit, back = front_part(at)
        term = back * unit
        row = jnp.sum(term, axis=0, keepdims=True)
        for p in range(nctx):
            some = slice(p * part, (p + 1) * part)
            gains[p, 0:1, c * part : (c + 1) * part] = row[:, some]
            gains[p, 1:2, c * part : (c + 1) * part] = gain_grad_ref[
                :, c * cols + p * part : c * cols + (p + 1) * part
            ]
        dots += jnp.sum(term * gain1_ref[:, at], axis=-1, keepdims=True)
    dots = dots / width
    gx_copies = [
        remote(gains.at[me ^ m], gains_x.at[m], gx_sem.at[0, m], gx_sem.at[1, m], {"ctx": me ^ m})
        for m in range(1, nctx)
    ]
    for copy in gx_copies:
        copy.start()
    for c in range(4):
        at = slice(c * cols, (c + 1) * cols)
        unit, back = front_part(at)
        acc[:, at] += factor * (back * gain1_ref[:, at] - unit * dots)
    grad_save = pltpu.make_async_copy(acc, input_grad, tail_sem.at[7])
    grad_save.start()
    total = gains[me]
    for m in range(1, nctx):
        gx_copies[m - 1].wait()
        total += gains_x[m]
    for b in range(ndp):
        gains_z[0, b] = total[:, b * part : (b + 1) * part]
    gz_copies = [
        remote(
            gains_z.at[0, lax.rem(z + s, ndp)],
            gains_z.at[1, s],
            gz_sem.at[0, s],
            gz_sem.at[1, s],
            peers[s - 1],
        )
        for s in range(1, ndp)
    ]
    for copy in gz_copies:
        copy.start()
    serve(2)
    total = gains_z[0, z]
    for s in range(1, ndp):
        gz_copies[s - 1].wait()
        total += gains_z[1, s]
    gains_ref[...] = total
    out_save.wait()
    grad_save.wait()
    for j in range(blocks):
        for m in range(1, nctx):
            share(j, m).wait_send()
    r_x.wait_send()
    r_core.wait_send()
    r_onward.wait_send()
    for w, at in ((1, out_cols), (0, qkv_cols)):
        for copy in att_copies(w, at):
            copy.wait()
        att_own_copy(w, at).wait()
    for w in range(3):
        for copy in z_copies(w):
            copy.wait()
        z_own_copy(w).wait()


def rear(
    where, q, kv, lse, cosine, sine, gain, gain1, dn, n2, n_all, og, og_all, og_far, wg, wu, wd,
    wq, wk, wv, wo, resid, n1p, n1_all, att, att_all, out_part, x, ndp, nctx, chunk=256, rows=256,
):
    span, width = n2.shape
    tokens, length = span * ndp, span * nctx
    units = wg.shape[1] // ndp
    part = width // (ndp * nctx)
    mine = ndp * part
    qw, kvw = wq.shape[1], wk.shape[1]
    qkvw = qw + 2 * kvw
    dma = pltpu.SemaphoreType.DMA
    flat = jax.ShapeDtypeStruct((part, ndp * units), BF)
    row = jax.ShapeDtypeStruct((span, width), BF)
    return pl.pallas_call(
        functools.partial(rear_kernel, ndp, nctx, qw // kvw, chunk, rows),
        in_specs=[SMEM_SPEC] + [VMEM_SPEC] * 8 + [HBM_SPEC] * 19,
        out_specs=[HBM_SPEC] * 9 + [VMEM_SPEC],
        out_shape=[
            jax.ShapeDtypeStruct((ndp, part, units), BF),
            flat,
            flat,
            jax.ShapeDtypeStruct((ndp, part, qkvw + qw), BF),
            row,
            row,
            jax.ShapeDtypeStruct((span, width), F32),
            row,
            jax.ShapeDtypeStruct((span, width), F32),
            jax.ShapeDtypeStruct((8, part), F32),
        ],
        scratch_shapes=[
            pltpu.VMEM((tokens, width), BF),
            pltpu.VMEM((tokens, width), BF),
            pltpu.VMEM((3 * tokens, units), BF),
            pltpu.VMEM((2, width, chunk), BF),
            pltpu.VMEM((2, width, chunk), BF),
            pltpu.VMEM((2, chunk, width), BF),
            pltpu.VMEM((2, 2, mine, units), BF),
            pltpu.VMEM((2, 2, mine, units), BF),
            pltpu.VMEM((3, mine, units), BF),
            pltpu.VMEM((3, mine, units), BF),
            pltpu.VMEM((3, mine, units), BF),
            pltpu.VMEM((length, width // nctx), BF),
            pltpu.VMEM((length, width // nctx), BF),
            pltpu.VMEM((length, qkvw), BF),
            pltpu.VMEM((length, qw), BF),
            pltpu.VMEM((mine, qkvw + qw), BF),
            pltpu.VMEM((span, width), BF),
            pltpu.VMEM((span, qw), BF),
            pltpu.VMEM((length, span), F32),
            pltpu.VMEM((kvw // 128, length, 256), BF),
            pltpu.VMEM((kvw // 128, nctx, span, 256), BF),
            pltpu.VMEM((span, width), F32),
            pltpu.VMEM((1, width), F32),
            pltpu.VMEM((nctx, 8, ndp * part), F32),
            pltpu.VMEM((nctx, 8, ndp * part), F32),
            pltpu.VMEM((2, ndp, 8, part), F32),
            dma((2, ndp)),
            dma((2, nctx)),
            dma((2, 3)),
            dma((4,)),
            dma((2, 2)),
            dma((2, nctx)),
            dma((2, kvw // 128, nctx)),
            dma((2, 3)),
            dma((2, 3)),
            dma((2, 3)),
            dma((2, 3, ndp)),
            dma((3,)),
            dma((2, 2, ndp)),
            dma((2, 2)),
            dma((3,)),
            dma((2,)),
            dma((8,)),
            dma((2, nctx)),
            dma((2, ndp)),
        ],
        compiler_params=pltpu.CompilerParams(
            vmem_limit_bytes=127 * 512 * 1024, collective_id=2, has_side_effects=True
        ),
        cost_estimate=cost(12 * tokens * width * units, 4 * tokens * width),
        name="rear",
    )(
        where, q, kv, lse, cosine, sine, gain.reshape(1, width), gain1.reshape(1, width), dn,
        n2, n_all, og, og_all, og_far, wg, wu, wd, wq, wk, wv, wo,
        resid, n1p, n1_all, att, att_all, out_part, x,
    )


def dot_plain(left, right):
    return jnp.dot(left, right, preferred_element_type=F32)


def dot_right(left, right):
    return lax.dot_general(left, right, (((1,), (1,)), ((), ())), preferred_element_type=F32)


def dot_left(left, right):
    return lax.dot_general(left, right, (((0,), (0,)), ((), ())), preferred_element_type=F32)


def normed(v, gain):
    return v * lax.rsqrt(jnp.mean(v * v, axis=-1, keepdims=True) + EPS) * gain


def norm_back(v, gain, grad):
    factor = lax.rsqrt(jnp.mean(v * v, axis=-1, keepdims=True) + EPS)
    unit = v * factor
    d_unit = grad * gain
    d_gain = jnp.sum(grad * unit, axis=0)
    d_v = factor * (d_unit - unit * jnp.mean(d_unit * unit, axis=-1, keepdims=True))
    return (d_v, d_gain)


def rotate(t, cosine, sine):
    half = t.shape[-1] // 2
    first, second = (t[..., :half], t[..., half:])
    return jnp.concatenate(
        [first * cosine - second * sine, second * cosine + first * sine], axis=-1
    )


def rotate_back(t, cosine, sine):
    half = t.shape[-1] // 2
    first, second = (t[..., :half], t[..., half:])
    return jnp.concatenate(
        [first * cosine + second * sine, second * cosine - first * sine], axis=-1
    )


def score_block(query5, key_all, allowed):
    scores = jnp.einsum(
        "scngd,slnd->sngcl", query5, key_all, preferred_element_type=F32
    ) * HD ** (-0.5)
    return jnp.where(allowed[:, None, None], scores, NEG)


def build(ndp, nctx, nten):
    def pull(v, axis, n, s):
        return lax.ppermute(v, axis, [((i + s) % n, i) for i in range(n)])

    def flip(v, axis, n, bit):
        return lax.ppermute(v, axis, [(i, i ^ bit) for i in range(n)])

    def tensor_sum(v):
        low = v.astype(BF)
        if nten == 2:
            return low.astype(F32) + flip(low, "tensor", 2, 1).astype(F32)
        return lax.psum(low, "tensor").astype(F32)

    def gather_dp(v):
        rows = v.shape[0] // nten
        part = lax.dynamic_slice_in_dim(v, lax.axis_index("tensor") * rows, rows, 0)
        pieces = [v]
        for s in range(1, ndp):
            got = pull(part, "dp", ndp, s)
            pieces.append(got)
            for t in range(1, nten):
                pieces.append(pull(got, "tensor", nten, t))
        return jnp.concatenate(pieces, axis=0)

    def ctx_sum(full):
        r = full.shape[0] // (ndp * nctx)
        me = lax.axis_index("ctx")
        work = full.reshape(ndp, nctx, r, full.shape[1])
        bit = 1
        while bit < nctx:
            left = work.shape[1] // 2
            work = work.reshape(ndp, left, 2, r, full.shape[1])
            mine = (me // bit) % 2
            keep = lax.dynamic_index_in_dim(work, mine, 2, keepdims=False)
            give = lax.dynamic_index_in_dim(work, 1 - mine, 2, keepdims=False)
            got = flip(give, "ctx", nctx, bit)
            work = (keep.astype(F32) + got.astype(F32)).astype(BF)
            bit *= 2
        return work.reshape(ndp, r, full.shape[1])

    def finish_slices(full):
        got = lax.all_to_all(ctx_sum(full), "dp", 0, 0, tiled=True)
        return jnp.swapaxes(got, 0, 1).reshape(got.shape[1], -1).astype(F32)

    def finish_sum(full):
        got = lax.all_to_all(ctx_sum(full), "dp", 0, 0, tiled=True)
        return jnp.sum(got.astype(F32), axis=0)

    def local(
        layer_input,
        output_grad,
        prefix,
        attn_gain,
        w_query,
        w_key,
        w_value,
        w_out,
        mlp_gain,
        w_gate,
        w_up,
        w_down,
    ):
        seqs, span, width = layer_input.shape
        q_heads = w_query.shape[1] // HD
        kv_heads = w_key.shape[1] // HD
        group = q_heads // kv_heads
        zi = lax.axis_index("dp")
        rows = layer_input.astype(F32).reshape(seqs * span, width)
        grad_low = output_grad.reshape(seqs * span, width)
        grad_rows = grad_low.astype(F32)
        grad_all = gather_dp(grad_low)

        first = lax.axis_index("ctx") * span
        position = (first + jnp.arange(span)).astype(F32)
        frequency = ROPE_BASE ** (-jnp.arange(HD // 2).astype(F32) * 2.0 / HD)
        angle = position[:, None] * frequency[None, :]
        cosine = jnp.cos(angle)[None, :, None, :]
        sine = jnp.sin(angle)[None, :, None, :]
        normed1 = normed(rows, attn_gain).astype(BF)
        query = rotate(
            dot_plain(normed1, w_query).reshape(seqs, span, q_heads, HD), cosine, sine
        ).astype(BF)
        keyed = rotate(
            dot_plain(normed1, w_key).reshape(seqs, span, kv_heads, HD), cosine, sine
        ).astype(BF)
        valued = dot_plain(normed1, w_value).astype(BF).reshape(seqs, span, kv_heads * HD)
        key_all, value_all = (
            lax.all_gather(
                keyed.reshape(seqs, span, kv_heads * HD), "ctx", axis=1, tiled=True
            ),
            lax.all_gather(valued, "ctx", axis=1, tiled=True),
        )
        length = key_all.shape[1]
        key_all = key_all.reshape(seqs, length, kv_heads, HD)
        value_all = value_all.reshape(seqs, length, kv_heads, HD)
        query5 = query.reshape(seqs, span, kv_heads, group, HD)
        query_pos = first + jnp.arange(span)
        key_pos = jnp.arange(length)
        allowed = (key_pos[None, None, :] <= query_pos[None, :, None]) | (
            key_pos[None, None, :] < prefix[:, None, None]
        )
        scores = score_block(query5, key_all, allowed)
        top = jnp.max(scores, axis=-1, keepdims=True)
        exponent = jnp.exp(scores - top)
        total = jnp.sum(exponent, axis=-1, keepdims=True)
        log_total = top + jnp.log(total)
        probs_low = (exponent / total).astype(BF)
        attended = jnp.einsum(
            "sngcl,slnd->scngd", probs_low, value_all, preferred_element_type=F32
        )
        attended = attended.astype(BF).reshape(seqs * span, q_heads * HD)
        resid = rows + tensor_sum(dot_plain(attended, w_out))
        normed2 = normed(resid, mlp_gain).astype(BF)
        normed2_all = gather_dp(normed2)
        gate = dot_plain(normed2, w_gate)
        up = dot_plain(normed2, w_up)
        act = (jax.nn.silu(gate) * up).astype(BF)

        def mlp_back(gate, up, d_act):
            sigmoid_gate = jax.nn.sigmoid(gate)
            d_gate_pre = (
                d_act * up * sigmoid_gate * (1.0 + gate * (1.0 - sigmoid_gate))
            ).astype(BF)
            d_up_pre = (d_act * gate * sigmoid_gate).astype(BF)
            return d_gate_pre, d_up_pre

        d_act = dot_right(grad_low, w_down)
        d_gate_pre, d_up_pre = mlp_back(gate, up, d_act)
        back_terms = dot_right(d_gate_pre, w_gate) + dot_right(d_up_pre, w_up)
        d_normed2 = tensor_sum(back_terms)
        output = (resid + tensor_sum(dot_plain(act, w_down))).astype(BF)
        output = output.reshape(seqs, span, width)

        units = w_gate.shape[1] // ndp
        wg = lax.dynamic_slice_in_dim(w_gate, zi * units, units, 1)
        wu = lax.dynamic_slice_in_dim(w_up, zi * units, units, 1)
        wd = lax.dynamic_slice_in_dim(w_down, zi * units, units, 0)
        gate_s = dot_plain(normed2_all, wg)
        up_s = dot_plain(normed2_all, wu)
        d_act_s = dot_right(grad_all, wd)
        act_s = (jax.nn.silu(gate_s) * up_s).astype(BF)
        d_gate_s, d_up_s = mlp_back(gate_s, up_s, d_act_s)
        s_down = finish_slices(dot_left(grad_all, act_s).astype(BF)).T
        s_gate = finish_slices(dot_left(normed2_all, d_gate_s).astype(BF))
        s_up = finish_slices(dot_left(normed2_all, d_up_s).astype(BF))

        d_resid_norm, g_mlp_gain = norm_back(resid, mlp_gain, d_normed2)
        d_resid = grad_rows + d_resid_norm
        d_resid_low = d_resid.astype(BF)
        s_out = finish_sum(dot_left(d_resid_low, attended).astype(BF)).T
        d_attended = dot_right(d_resid_low, w_out).astype(BF).reshape(query5.shape)
        scores = score_block(query5, key_all, allowed)
        probs = jnp.exp(scores - log_total)
        probs_low = probs.astype(BF)
        d_probs = jnp.einsum(
            "scngd,slnd->sngcl", d_attended, value_all, preferred_element_type=F32
        )
        delta = jnp.sum(probs * d_probs, axis=-1, keepdims=True)
        d_scores = (probs * (d_probs - delta)).astype(BF)
        scale = HD ** (-0.5)
        d_query = (
            jnp.einsum("sngcl,slnd->scngd", d_scores, key_all, preferred_element_type=F32) * scale
        )
        d_key_all = (
            jnp.einsum("sngcl,scngd->slnd", d_scores, query5, preferred_element_type=F32) * scale
        )
        d_value_all = jnp.einsum(
            "sngcl,scngd->slnd", probs_low, d_attended, preferred_element_type=F32
        )
        d_kv = jnp.concatenate(
            [
                d_key_all.reshape(length, kv_heads * HD).astype(BF),
                d_value_all.reshape(length, kv_heads * HD).astype(BF),
            ],
            axis=1,
        )
        d_kv = lax.psum_scatter(d_kv, "ctx", scatter_dimension=0, tiled=True).astype(F32)
        d_key, d_val = d_kv[:, : kv_heads * HD], d_kv[:, kv_heads * HD :]
        d_qp = (
            rotate_back(d_query.reshape(seqs, span, q_heads, HD), cosine, sine)
            .astype(BF)
            .reshape(seqs * span, q_heads * HD)
        )
        d_kp = (
            rotate_back(d_key.reshape(seqs, span, kv_heads, HD), cosine, sine)
            .astype(BF)
            .reshape(seqs * span, kv_heads * HD)
        )
        d_vp = d_val.astype(BF).reshape(seqs * span, kv_heads * HD)
        front_terms = dot_right(d_qp, w_query) + dot_right(d_kp, w_key) + dot_right(d_vp, w_value)
        d_normed1 = tensor_sum(front_terms)
        d_rows_norm, g_attn_gain = norm_back(rows, attn_gain, d_normed1)
        d_input = d_resid + d_rows_norm
        d_input = d_input.reshape(seqs, span, width)
        s_qkv = finish_sum(
            dot_left(normed1, jnp.concatenate([d_qp, d_kp, d_vp], axis=1)).astype(BF)
        )
        nq, nk = q_heads * HD, kv_heads * HD
        s_query, s_key, s_value = s_qkv[:, :nq], s_qkv[:, nq : nq + nk], s_qkv[:, nq + nk :]
        gains = jnp.stack([g_attn_gain, g_mlp_gain])
        gains = lax.psum_scatter(gains, ("dp", "ctx"), scatter_dimension=1, tiled=True)
        return (
            output,
            d_input,
            gains[0],
            s_query,
            s_key,
            s_value,
            s_out,
            gains[1],
            s_gate,
            s_up,
            s_down,
        )

    return local


def suits(ndp, nctx, nten, layer_input, output_grad, prefix, attn_gain, w_query, w_key, w_value, w_out, mlp_gain, w_gate, w_up, w_down):
    seqs, span, width = layer_input.shape
    return (
        seqs == 1
        and (ndp, nctx, nten) == (4, 4, 2)
        and (span, width) == (256, 2048)
        and (w_query.shape[1], w_key.shape[1], w_gate.shape[1]) == (1024, 256, 4096)
    )


def build_fast(ndp, nctx, nten):
    def local(
        layer_input,
        output_grad,
        prefix,
        attn_gain,
        w_query,
        w_key,
        w_value,
        w_out,
        mlp_gain,
        w_gate,
        w_up,
        w_down,
    ):
        seqs, span, width = layer_input.shape
        kvw, nq = w_key.shape[1], w_query.shape[1]
        low = layer_input.reshape(span, width)
        grad_low = output_grad.reshape(span, width)
        first = lax.axis_index("ctx") * span
        where = jnp.stack([first, prefix[0]]).astype(jnp.int32)
        cosine, sine = rope_tables(first, span)
        n1p, query, kv, attended, lse, resid, normed2, grad_all = front(
            where, low, attn_gain, w_query, w_key, w_value, w_out, cosine, sine, mlp_gain, grad_low, ndp, nctx
        )
        out_part, dn, n_all, n1_all, att_all, grad_far = middle(
            normed2, grad_low, w_gate, w_up, w_down, n1p, attended, grad_all, ndp, nctx
        )
        down_z, gate_z, up_z, att_z, _, _, _, output, d_input, gains = rear(
            where, query, kv, lse, cosine, sine, mlp_gain, attn_gain, dn, normed2, n_all, grad_low,
            grad_all, grad_far, w_gate, w_up, w_down, w_query, w_key, w_value, w_out, resid, n1p, n1_all,
            attended, att_all, out_part, low, ndp, nctx,
        )
        output = output.reshape(seqs, span, width)
        d_input = d_input.reshape(seqs, span, width)
        s_down = jnp.swapaxes(down_z, 1, 2).reshape(w_down.shape[0], -1).astype(F32)
        s_gate, s_up = gate_z.astype(F32), up_z.astype(F32)
        s_att = jnp.sum(att_z.astype(F32), axis=0)
        s_query, s_key = s_att[:, :nq], s_att[:, nq : nq + kvw]
        s_value, s_out = s_att[:, nq + kvw : nq + 2 * kvw], s_att[:, nq + 2 * kvw :].T
        return (
            output,
            d_input,
            gains[0],
            s_query,
            s_key,
            s_value,
            s_out,
            gains[1],
            s_gate,
            s_up,
            s_down,
        )

    return local


def solution(mesh):
    sizes = mesh.shape["dp"], mesh.shape["ctx"], mesh.shape["tensor"]
    plain, fast = build(*sizes), build_fast(*sizes)

    def local(*args):
        return (fast if suits(*sizes, *args) else plain)(*args)

    return jax.shard_map(
        local,
        mesh=mesh,
        in_specs=(
            P("dp", "ctx", None),
            P("dp", "ctx", None),
            P("dp"),
            P(),
            P(None, "tensor"),
            P(None, "tensor"),
            P(None, "tensor"),
            P("tensor", None),
            P(),
            P(None, "tensor"),
            P(None, "tensor"),
            P("tensor", None),
        ),
        out_specs=(
            P("dp", "ctx", None),
            P("dp", "ctx", None),
            P(("dp", "ctx")),
            P(("dp", "ctx"), "tensor"),
            P(("dp", "ctx"), "tensor"),
            P(("dp", "ctx"), "tensor"),
            P("tensor", ("dp", "ctx")),
            P(("dp", "ctx")),
            P(("dp", "ctx"), "tensor"),
            P(("dp", "ctx"), "tensor"),
            P("tensor", ("dp", "ctx")),
        ),
        check_vma=False,
    )
```

```python
import functools
import jax
import jax.numpy as jnp
from jax import lax
from jax.experimental import pallas as pl
from jax.experimental.pallas import tpu as pltpu
from jax.sharding import PartitionSpec as P

HD = 64
EPS = 1e-05
ROPE_BASE = 500000.0
NEG = -1e30
BF = jnp.bfloat16
F32 = jnp.float32
VMEM_MOST = 60 * 1024 * 1024


def cost(flops, nbytes, trans=0):
    return pl.CostEstimate(flops=int(flops), bytes_accessed=int(nbytes), transcendentals=int(trans))


def nt(a, b):
    return lax.dot_general(a, b, (((1,), (1,)), ((), ())), preferred_element_type=F32)


def tn(a, b):
    return lax.dot_general(a, b, (((0,), (0,)), ((), ())), preferred_element_type=F32)


def nn(a, b):
    return jnp.dot(a, b, preferred_element_type=F32)


def swap_halves(t):
    lane = lax.broadcasted_iota(jnp.int32, t.shape, 1) % HD
    n = t.shape[1]
    return jnp.where(
        lane < HD // 2, pltpu.roll(t, n - HD // 2, 1), pltpu.roll(t, HD // 2, 1)
    )


def rope_tables(first, span):
    position = (first + jnp.arange(span)).astype(F32)
    frequency = ROPE_BASE ** (-jnp.arange(HD // 2).astype(F32) * 2.0 / HD)
    angle = position[:, None] * frequency[None, :]
    cosine, sine = jnp.cos(angle), jnp.sin(angle)
    return (
        jnp.concatenate([cosine, cosine, cosine, cosine], axis=1),
        jnp.concatenate([-sine, sine, -sine, sine], axis=1),
    )


def mask_bias(first, prefix, length, span):
    key = lax.broadcasted_iota(jnp.int32, (length, span), 0)
    query = lax.broadcasted_iota(jnp.int32, (length, span), 1) + first
    return jnp.where((key <= query) | (key < prefix), 0.0, NEG).astype(F32)


def gate_parts(gate, up, d_act):
    sig = 1.0 / (1.0 + jnp.exp(-gate))
    silu = gate * sig
    return (
        (silu * up).astype(BF),
        (d_act * up * (sig + silu * (1.0 - sig))).astype(BF),
        (d_act * silu).astype(BF),
    )


MESH = pl.DeviceIdType.MESH


def remote(src, dst, send, recv, to):
    return pltpu.make_async_remote_copy(
        src_ref=src, dst_ref=dst, send_sem=send, recv_sem=recv, device_id=to, device_id_type=MESH
    )


def enter(devices):
    barrier = pltpu.get_barrier_semaphore()
    for to in devices:
        pl.semaphore_signal(barrier, inc=1, device_id=to, device_id_type=MESH)
    pl.semaphore_wait(barrier, len(devices))


def around(z, ndp):
    return [{"dp": lax.rem(z + 1, ndp)}, {"dp": lax.rem(z + ndp - 1, ndp)}]


def mates(me, y):
    return [{"ctx": me ^ 1}, {"ctx": me ^ 2}, {"ctx": me ^ 3}, {"tensor": 1 - y}]


class Relay:
    def __init__(self, z, ndp, hop, own, blocks, sems):
        self.z, self.ndp, self.hop = z, ndp, hop
        self.own, self.blocks, self.sems = own, blocks, sems

    def copy(self, way, block, to):
        src = self.own if self.hop == 1 else self.blocks.at[block]
        at = 0 if way > 0 else 1
        return remote(
            src, self.blocks.at[block], self.sems.at[0, at], self.sems.at[1, at], {"dp": to}
        )

    def each(self, act, incoming):
        z, hop = self.z, self.hop
        for way in (1, -1):
            if incoming:
                block = z - way * hop
                ok = block >= 0 if way > 0 else block < self.ndp
            else:
                block = z - way * (hop - 1)
                ok = (block >= 0) & (z < self.ndp - 1) if way > 0 else (block < self.ndp) & (z > 0)

            @pl.when(ok)
            def _(way=way, block=block):
                act(self.copy(way, block, z if incoming else z + way))

    def start(self):
        self.each(lambda c: c.start(), False)

    def wait_recv(self):
        self.each(lambda c: c.wait_recv(), True)

    def wait_send(self):
        self.each(lambda c: c.wait_send(), False)


def rope_parts(t, cosine, sine):
    pieces = []
    for i in range(t.shape[1] // 128):
        part = t[:, 128 * i : 128 * (i + 1)]
        pieces.append((part * cosine + swap_halves(part) * sine).astype(BF))
    return pieces


def front_kernel(
    ndp, nctx, group,
    where_ref, x_ref, gain1_ref, wq_hbm, wk_hbm, wv_hbm, wo_hbm, cos_ref, sin_ref, gain2_ref, og_hbm,
    n1_ref, q_ref, kv_out, att_ref, lse_ref, resid_ref, n2_ref, og_all,
    n1_buf, wq, wk, wv, wo, kv, bias_ref, part, part_got,
    w_sem, kv_sem, kv_out_sem, part_sem, z_sem,
):
    z, me, y = lax.axis_index("dp"), lax.axis_index("ctx"), lax.axis_index("tensor")
    span, width = x_ref.shape
    length = kv.shape[0]
    kvw = wk.shape[1]
    loads = [
        pltpu.make_async_copy(src, dst, w_sem.at[i])
        for i, (src, dst) in enumerate(((wk_hbm, wk), (wv_hbm, wv), (wq_hbm, wq), (wo_hbm, wo)))
    ]
    for copy in loads:
        copy.start()
    hop1 = Relay(z, ndp, 1, og_hbm, og_all, z_sem.at[0])
    hop2 = Relay(z, ndp, 2, og_hbm, og_all, z_sem.at[1])
    enter(around(z, ndp) + mates(me, y))
    hop1.start()
    v = x_ref[...].astype(F32)
    factor = lax.rsqrt(jnp.mean(v * v, axis=-1, keepdims=True) + EPS)
    n1_buf[...] = (v * factor * gain1_ref[...]).astype(BF)
    cosine, sine = cos_ref[...], sin_ref[...]
    mine = pl.ds(pl.multiple_of(me * span, span), span)
    loads[0].wait()
    for i, piece in enumerate(rope_parts(nn(n1_buf[...], wk[...]), cosine, sine)):
        kv[mine, 128 * i : 128 * (i + 1)] = piece
    loads[1].wait()
    kv[mine, kvw:] = nn(n1_buf[...], wv[...]).astype(BF)

    def kv_copy(which, block, mask):
        rows = pl.ds(pl.multiple_of(block * span, span), span)
        return remote(kv.at[rows], kv.at[rows], kv_sem.at[0, which], kv_sem.at[1, which], {"ctx": me ^ mask})

    to_x = kv_copy(0, me, 2)
    to_core = kv_copy(1, me, 1)
    onward = kv_copy(2, me ^ 2, 1)
    to_x.start()
    to_core.start()
    loads[2].wait()
    for i, piece in enumerate(rope_parts(nn(n1_buf[...], wq[...]), cosine, sine)):
        q_ref[:, 128 * i : 128 * (i + 1)] = piece
    part_width = width // (ndp * nctx)
    for p in range(nctx):
        for b in range(ndp):
            at = (b * nctx + p) * part_width
            n1_ref[p, :, b * part_width : (b + 1) * part_width] = n1_buf[:, at : at + part_width]
    bias_ref[...] = mask_bias(where_ref[0], where_ref[1], length, span)
    to_x.wait_recv()
    onward.start()
    to_core.wait_recv()
    onward.wait_recv()
    to_x.wait_send()
    to_core.wait_send()
    onward.wait_send()
    save_kv = pltpu.make_async_copy(kv, kv_out, kv_out_sem)
    save_kv.start()

    wide = 128 * group
    heads = wide // HD

    @pl.loop(0, kvw // 128)
    def _(j):
        lanes = pl.ds(pl.multiple_of(j * wide, 128), wide)
        queries = q_ref[:, lanes] * jnp.asarray(HD**-0.5, BF)
        keys = kv[:, pl.ds(pl.multiple_of(j * 128, 128), 128)]
        values = kv[:, pl.ds(pl.multiple_of(kvw + j * 128, 128), 128)]
        rows, outs = [], []
        for h in range(heads):
            at = slice(HD * (h // group), HD * (h // group + 1))
            scores = nt(keys[:, at], queries[:, HD * h : HD * (h + 1)]) + bias_ref[...]
            top = jnp.max(scores, axis=0, keepdims=True)
            exponent = jnp.exp(scores - top)
            total = jnp.sum(exponent, axis=0, keepdims=True)
            rows.append(top + jnp.log(total))
            outs.append(tn(values[:, at], exponent.astype(BF)) / total)
            if h % 2:
                both = jnp.concatenate(outs, axis=0).T.astype(BF)
                att_ref[:, pl.ds(pl.multiple_of(j * wide + HD * (h - 1), 128), 128)] = both
                outs = []
        lse_ref[pl.ds(pl.multiple_of(j * heads, heads), heads), :] = jnp.concatenate(rows, axis=0)

    hop1.wait_recv()
    hop2.start()
    save_kv.wait()
    loads[3].wait()
    count, _, cols = part.shape
    copies = [
        remote(part.at[c], part_got.at[c], part_sem.at[0, c], part_sem.at[1, c], {"tensor": 1 - y})
        for c in range(count)
    ]
    for c in range(count):
        part[c] = nn(att_ref[...], wo[:, c * cols : (c + 1) * cols]).astype(BF)
        copies[c].start()
    square = jnp.zeros((span, 1), F32)
    for c in range(count):
        at = slice(c * cols, (c + 1) * cols)
        copies[c].wait_recv()
        r = x_ref[:, at].astype(F32) + (part[c].astype(F32) + part_got[c].astype(F32))
        resid_ref[:, at] = r
        square += jnp.sum(r * r, axis=-1, keepdims=True)
    factor = lax.rsqrt(square / width + EPS)
    for c in range(count):
        at = slice(c * cols, (c + 1) * cols)
        n2_ref[:, at] = (resid_ref[:, at] * factor * gain2_ref[:, at]).astype(BF)
    for copy in copies:
        copy.wait_send()
    hop1.wait_send()
    hop2.wait_recv()
    hop2.wait_send()


HBM_SPEC = pl.BlockSpec(memory_space=pl.ANY)
VMEM_SPEC = pl.BlockSpec(memory_space=pltpu.VMEM)
SMEM_SPEC = pl.BlockSpec(memory_space=pltpu.SMEM)


def own(number):
    return pltpu.CompilerParams(
        vmem_limit_bytes=VMEM_MOST, collective_id=number, has_side_effects=True
    )


def front(where, x, gain1, wq, wk, wv, wo, cosine, sine, gain2, og, ndp, nctx):
    span, width = x.shape
    qw, kvw = wq.shape[1], wk.shape[1]
    group = qw // kvw
    length = span * nctx
    chunks = 4
    dma = pltpu.SemaphoreType.DMA
    return pl.pallas_call(
        functools.partial(front_kernel, ndp, nctx, group),
        in_specs=[SMEM_SPEC, VMEM_SPEC, VMEM_SPEC] + [HBM_SPEC] * 4 + [VMEM_SPEC] * 3 + [HBM_SPEC],
        out_specs=[VMEM_SPEC, VMEM_SPEC, HBM_SPEC] + [VMEM_SPEC] * 4 + [HBM_SPEC],
        out_shape=[
            jax.ShapeDtypeStruct((nctx, span, width // nctx), BF),
            jax.ShapeDtypeStruct((span, qw), BF),
            jax.ShapeDtypeStruct((length, 2 * kvw), BF),
            jax.ShapeDtypeStruct((span, qw), BF),
            jax.ShapeDtypeStruct((qw // HD, span), F32),
            jax.ShapeDtypeStruct((span, width), F32),
            jax.ShapeDtypeStruct((span, width), BF),
            jax.ShapeDtypeStruct((ndp, span, width), BF),
        ],
        scratch_shapes=[
            pltpu.VMEM((span, width), BF),
            pltpu.VMEM((width, qw), BF),
            pltpu.VMEM((width, kvw), BF),
            pltpu.VMEM((width, kvw), BF),
            pltpu.VMEM((qw, width), BF),
            pltpu.VMEM((length, 2 * kvw), BF),
            pltpu.VMEM((length, span), F32),
            pltpu.VMEM((chunks, span, width // chunks), BF),
            pltpu.VMEM((chunks, span, width // chunks), BF),
            dma((4,)),
            dma((2, 3)),
            dma,
            dma((2, chunks)),
            dma((2, 2, 2)),
        ],
        compiler_params=own(0),
        cost_estimate=cost(2 * span * width * (2 * qw + 2 * kvw), 4 * width * (qw + kvw)),
        name="front",
    )(where, x, gain1.reshape(1, width), wq, wk, wv, wo, cosine, sine, gain2.reshape(1, width), og)


def halves(y, span):
    return pl.ds(pl.multiple_of(y * (span // 2), span // 2), span // 2)


class Far:
    def __init__(self, z, y, blocks, far, sems):
        rows = halves(y, far.shape[0])
        block = jnp.where(z == 1, 3, 0)
        to = jnp.where(z == 1, 0, 3)
        self.over = remote(blocks.at[block, rows], far.at[rows], sems.at[0], sems.at[1], {"dp": to})
        self.gives = (z == 1) | (z == 2)
        self.takes = (z == 0) | (z == 3)

    def start(self):
        pl.when(self.gives)(lambda: self.over.start())

    def finish(self):
        pl.when(self.takes)(lambda: self.over.wait_recv())
        pl.when(self.gives)(lambda: self.over.wait_send())


class Gather:
    def __init__(self, z, y, ndp, own, blocks, sems, swaps):
        self.z, self.y, self.ndp = z, y, ndp
        self.own, self.blocks, self.sems, self.swaps = own, blocks, sems, swaps
        self.rows = halves(y, own.shape[0])

    def over(self, way, hop, block, to):
        src = self.own.at[self.rows] if hop == 1 else self.blocks.at[block, self.rows]
        at = 0 if way > 0 else 1
        return remote(
            src, self.blocks.at[block, self.rows],
            self.sems.at[hop - 1, 0, at], self.sems.at[hop - 1, 1, at], {"dp": to},
        )

    def swap(self, way, hop, block):
        at = 0 if way > 0 else 1
        part = self.blocks.at[block, self.rows]
        return remote(
            part, part, self.swaps.at[hop - 1, 0, at], self.swaps.at[hop - 1, 1, at],
            {"tensor": 1 - self.y},
        )

    def comes(self, way, hop):
        block = self.z - way * hop
        return block, (block >= 0 if way > 0 else block < self.ndp)

    def leaves(self, way, hop):
        block = self.z - way * (hop - 1)
        if way > 0:
            return block, (block >= 0) & (self.z < self.ndp - 1)
        return block, (block < self.ndp) & (self.z > 0)

    def send(self, hop):
        for way in (1, -1):
            block, ok = self.leaves(way, hop)

            @pl.when(ok)
            def _(way=way, block=block):
                self.over(way, hop, block, self.z + way).start()

    def step(self, hop):
        for way in (1, -1):
            block, ok = self.comes(way, hop)

            @pl.when(ok)
            def _(way=way, block=block):
                self.over(way, hop, block, self.z).wait_recv()
                self.swap(way, hop, block).start()

        if hop < self.ndp - 1:
            self.send(hop + 1)

    def finish(self):
        for hop in range(1, self.ndp):
            for way in (1, -1):
                block, ok = self.comes(way, hop)

                @pl.when(ok)
                def _(way=way, block=block, hop=hop):
                    self.swap(way, hop, block).wait()

                block, ok = self.leaves(way, hop)

                @pl.when(ok)
                def _(way=way, block=block, hop=hop):
                    self.over(way, hop, block, self.z + way).wait_send()


def middle_kernel(
    ndp, nctx,
    n_ref, g_ref, wg_ref, wu_ref, wd_ref, n_hbm, n1_hbm, att_hbm, g_near,
    o_ref, dn_ref, n_all, n1_all, att_all, g_far,
    o_acc, dn_acc,
    z_sem, swap_sem, n1_sem, att_sem, far_sem,
):
    z, me, y = lax.axis_index("dp"), lax.axis_index("ctx"), lax.axis_index("tensor")
    j = pl.program_id(0)
    last = pl.num_programs(0) - 1
    gather = Gather(z, y, ndp, n_hbm, n_all, z_sem, swap_sem)
    far = Far(z, y, g_near, g_far, far_sem)
    spreads = []
    for m in range(1, nctx):
        spreads.append(
            remote(n1_hbm.at[me ^ m], n1_all.at[me], n1_sem.at[0, m], n1_sem.at[1, m], {"ctx": me ^ m})
        )
        spreads.append(
            remote(att_hbm, att_all.at[me], att_sem.at[0, m], att_sem.at[1, m], {"ctx": me ^ m})
        )

    @pl.when(j == 0)
    def _():
        enter(around(z, ndp) + mates(me, y))
        gather.send(1)
        for copy in spreads:
            copy.start()

    normed2, grad = n_ref[...], g_ref[...]
    gate = nn(normed2, wg_ref[...])
    up = nn(normed2, wu_ref[...])
    d_act = nt(grad, wd_ref[...])
    act, d_gate, d_up = gate_parts(gate, up, d_act)

    @pl.when(j == 0)
    def _():
        o_acc[...] = nn(act, wd_ref[...])
        dn_acc[...] = nt(d_gate, wg_ref[...]) + nt(d_up, wu_ref[...])

    @pl.when(j > 0)
    def _():
        o_acc[...] += nn(act, wd_ref[...])
        dn_acc[...] += nt(d_gate, wg_ref[...]) + nt(d_up, wu_ref[...])

    @pl.when(j == 3)
    def _():
        gather.step(1)

    @pl.when(j == 5)
    def _():
        gather.step(2)
        far.start()

    @pl.when(j == last)
    def _():
        gather.step(3)
        o_ref[...] = o_acc[...].astype(BF)
        dn_ref[...] = dn_acc[...].astype(BF)
        for copy in spreads:
            copy.wait()
        far.finish()
        gather.finish()


def middle(n2, og, wg, wu, wd, n1p, att, og_all, ndp, nctx, step=512):
    span, width = n2.shape
    units = wg.shape[1]
    dma = pltpu.SemaphoreType.DMA
    whole = pl.BlockSpec((span, width), lambda j: (0, 0))
    cols = pl.BlockSpec((width, step), lambda j: (0, j))
    return pl.pallas_call(
        functools.partial(middle_kernel, ndp, nctx),
        grid=(units // step,),
        in_specs=[
            whole, whole, cols, cols, pl.BlockSpec((step, width), lambda j: (j, 0)),
            HBM_SPEC, HBM_SPEC, HBM_SPEC, HBM_SPEC,
        ],
        out_specs=[whole, whole, HBM_SPEC, HBM_SPEC, HBM_SPEC, HBM_SPEC],
        out_shape=[
            jax.ShapeDtypeStruct((span, width), BF),
            jax.ShapeDtypeStruct((span, width), BF),
            jax.ShapeDtypeStruct((ndp, span, width), BF),
            jax.ShapeDtypeStruct((nctx, span, width // nctx), BF),
            jax.ShapeDtypeStruct((nctx,) + att.shape, BF),
            jax.ShapeDtypeStruct((span, width), BF),
        ],
        scratch_shapes=[
            pltpu.VMEM((span, width), F32),
            pltpu.VMEM((span, width), F32),
            dma((ndp - 1, 2, 2)),
            dma((ndp - 1, 2, 2)),
            dma((2, nctx)),
            dma((2, nctx)),
            dma((2,)),
        ],
        compiler_params=own(1),
        cost_estimate=cost(12 * span * width * units, 6 * width * units),
        name="middle",
    )(n2, og, wg, wu, wd, n2, n1p, att, og_all)


def rear_kernel(
    ndp, nctx, group, chunk, rows,
    where_ref, q_ref, kv_ref, lse_ref, cos_ref, sin_ref, gain_ref, gain1_ref, dn_ref,
    n_own, n_near, g_own, g_near, g_far, wg_hbm, wu_hbm, wd_hbm, wq_hbm, wk_hbm, wv_hbm, wo_hbm,
    resid_hbm, n1_own, n1_near, att_own, att_near, out_hbm, x_hbm,
    down_z, gate_z, up_z, att_z, front_got, out_got, dr_out, output, input_grad, gains_ref,
    n_all, g_all, acts, wg_buf, wu_buf, wd_buf, give, take, x_give, x_take, x_keep,
    left1, left2, right1, right2, prod, low, bias_ref, dkv, land, acc,
    gain_grad_ref, gains, gains_x, gains_z,
    in_sem, l_sem, w_sem, back_sem, dn_sem, low_sem, dkv_sem, r_sem, core_sem, x_sem, zz_sem, z_own,
    att_sem, y_sem, save_sem, far_sem, tail_sem, gx_sem, gz_sem,
):
    z, me, y = lax.axis_index("dp"), lax.axis_index("ctx"), lax.axis_index("tensor")
    tokens, width = n_all.shape
    span, qw = q_ref.shape
    length = kv_ref.shape[0]
    kvw = kv_ref.shape[1] // 2
    units = acts.shape[1]
    core, xpos = me % 2, me // 2
    part = width // (ndp * nctx)
    start = z * units
    peers = [{"dp": lax.rem(z + s, ndp)} for s in range(1, ndp)]
    mate = {"tensor": 1 - y}
    mine = pl.ds(pl.multiple_of(me * span, span), span)
    cross = pl.ds(pl.multiple_of((me ^ 2) * span, span), span)

    def block_load(r, own_ref, near, dst, sem):
        block = lax.rem(jnp.where(z < ndp // 2, z + r, z + ndp - r), ndp)
        at = dst.at[pl.ds(r * span, span)]
        return pltpu.make_async_copy(own_ref if r == 0 else near.at[block], at, sem)

    def go(copies):
        for ok, copy in copies:
            if ok is None:
                copy.start()
            else:
                pl.when(ok)(lambda copy=copy: copy.start())

    def done(copies):
        copies[0][1].wait()

    n_loads = [block_load(r, n_own, n_near, n_all, in_sem.at[0, r]) for r in range(ndp)]
    g_loads = [block_load(r, g_own, g_near, g_all, in_sem.at[1, r]) for r in range(ndp)]
    end = (z == 0) | (z == ndp - 1)
    tail = ndp - 1
    half_rows = halves(y, span)
    half_at = g_all.at[pl.ds(pl.multiple_of(tail * span + y * (span // 2), span // 2), span // 2)]
    half_load = pltpu.make_async_copy(g_far.at[half_rows], half_at, in_sem.at[1, tail])
    half_swap = remote(g_far.at[half_rows], half_at, far_sem.at[0], far_sem.at[1], mate)

    def ctx_load(p, own_ref, near, dst, sem):
        at = dst.at[pl.ds(p * span, span)]
        here = me == p
        return [
            (here, pltpu.make_async_copy(own_ref, at, sem)),
            (jnp.logical_not(here), pltpu.make_async_copy(near.at[p], at, sem)),
        ]

    l_loads = []
    for p in range(nctx):
        l_loads.append(ctx_load(p, att_own, att_near, right2, l_sem.at[0, p]))
        l_loads.append(ctx_load(p, n1_own.at[p], n1_near, left1, l_sem.at[1, p]))

    def weights(j, slot):
        at = pl.multiple_of(start + j * chunk, chunk)
        return (
            pltpu.make_async_copy(wg_hbm.at[:, pl.ds(at, chunk)], wg_buf.at[slot], w_sem.at[slot, 0]),
            pltpu.make_async_copy(wu_hbm.at[:, pl.ds(at, chunk)], wu_buf.at[slot], w_sem.at[slot, 1]),
            pltpu.make_async_copy(wd_hbm.at[pl.ds(at, chunk)], wd_buf.at[slot], w_sem.at[slot, 2]),
        )

    for copy in n_loads + g_loads[:tail]:
        copy.start()
    pl.when(end)(lambda: half_load.start())
    pl.when(jnp.logical_not(end))(lambda: g_loads[tail].start())
    for copy in weights(0, 0):
        copy.start()
    resid_load = pltpu.make_async_copy(resid_hbm, acc, save_sem.at[0])
    resid_load.start()
    for copies in l_loads:
        go(copies)
    dn_got = [x_take.at[2, pl.ds(h * span, span)] for h in range(2)]
    half = width // 2
    dn_copies = [
        remote(
            dn_ref.at[:, pl.ds(h * half, half)], dn_got[h], dn_sem.at[0, h], dn_sem.at[1, h], mate
        )
        for h in range(2)
    ]
    enter(peers + mates(me, y))
    pl.when(end)(lambda: half_swap.start())
    for copy in dn_copies:
        copy.start()

    count = units // chunk
    for copy in n_loads + g_loads[:tail]:
        copy.wait()

    @pl.loop(0, count)
    def _(j):
        slot = j % 2
        for copy in weights(j, slot):
            copy.wait()

        @pl.when(j + 1 < count)
        def _():
            for copy in weights(j + 1, 1 - slot):
                copy.start()

        cols = pl.ds(pl.multiple_of(j * chunk, chunk), chunk)

        @pl.loop(0, tokens // rows)
        def _(i):
            @pl.when((j == 0) & (i == tail))
            def _():
                pl.when(jnp.logical_not(end))(lambda: g_loads[tail].wait())

                @pl.when(end)
                def _():
                    half_load.wait()
                    half_swap.wait()

            some = pl.ds(pl.multiple_of(i * rows, rows), rows)
            gate = nn(n_all[some], wg_buf[slot])
            up = nn(n_all[some], wu_buf[slot])
            d_act = nt(g_all[some], wd_buf[slot])
            for w, value in enumerate(gate_parts(gate, up, d_act)):
                acts[pl.ds(pl.multiple_of(w * tokens + i * rows, rows), rows), cols] = value

    lefts = (g_all, n_all, n_all)

    def product(w, x, c):
        left = lefts[w]
        block = jnp.concatenate(
            [
                left[:, pl.ds(pl.multiple_of((k * nctx + x * 2 + c) * part, part), part)]
                for k in range(ndp)
            ],
            axis=1,
        )
        return tn(block, acts[w * tokens : (w + 1) * tokens])

    core_copies = [
        remote(give.at[w % 2], take.at[w % 2], core_sem.at[0, w], core_sem.at[1, w], {"ctx": me ^ 1})
        for w in range(3)
    ]

    def z_rows(k):
        return pl.ds(pl.multiple_of(k * part, part), part)

    def x_copies(w):
        some = [z_rows(lax.rem(z + s, ndp)) for s in range(1, ndp)] + [z_rows(z)]
        return [
            remote(
                x_give.at[w, at], x_take.at[w, at], x_sem.at[0, w, s], x_sem.at[1, w, s],
                {"ctx": me ^ 2},
            )
            for s, at in enumerate(some)
        ]

    def hand(w):
        give[w % 2, 0] = product(w, 1 - xpos, 1 - core).astype(BF)
        give[w % 2, 1] = product(w, xpos, 1 - core).astype(BF)
        core_copies[w].start()

    def keep(w):
        there = product(w, 1 - xpos, core)
        core_copies[w].wait()
        x_give[w] = (there + take[w % 2, 0].astype(F32)).astype(BF)
        if w < 2:
            for copy in x_copies(w):
                copy.start()
        x_keep[w] = (product(w, xpos, core) + take[w % 2, 1].astype(F32)).astype(BF)

    hand(0)
    keep(0)
    hand(1)
    keep(1)
    hand(2)
    keep(2)

    z_units = pl.ds(pl.multiple_of(start, units), units)

    def landing(w):
        return down_z.at[z] if w == 0 else (gate_z, up_z)[w - 1].at[:, z_units]

    def z_copies(w):
        return [
            remote(
                x_keep.at[w, z_rows(lax.rem(z + s, ndp))],
                landing(w),
                zz_sem.at[0, w, s],
                zz_sem.at[1, w, s],
                peers[s - 1],
            )
            for s in range(1, ndp)
        ]

    def z_own_copy(w):
        return pltpu.make_async_copy(x_keep.at[w, z_rows(z)], landing(w), z_own.at[w])

    def serve(w):
        onward = z_copies(w) + [z_own_copy(w)]
        for s, copy in enumerate(x_copies(w)):
            at = z_rows(lax.rem(z + 1 + s, ndp))
            copy.wait()
            x_keep[w, at] = (x_keep[w, at].astype(F32) + x_take[w, at].astype(F32)).astype(BF)
            onward[s].start()

    wo, wq = n_all, acts.at[pl.ds(0, width)]
    wk, wv = wg_buf.at[0], wu_buf.at[0]
    loads = [
        pltpu.make_async_copy(src, dst, back_sem.at[i])
        for i, (src, dst) in enumerate(((wo_hbm, wo), (wq_hbm, wq), (wk_hbm, wk), (wv_hbm, wv)))
    ]
    for copy in loads:
        copy.start()
    bias_ref[...] = mask_bias(where_ref[0], where_ref[1], length, span)
    resid_load.wait()
    v = acc[...]
    factor = lax.rsqrt(jnp.mean(v * v, axis=-1, keepdims=True) + EPS)
    for copy in dn_copies:
        copy.wait()
    y_out = remote(out_hbm, out_got, y_sem.at[0, 1], y_sem.at[1, 1], mate)
    y_out.start()
    cols = width // 4

    def dn_part(c):
        return dn_got[c // 2][:, (c % 2) * cols : (c % 2 + 1) * cols]

    dots = jnp.zeros((span, 1), F32)
    for c in range(4):
        at = slice(c * cols, (c + 1) * cols)
        unit = acc[:, at] * factor
        back = dn_ref[:, at].astype(F32) + dn_part(c).astype(F32)
        term = back * unit
        gain_grad_ref[:, at] = jnp.sum(term, axis=0, keepdims=True)
        dots += jnp.sum(term * gain_ref[:, at], axis=-1, keepdims=True)
    dots = dots / width
    for c in range(4):
        at = slice(c * cols, (c + 1) * cols)
        unit = acc[:, at] * factor
        back = dn_ref[:, at].astype(F32) + dn_part(c).astype(F32)
        total = g_all[:span, at].astype(F32) + factor * (back * gain_ref[:, at] - unit * dots)
        acc[:, at] = total
        low[:, at] = total.astype(BF)
    dr_save = pltpu.make_async_copy(acc, dr_out, save_sem.at[1])
    dr_save.start()

    spread = width // nctx

    def low_rows(p):
        return pl.ds(pl.multiple_of(p // 2 * span, span), span)

    def low_cols(p):
        return pl.ds(pl.multiple_of(p % 2 * spread, spread), spread)

    for p in range(nctx):
        for b in range(ndp):
            at = (b * nctx + p) * part
            to = p % 2 * spread + b * part
            give[0, 0, p // 2 * span : (p // 2 + 1) * span, to : to + part] = low[:, at : at + part]
    spreads = [
        remote(
            give.at[0, 0, low_rows(me ^ m), low_cols(me ^ m)],
            left2.at[mine],
            low_sem.at[0, m],
            low_sem.at[1, m],
            {"ctx": me ^ m},
        )
        for m in range(1, nctx)
    ]
    for copy in spreads:
        copy.start()
    left2[mine, :] = give[0, 0, low_rows(me), low_cols(me)]
    loads[0].wait()
    d_att = give.at[1, 0, pl.ds(0, span)]
    d_att[...] = nt(low[...], wo[...]).astype(BF)
    wide = 128 * group
    heads = wide // HD
    blocks = kvw // 128
    scale = jnp.asarray(HD**-0.5, BF)

    def share(j, m):
        some = pl.ds(pl.multiple_of((me ^ m) * span, span), span)
        return remote(
            dkv.at[j, some], land.at[j, m], dkv_sem.at[0, j, m], dkv_sem.at[1, j, m], {"ctx": me ^ m}
        )

    @pl.loop(0, blocks)
    def _(j):
        lanes = pl.ds(pl.multiple_of(j * wide, 128), wide)
        queries = q_ref[:, lanes] * scale
        grads = d_att[:, lanes]
        keys = kv_ref[:, pl.ds(pl.multiple_of(j * 128, 128), 128)]
        values = kv_ref[:, pl.ds(pl.multiple_of(kvw + j * 128, 128), 128)]
        lse = lse_ref[pl.ds(pl.multiple_of(j * heads, heads), heads), :]
        pair = []
        for h in range(heads):
            at = slice(HD * (h // group), HD * (h // group + 1))
            key, value = keys[:, at], values[:, at]
            query = queries[:, HD * h : HD * (h + 1)]
            grad = grads[:, HD * h : HD * (h + 1)]
            probs = jnp.exp(nt(key, query) + (bias_ref[...] - lse[h : h + 1, :]))
            d_probs = nt(value, grad)
            delta = jnp.sum(probs * d_probs, axis=0, keepdims=True)
            d_scores = (probs * (d_probs - delta)).astype(BF)
            d_value = nn(probs.astype(BF), grad)
            d_key = nn(d_scores, query)
            if h % group == 0:
                sum_key, sum_value = d_key, d_value
            else:
                sum_key, sum_value = sum_key + d_key, sum_value + d_value
            if h % group == group - 1:
                dkv[j, :, at] = sum_key.astype(BF)
                dkv[j, :, slice(128 + at.start, 128 + at.stop)] = sum_value.astype(BF)
            pair.append(tn(key * scale, d_scores))
            if h % 2:
                both = jnp.concatenate(pair, axis=0).T
                turned = both * cos_ref[...] - swap_halves(both) * sin_ref[...]
                right1[mine, pl.ds(pl.multiple_of(j * wide + HD * (h - 1), 128), 128)] = turned.astype(BF)
                pair = []
        for m in range(1, nctx):
            share(j, m).start()

        @pl.when(j == 0)
        def _():
            serve(0)

    loads[1].wait()
    dr_save.wait()
    acc[...] = nt(right1[mine, :qw], wq[...])
    serve(1)
    for j in range(blocks):
        total = dkv[j, mine].astype(F32)
        for m in range(1, nctx):
            share(j, m).wait_recv()
            total += land[j, m].astype(F32)
        d_key = total[:, :128]
        d_key = d_key * cos_ref[...] - swap_halves(d_key) * sin_ref[...]
        right1[mine, qw + 128 * j : qw + 128 * (j + 1)] = d_key.astype(BF)
        right1[mine, qw + kvw + 128 * j : qw + kvw + 128 * (j + 1)] = total[:, 128:].astype(BF)
    own_rows = right1.at[mine]
    r_x = remote(own_rows, own_rows, r_sem.at[0, 0], r_sem.at[1, 0], {"ctx": me ^ 2})
    r_core = remote(own_rows, own_rows, r_sem.at[0, 1], r_sem.at[1, 1], {"ctx": me ^ 1})
    r_onward = remote(
        right1.at[cross], right1.at[cross], r_sem.at[0, 2], r_sem.at[1, 2], {"ctx": me ^ 1}
    )
    r_x.start()
    r_core.start()
    for copy in x_copies(2):
        copy.start()
    loads[2].wait()
    loads[3].wait()
    low[...] = (
        acc[...]
        + nt(right1[mine, qw : qw + kvw], wk[...])
        + nt(right1[mine, qw + kvw :], wv[...])
    ).astype(BF)
    y_front = remote(low, front_got, y_sem.at[0, 0], y_sem.at[1, 0], mate)
    y_front.start()

    nq = right1.shape[1]

    def att_copies(w, at):
        return [
            remote(
                prod.at[z_rows(lax.rem(z + s, ndp)), at],
                att_z.at[z, :, at],
                att_sem.at[0, w, s],
                att_sem.at[1, w, s],
                peers[s - 1],
            )
            for s in range(1, ndp)
        ]

    def att_own_copy(w, at):
        return pltpu.make_async_copy(
            prod.at[z_rows(z), at], att_z.at[z, :, at], att_sem.at[0, w, 0]
        )

    out_cols = slice(nq, prod.shape[1])
    qkv_cols = slice(0, nq)
    for copies in l_loads:
        done(copies)
    for copy in spreads:
        copy.wait()
    prod[:, out_cols] = tn(left2[...], right2[...]).astype(BF)
    for copy in att_copies(1, out_cols):
        copy.start()
    att_own_copy(1, out_cols).start()
    r_x.wait_recv()
    r_onward.start()
    r_core.wait_recv()
    r_onward.wait_recv()
    prod[:, qkv_cols] = tn(left1[...], right1[...]).astype(BF)
    for copy in att_copies(0, qkv_cols):
        copy.start()
    att_own_copy(0, qkv_cols).start()

    room = [n_all.at[pl.ds(i * span, span)] for i in range(4)]

    def fetch(src, dst, i):
        return pltpu.make_async_copy(src, dst, tail_sem.at[i])

    first = [fetch(resid_hbm, acc, 0), fetch(out_hbm, room[0], 1), fetch(x_hbm, room[1], 2)]
    for copy in first:
        copy.start()
    y_out.wait()
    got = fetch(out_got, room[2], 3)
    got.start()
    for copy in first + [got]:
        copy.wait()
    g_all[:span] = (
        acc[...] + (n_all[:span].astype(F32) + n_all[2 * span : 3 * span].astype(F32))
    ).astype(BF)
    out_save = pltpu.make_async_copy(g_all.at[pl.ds(0, span)], output, tail_sem.at[4])
    out_save.start()
    y_front.wait()
    last = [fetch(dr_out, acc, 5), fetch(front_got, room[3], 6)]
    for copy in last:
        copy.start()
    for copy in last:
        copy.wait()
    v = n_all[span : 2 * span].astype(F32)
    factor = lax.rsqrt(jnp.mean(v * v, axis=-1, keepdims=True) + EPS)

    def front_part(at):
        x = n_all[span : 2 * span, at].astype(F32)
        return x * factor, low[:, at].astype(F32) + n_all[3 * span :, at].astype(F32)

    gains[...] = jnp.zeros(gains.shape, F32)
    dots = jnp.zeros((span, 1), F32)
    for c in range(ndp):
        at = slice(c * cols, (c + 1) * cols)
        unit, back = front_part(at)
        term = back * unit
        row = jnp.sum(term, axis=0, keepdims=True)
        for p in range(nctx):
            some = slice(p * part, (p + 1) * part)
            gains[p, 0:1, c * part : (c + 1) * part] = row[:, some]
            gains[p, 1:2, c * part : (c + 1) * part] = gain_grad_ref[
                :, c * cols + p * part : c * cols + (p + 1) * part
            ]
        dots += jnp.sum(term * gain1_ref[:, at], axis=-1, keepdims=True)
    dots = dots / width
    gx_copies = [
        remote(gains.at[me ^ m], gains_x.at[m], gx_sem.at[0, m], gx_sem.at[1, m], {"ctx": me ^ m})
        for m in range(1, nctx)
    ]
    for copy in gx_copies:
        copy.start()
    for c in range(4):
        at = slice(c * cols, (c + 1) * cols)
        unit, back = front_part(at)
        acc[:, at] += factor * (back * gain1_ref[:, at] - unit * dots)
    grad_save = pltpu.make_async_copy(acc, input_grad, tail_sem.at[7])
    grad_save.start()
    total = gains[me]
    for m in range(1, nctx):
        gx_copies[m - 1].wait()
        total += gains_x[m]
    for b in range(ndp):
        gains_z[0, b] = total[:, b * part : (b + 1) * part]
    gz_copies = [
        remote(
            gains_z.at[0, lax.rem(z + s, ndp)],
            gains_z.at[1, s],
            gz_sem.at[0, s],
            gz_sem.at[1, s],
            peers[s - 1],
        )
        for s in range(1, ndp)
    ]
    for copy in gz_copies:
        copy.start()
    serve(2)
    total = gains_z[0, z]
    for s in range(1, ndp):
        gz_copies[s - 1].wait()
        total += gains_z[1, s]
    gains_ref[...] = total
    out_save.wait()
    grad_save.wait()
    for j in range(blocks):
        for m in range(1, nctx):
            share(j, m).wait_send()
    r_x.wait_send()
    r_core.wait_send()
    r_onward.wait_send()
    for w, at in ((1, out_cols), (0, qkv_cols)):
        for copy in att_copies(w, at):
            copy.wait()
        att_own_copy(w, at).wait()
    for w in range(3):
        for copy in z_copies(w):
            copy.wait()
        z_own_copy(w).wait()


def rear(
    where, q, kv, lse, cosine, sine, gain, gain1, dn, n2, n_all, og, og_all, og_far, wg, wu, wd,
    wq, wk, wv, wo, resid, n1p, n1_all, att, att_all, out_part, x, ndp, nctx, chunk=256, rows=256,
):
    span, width = n2.shape
    tokens, length = span * ndp, span * nctx
    units = wg.shape[1] // ndp
    part = width // (ndp * nctx)
    mine = ndp * part
    qw, kvw = wq.shape[1], wk.shape[1]
    qkvw = qw + 2 * kvw
    dma = pltpu.SemaphoreType.DMA
    flat = jax.ShapeDtypeStruct((part, ndp * units), BF)
    row = jax.ShapeDtypeStruct((span, width), BF)
    return pl.pallas_call(
        functools.partial(rear_kernel, ndp, nctx, qw // kvw, chunk, rows),
        in_specs=[SMEM_SPEC] + [VMEM_SPEC] * 8 + [HBM_SPEC] * 19,
        out_specs=[HBM_SPEC] * 9 + [VMEM_SPEC],
        out_shape=[
            jax.ShapeDtypeStruct((ndp, part, units), BF),
            flat,
            flat,
            jax.ShapeDtypeStruct((ndp, part, qkvw + qw), BF),
            row,
            row,
            jax.ShapeDtypeStruct((span, width), F32),
            row,
            jax.ShapeDtypeStruct((span, width), F32),
            jax.ShapeDtypeStruct((8, part), F32),
        ],
        scratch_shapes=[
            pltpu.VMEM((tokens, width), BF),
            pltpu.VMEM((tokens, width), BF),
            pltpu.VMEM((3 * tokens, units), BF),
            pltpu.VMEM((2, width, chunk), BF),
            pltpu.VMEM((2, width, chunk), BF),
            pltpu.VMEM((2, chunk, width), BF),
            pltpu.VMEM((2, 2, mine, units), BF),
            pltpu.VMEM((2, 2, mine, units), BF),
            pltpu.VMEM((3, mine, units), BF),
            pltpu.VMEM((3, mine, units), BF),
            pltpu.VMEM((3, mine, units), BF),
            pltpu.VMEM((length, width // nctx), BF),
            pltpu.VMEM((length, width // nctx), BF),
            pltpu.VMEM((length, qkvw), BF),
            pltpu.VMEM((length, qw), BF),
            pltpu.VMEM((mine, qkvw + qw), BF),
            pltpu.VMEM((span, width), BF),
            pltpu.VMEM((length, span), F32),
            pltpu.VMEM((kvw // 128, length, 256), BF),
            pltpu.VMEM((kvw // 128, nctx, span, 256), BF),
            pltpu.VMEM((span, width), F32),
            pltpu.VMEM((1, width), F32),
            pltpu.VMEM((nctx, 8, ndp * part), F32),
            pltpu.VMEM((nctx, 8, ndp * part), F32),
            pltpu.VMEM((2, ndp, 8, part), F32),
            dma((2, ndp)),
            dma((2, nctx)),
            dma((2, 3)),
            dma((4,)),
            dma((2, 2)),
            dma((2, nctx)),
            dma((2, kvw // 128, nctx)),
            dma((2, 3)),
            dma((2, 3)),
            dma((2, 3, ndp)),
            dma((2, 3, ndp)),
            dma((3,)),
            dma((2, 2, ndp)),
            dma((2, 2)),
            dma((3,)),
            dma((2,)),
            dma((8,)),
            dma((2, nctx)),
            dma((2, ndp)),
        ],
        compiler_params=pltpu.CompilerParams(
            vmem_limit_bytes=127 * 512 * 1024, collective_id=2, has_side_effects=True
        ),
        cost_estimate=cost(12 * tokens * width * units, 4 * tokens * width),
        name="rear",
    )(
        where, q, kv, lse, cosine, sine, gain.reshape(1, width), gain1.reshape(1, width), dn,
        n2, n_all, og, og_all, og_far, wg, wu, wd, wq, wk, wv, wo,
        resid, n1p, n1_all, att, att_all, out_part, x,
    )


def dot_plain(left, right):
    return jnp.dot(left, right, preferred_element_type=F32)


def dot_right(left, right):
    return lax.dot_general(left, right, (((1,), (1,)), ((), ())), preferred_element_type=F32)


def dot_left(left, right):
    return lax.dot_general(left, right, (((0,), (0,)), ((), ())), preferred_element_type=F32)


def normed(v, gain):
    return v * lax.rsqrt(jnp.mean(v * v, axis=-1, keepdims=True) + EPS) * gain


def norm_back(v, gain, grad):
    factor = lax.rsqrt(jnp.mean(v * v, axis=-1, keepdims=True) + EPS)
    unit = v * factor
    d_unit = grad * gain
    d_gain = jnp.sum(grad * unit, axis=0)
    d_v = factor * (d_unit - unit * jnp.mean(d_unit * unit, axis=-1, keepdims=True))
    return (d_v, d_gain)


def rotate(t, cosine, sine):
    half = t.shape[-1] // 2
    first, second = (t[..., :half], t[..., half:])
    return jnp.concatenate(
        [first * cosine - second * sine, second * cosine + first * sine], axis=-1
    )


def rotate_back(t, cosine, sine):
    half = t.shape[-1] // 2
    first, second = (t[..., :half], t[..., half:])
    return jnp.concatenate(
        [first * cosine + second * sine, second * cosine - first * sine], axis=-1
    )


def score_block(query5, key_all, allowed):
    scores = jnp.einsum(
        "scngd,slnd->sngcl", query5, key_all, preferred_element_type=F32
    ) * HD ** (-0.5)
    return jnp.where(allowed[:, None, None], scores, NEG)


def build(ndp, nctx, nten):
    def pull(v, axis, n, s):
        return lax.ppermute(v, axis, [((i + s) % n, i) for i in range(n)])

    def flip(v, axis, n, bit):
        return lax.ppermute(v, axis, [(i, i ^ bit) for i in range(n)])

    def tensor_sum(v):
        low = v.astype(BF)
        if nten == 2:
            return low.astype(F32) + flip(low, "tensor", 2, 1).astype(F32)
        return lax.psum(low, "tensor").astype(F32)

    def gather_dp(v):
        rows = v.shape[0] // nten
        part = lax.dynamic_slice_in_dim(v, lax.axis_index("tensor") * rows, rows, 0)
        pieces = [v]
        for s in range(1, ndp):
            got = pull(part, "dp", ndp, s)
            pieces.append(got)
            for t in range(1, nten):
                pieces.append(pull(got, "tensor", nten, t))
        return jnp.concatenate(pieces, axis=0)

    def ctx_sum(full):
        r = full.shape[0] // (ndp * nctx)
        me = lax.axis_index("ctx")
        work = full.reshape(ndp, nctx, r, full.shape[1])
        bit = 1
        while bit < nctx:
            left = work.shape[1] // 2
            work = work.reshape(ndp, left, 2, r, full.shape[1])
            mine = (me // bit) % 2
            keep = lax.dynamic_index_in_dim(work, mine, 2, keepdims=False)
            give = lax.dynamic_index_in_dim(work, 1 - mine, 2, keepdims=False)
            got = flip(give, "ctx", nctx, bit)
            work = (keep.astype(F32) + got.astype(F32)).astype(BF)
            bit *= 2
        return work.reshape(ndp, r, full.shape[1])

    def finish_slices(full):
        got = lax.all_to_all(ctx_sum(full), "dp", 0, 0, tiled=True)
        return jnp.swapaxes(got, 0, 1).reshape(got.shape[1], -1).astype(F32)

    def finish_sum(full):
        got = lax.all_to_all(ctx_sum(full), "dp", 0, 0, tiled=True)
        return jnp.sum(got.astype(F32), axis=0)

    def local(
        layer_input,
        output_grad,
        prefix,
        attn_gain,
        w_query,
        w_key,
        w_value,
        w_out,
        mlp_gain,
        w_gate,
        w_up,
        w_down,
    ):
        seqs, span, width = layer_input.shape
        q_heads = w_query.shape[1] // HD
        kv_heads = w_key.shape[1] // HD
        group = q_heads // kv_heads
        zi = lax.axis_index("dp")
        rows = layer_input.astype(F32).reshape(seqs * span, width)
        grad_low = output_grad.reshape(seqs * span, width)
        grad_rows = grad_low.astype(F32)
        grad_all = gather_dp(grad_low)

        first = lax.axis_index("ctx") * span
        position = (first + jnp.arange(span)).astype(F32)
        frequency = ROPE_BASE ** (-jnp.arange(HD // 2).astype(F32) * 2.0 / HD)
        angle = position[:, None] * frequency[None, :]
        cosine = jnp.cos(angle)[None, :, None, :]
        sine = jnp.sin(angle)[None, :, None, :]
        normed1 = normed(rows, attn_gain).astype(BF)
        query = rotate(
            dot_plain(normed1, w_query).reshape(seqs, span, q_heads, HD), cosine, sine
        ).astype(BF)
        keyed = rotate(
            dot_plain(normed1, w_key).reshape(seqs, span, kv_heads, HD), cosine, sine
        ).astype(BF)
        valued = dot_plain(normed1, w_value).astype(BF).reshape(seqs, span, kv_heads * HD)
        key_all, value_all = (
            lax.all_gather(
                keyed.reshape(seqs, span, kv_heads * HD), "ctx", axis=1, tiled=True
            ),
            lax.all_gather(valued, "ctx", axis=1, tiled=True),
        )
        length = key_all.shape[1]
        key_all = key_all.reshape(seqs, length, kv_heads, HD)
        value_all = value_all.reshape(seqs, length, kv_heads, HD)
        query5 = query.reshape(seqs, span, kv_heads, group, HD)
        query_pos = first + jnp.arange(span)
        key_pos = jnp.arange(length)
        allowed = (key_pos[None, None, :] <= query_pos[None, :, None]) | (
            key_pos[None, None, :] < prefix[:, None, None]
        )
        scores = score_block(query5, key_all, allowed)
        top = jnp.max(scores, axis=-1, keepdims=True)
        exponent = jnp.exp(scores - top)
        total = jnp.sum(exponent, axis=-1, keepdims=True)
        log_total = top + jnp.log(total)
        probs_low = (exponent / total).astype(BF)
        attended = jnp.einsum(
            "sngcl,slnd->scngd", probs_low, value_all, preferred_element_type=F32
        )
        attended = attended.astype(BF).reshape(seqs * span, q_heads * HD)
        resid = rows + tensor_sum(dot_plain(attended, w_out))
        normed2 = normed(resid, mlp_gain).astype(BF)
        normed2_all = gather_dp(normed2)
        gate = dot_plain(normed2, w_gate)
        up = dot_plain(normed2, w_up)
        act = (jax.nn.silu(gate) * up).astype(BF)

        def mlp_back(gate, up, d_act):
            sigmoid_gate = jax.nn.sigmoid(gate)
            d_gate_pre = (
                d_act * up * sigmoid_gate * (1.0 + gate * (1.0 - sigmoid_gate))
            ).astype(BF)
            d_up_pre = (d_act * gate * sigmoid_gate).astype(BF)
            return d_gate_pre, d_up_pre

        d_act = dot_right(grad_low, w_down)
        d_gate_pre, d_up_pre = mlp_back(gate, up, d_act)
        back_terms = dot_right(d_gate_pre, w_gate) + dot_right(d_up_pre, w_up)
        d_normed2 = tensor_sum(back_terms)
        output = (resid + tensor_sum(dot_plain(act, w_down))).astype(BF)
        output = output.reshape(seqs, span, width)

        units = w_gate.shape[1] // ndp
        wg = lax.dynamic_slice_in_dim(w_gate, zi * units, units, 1)
        wu = lax.dynamic_slice_in_dim(w_up, zi * units, units, 1)
        wd = lax.dynamic_slice_in_dim(w_down, zi * units, units, 0)
        gate_s = dot_plain(normed2_all, wg)
        up_s = dot_plain(normed2_all, wu)
        d_act_s = dot_right(grad_all, wd)
        act_s = (jax.nn.silu(gate_s) * up_s).astype(BF)
        d_gate_s, d_up_s = mlp_back(gate_s, up_s, d_act_s)
        s_down = finish_slices(dot_left(grad_all, act_s).astype(BF)).T
        s_gate = finish_slices(dot_left(normed2_all, d_gate_s).astype(BF))
        s_up = finish_slices(dot_left(normed2_all, d_up_s).astype(BF))

        d_resid_norm, g_mlp_gain = norm_back(resid, mlp_gain, d_normed2)
        d_resid = grad_rows + d_resid_norm
        d_resid_low = d_resid.astype(BF)
        s_out = finish_sum(dot_left(d_resid_low, attended).astype(BF)).T
        d_attended = dot_right(d_resid_low, w_out).astype(BF).reshape(query5.shape)
        scores = score_block(query5, key_all, allowed)
        probs = jnp.exp(scores - log_total)
        probs_low = probs.astype(BF)
        d_probs = jnp.einsum(
            "scngd,slnd->sngcl", d_attended, value_all, preferred_element_type=F32
        )
        delta = jnp.sum(probs * d_probs, axis=-1, keepdims=True)
        d_scores = (probs * (d_probs - delta)).astype(BF)
        scale = HD ** (-0.5)
        d_query = (
            jnp.einsum("sngcl,slnd->scngd", d_scores, key_all, preferred_element_type=F32) * scale
        )
        d_key_all = (
            jnp.einsum("sngcl,scngd->slnd", d_scores, query5, preferred_element_type=F32) * scale
        )
        d_value_all = jnp.einsum(
            "sngcl,scngd->slnd", probs_low, d_attended, preferred_element_type=F32
        )
        d_kv = jnp.concatenate(
            [
                d_key_all.reshape(length, kv_heads * HD).astype(BF),
                d_value_all.reshape(length, kv_heads * HD).astype(BF),
            ],
            axis=1,
        )
        d_kv = lax.psum_scatter(d_kv, "ctx", scatter_dimension=0, tiled=True).astype(F32)
        d_key, d_val = d_kv[:, : kv_heads * HD], d_kv[:, kv_heads * HD :]
        d_qp = (
            rotate_back(d_query.reshape(seqs, span, q_heads, HD), cosine, sine)
            .astype(BF)
            .reshape(seqs * span, q_heads * HD)
        )
        d_kp = (
            rotate_back(d_key.reshape(seqs, span, kv_heads, HD), cosine, sine)
            .astype(BF)
            .reshape(seqs * span, kv_heads * HD)
        )
        d_vp = d_val.astype(BF).reshape(seqs * span, kv_heads * HD)
        front_terms = dot_right(d_qp, w_query) + dot_right(d_kp, w_key) + dot_right(d_vp, w_value)
        d_normed1 = tensor_sum(front_terms)
        d_rows_norm, g_attn_gain = norm_back(rows, attn_gain, d_normed1)
        d_input = d_resid + d_rows_norm
        d_input = d_input.reshape(seqs, span, width)
        s_qkv = finish_sum(
            dot_left(normed1, jnp.concatenate([d_qp, d_kp, d_vp], axis=1)).astype(BF)
        )
        nq, nk = q_heads * HD, kv_heads * HD
        s_query, s_key, s_value = s_qkv[:, :nq], s_qkv[:, nq : nq + nk], s_qkv[:, nq + nk :]
        gains = jnp.stack([g_attn_gain, g_mlp_gain])
        gains = lax.psum_scatter(gains, ("dp", "ctx"), scatter_dimension=1, tiled=True)
        return (
            output,
            d_input,
            gains[0],
            s_query,
            s_key,
            s_value,
            s_out,
            gains[1],
            s_gate,
            s_up,
            s_down,
        )

    return local


def suits(ndp, nctx, nten, layer_input, output_grad, prefix, attn_gain, w_query, w_key, w_value, w_out, mlp_gain, w_gate, w_up, w_down):
    seqs, span, width = layer_input.shape
    return (
        seqs == 1
        and (ndp, nctx, nten) == (4, 4, 2)
        and (span, width) == (256, 2048)
        and (w_query.shape[1], w_key.shape[1], w_gate.shape[1]) == (1024, 256, 4096)
    )


def build_fast(ndp, nctx, nten):
    def local(
        layer_input,
        output_grad,
        prefix,
        attn_gain,
        w_query,
        w_key,
        w_value,
        w_out,
        mlp_gain,
        w_gate,
        w_up,
        w_down,
    ):
        seqs, span, width = layer_input.shape
        kvw, nq = w_key.shape[1], w_query.shape[1]
        low = layer_input.reshape(span, width)
        grad_low = output_grad.reshape(span, width)
        first = lax.axis_index("ctx") * span
        where = jnp.stack([first, prefix[0]]).astype(jnp.int32)
        cosine, sine = rope_tables(first, span)
        n1p, query, kv, attended, lse, resid, normed2, grad_all = front(
            where, low, attn_gain, w_query, w_key, w_value, w_out, cosine, sine, mlp_gain, grad_low, ndp, nctx
        )
        out_part, dn, n_all, n1_all, att_all, grad_far = middle(
            normed2, grad_low, w_gate, w_up, w_down, n1p, attended, grad_all, ndp, nctx
        )
        down_z, gate_z, up_z, att_z, _, _, _, output, d_input, gains = rear(
            where, query, kv, lse, cosine, sine, mlp_gain, attn_gain, dn, normed2, n_all, grad_low,
            grad_all, grad_far, w_gate, w_up, w_down, w_query, w_key, w_value, w_out, resid, n1p, n1_all,
            attended, att_all, out_part, low, ndp, nctx,
        )
        output = output.reshape(seqs, span, width)
        d_input = d_input.reshape(seqs, span, width)
        s_down = jnp.swapaxes(down_z, 1, 2).reshape(w_down.shape[0], -1).astype(F32)
        s_gate, s_up = gate_z.astype(F32), up_z.astype(F32)
        s_att = jnp.sum(att_z.astype(F32), axis=0)
        s_query, s_key = s_att[:, :nq], s_att[:, nq : nq + kvw]
        s_value, s_out = s_att[:, nq + kvw : nq + 2 * kvw], s_att[:, nq + 2 * kvw :].T
        return (
            output,
            d_input,
            gains[0],
            s_query,
            s_key,
            s_value,
            s_out,
            gains[1],
            s_gate,
            s_up,
            s_down,
        )

    return local


def solution(mesh):
    sizes = mesh.shape["dp"], mesh.shape["ctx"], mesh.shape["tensor"]
    plain, fast = build(*sizes), build_fast(*sizes)

    def local(*args):
        return (fast if suits(*sizes, *args) else plain)(*args)

    return jax.shard_map(
        local,
        mesh=mesh,
        in_specs=(
            P("dp", "ctx", None),
            P("dp", "ctx", None),
            P("dp"),
            P(),
            P(None, "tensor"),
            P(None, "tensor"),
            P(None, "tensor"),
            P("tensor", None),
            P(),
            P(None, "tensor"),
            P(None, "tensor"),
            P("tensor", None),
        ),
        out_specs=(
            P("dp", "ctx", None),
            P("dp", "ctx", None),
            P(("dp", "ctx")),
            P(("dp", "ctx"), "tensor"),
            P(("dp", "ctx"), "tensor"),
            P(("dp", "ctx"), "tensor"),
            P("tensor", ("dp", "ctx")),
            P(("dp", "ctx")),
            P(("dp", "ctx"), "tensor"),
            P(("dp", "ctx"), "tensor"),
            P("tensor", ("dp", "ctx")),
        ),
        check_vma=False,
    )
```
